32 devices in a mesh: dp: 16 (over z, x, core), tensor: 2 (over y).
Axes of the slice: x: 2, y: 2, z: 4, core: 2. Of those that a mesh axis runs over, the one named last changes fastest.
Arguments:
- tokens: bfloat16 [8192, 1024], P(('dp', 'tensor')), may hold values from -6 to 6
- cotangent: bfloat16 [8192, 1024], P(('dp', 'tensor')), may hold values from -6 to 6
- segments: int32 [16, 512], P('dp'), may hold values from 0 to 7, never falling along the last dimension, each value on 1 to 128 neighbouring positions
- ln_gain: float32 [1024], replicated, may hold values from 0.5 to 1.5
- ln_bias: float32 [1024], replicated, may hold values from -2 to 2
- w_qkv: bfloat16 [1024, 3072], P('dp', 'tensor'), may hold values from -0.1875 to 0.1875
- b_qkv: float32 [3072], P('tensor'), may hold values from -2 to 2
- w_dense: bfloat16 [1024, 1024], P('tensor', 'dp'), may hold values from -0.5 to 0.5
- b_dense: float32 [1024], replicated, may hold values from -2 to 2
- w_up: bfloat16 [1024, 4096], P('dp', 'tensor'), may hold values from -0.1875 to 0.1875
- b_up: float32 [4096], P('tensor'), may hold values from -2 to 2
- w_down: bfloat16 [4096, 1024], P('tensor', 'dp'), may hold values from -0.09375 to 0.09375
- b_down: float32 [1024], replicated, may hold values from -2 to 2
Outputs:
- output: bfloat16 [8192, 1024], P(('dp', 'tensor'))
- input_grad: float32 [8192, 1024], P(('dp', 'tensor'))
- ln_gain_grad: float32 [1024], replicated
- ln_bias_grad: float32 [1024], replicated
- qkv_grad: float32 [1024, 3072], P('dp', 'tensor')
- qkv_bias_grad: float32 [3072], P('tensor')
- dense_grad: float32 [1024, 1024], P('tensor', 'dp')
- dense_bias_grad: float32 [1024], replicated
- up_grad: float32 [1024, 4096], P('dp', 'tensor')
- up_bias_grad: float32 [4096], P('tensor')
- down_grad: float32 [4096, 1024], P('tensor', 'dp')
- down_bias_grad: float32 [1024], replicated
The draws below stay inside these ranges and needn't reach their ends.
Inputs may be any that keep to these rules, and one draw needn't show every extreme that they name: `segments`: within each sequence the document numbers never fall, every number from 0 to 7 is used, each document has at least one token and some document has exactly 128 tokens.
All inputs are finite; a program needn't handle non-finite values.
Results may differ from the reference program's by a relative error of at most 0.0085.
Values may be sent and summed in bfloat16 or wider, within the bound.
A program may use at most 128 MiB of HBM per device.

```python
import math
import jax
import jax.numpy as jnp
import numpy as np
from jax import lax

D = 1024
HEADS = 16
HEAD = 64
ROT = 16
FF = 4096
SEQ = 512
TOKENS = 8192
DOCS = 8
MOST_DOC = 128
N_DP = 16


def block_scale(stream_key, extent, cuts, low, high):
    level, own = 1.0, jax.random.fold_in(stream_key, 6)
    for position, blocks in cuts:
        steps = jnp.exp(jax.random.uniform(jax.random.fold_in(own, position), (blocks,), jnp.float32, low / len(cuts), high / len(cuts)))
        level = level * jnp.repeat(steps, extent[position] // blocks).reshape([-1 if axis == position else 1 for axis in range(len(extent))])
    return level


def profile(count, total, most, lean):
    loads = [(1 << 20) // math.isqrt(rank ** lean) + 1 for rank in range(2, count + 1)]
    spare, holding = total - most - (count - 1), [1] * (count - 1)
    while spare > 0:
        movable = [i for i in range(count - 1) if holding[i] < most]
        pool, left = sum([loads[i] for i in movable]), spare
        for i in movable:
            addition = min(most - holding[i], max(1, left * loads[i] // pool), spare)
            holding[i] = holding[i] + addition
            spare = spare - addition
    return np.array([most] + holding)


def ragged(own_key, amount, total, limit, skew):
    if amount == 2:
        one = jax.random.randint(own_key, (), max(1, total - limit), min(limit, total - 1) + 1)
        return jnp.stack([one, total - one])
    lengths = jnp.asarray(profile(amount, total, limit, skew), jnp.int32)
    couples = (amount - 1) // 2
    giver, receiver = lengths[1:1 + 2 * couples:2], lengths[2:2 + 2 * couples:2]
    margin = jnp.minimum(giver - 1, limit - receiver)
    moved = jax.random.randint(jax.random.fold_in(own_key, 1), (couples,), 0, 1 << 20) % (margin + 1)
    lengths = lengths.at[1:1 + 2 * couples:2].set(giver - moved).at[2:2 + 2 * couples:2].set(receiver + moved)
    return lengths[jax.random.permutation(jax.random.fold_in(own_key, 2), amount)]


def bell_draw(own_key, extent, scale, limit, cuts=(), held_as=jnp.bfloat16):
    factor_of = block_scale(own_key, extent, cuts, -0.22, 0.18) if cuts else 1.0
    values = jax.random.normal(own_key, extent, jnp.float32) * scale * factor_of
    return jnp.minimum(jnp.maximum(values, -limit), limit).astype(held_as)


def setup_inputs(seed: int = 0) -> dict:
    seeds = jax.random.split(jax.random.key(seed), 14)
    tokens = bell_draw(seeds[0], (TOKENS, D), 1.0, 6.0, ((0, 32),))
    cotangent = bell_draw(seeds[1], (TOKENS, D), 1.0, 6.0, ((0, 32),))
    segments = jax.vmap(lambda own: jnp.searchsorted(jnp.cumsum(ragged(own, DOCS, SEQ, MOST_DOC, 2)), jnp.arange(SEQ), side="right"))(jax.random.split(seeds[2], N_DP)).reshape((N_DP, SEQ)).astype(jnp.int32)
    ln_gain = jnp.clip(1.0 + 0.1 * jax.random.normal(seeds[3], (D,), jnp.float32), 0.5, 1.5)
    ln_bias = bell_draw(seeds[4], (D,), 0.3, 2.0, (), jnp.float32)
    w_qkv = bell_draw(seeds[5], (D, 3 * D), D ** -0.5, 0.1875, ((0, 16), (1, 2)))
    b_qkv = bell_draw(seeds[6], (3 * D,), 0.3, 2.0, ((0, 2),), jnp.float32)
    w_dense = bell_draw(seeds[7], (D, D), (D // 8) ** -0.5, 0.5, ((0, 2), (1, 16)))
    b_dense = bell_draw(seeds[8], (D,), 0.3, 2.0, (), jnp.float32)
    w_up = bell_draw(seeds[9], (D, FF), D ** -0.5, 0.1875, ((0, 16), (1, 2)))
    b_up = bell_draw(seeds[10], (FF,), 0.3, 2.0, ((0, 2),), jnp.float32)
    w_down = bell_draw(seeds[11], (FF, D), FF ** -0.5, 0.09375, ((0, 2), (1, 16)))
    b_down = bell_draw(seeds[12], (D,), 0.3, 2.0, (), jnp.float32)
    return {"tokens": tokens, "cotangent": cotangent, "segments": segments, "ln_gain": ln_gain, "ln_bias": ln_bias, "w_qkv": w_qkv, "b_qkv": b_qkv, "w_dense": w_dense, "b_dense": b_dense, "w_up": w_up, "b_up": b_up, "w_down": w_down, "b_down": b_down}


@jax.custom_vjp
def low(v):
    return lax.optimization_barrier(v.astype(jnp.bfloat16)).astype(jnp.float32)

@jax.custom_vjp
def low_back(v):
    return v

def low_keep(v):
    return (low(v), None)

def low_pass(kept, grad):
    return (grad,)

def back_keep(v):
    return (v, None)

def back_low(kept, grad):
    return (low(grad),)
low.defvjp(low_keep, low_pass)
low_back.defvjp(back_keep, back_low)
norm_eps = 1e-05
rotary_base = 10000.0
precise = lax.Precision.HIGHEST

def matmul(left, right):
    return jnp.dot(left, right, precision=precise, preferred_element_type=jnp.float32)

def rotary_tables(length, rotary):
    halfway = rotary // 2
    places = jnp.arange(length, dtype=jnp.float32)
    inverse = rotary_base ** (-(jnp.arange(halfway, dtype=jnp.float32) * 2.0 / rotary))
    angles = places[:, None] * inverse[None, :]
    return (jnp.cos(angles)[:, None, :], jnp.sin(angles)[:, None, :])

def rotate(part, cos_table, sin_table, rotary):
    halfway = rotary // 2
    leading = part[..., :halfway]
    trailing = part[..., halfway:rotary]
    return jnp.concatenate([leading * cos_table - trailing * sin_table, trailing * cos_table + leading * sin_table, part[..., rotary:]], axis=-1)

def layer(inputs, doc_ids, ln_gain, ln_bias, w_qkv, b_qkv, w_dense, b_dense, w_up, b_up, w_down, b_down):
    length = inputs.shape[0]
    centred = inputs - lax.optimization_barrier(jnp.mean(inputs, axis=-1, keepdims=True))
    variance = lax.optimization_barrier(jnp.mean(centred * centred, axis=-1, keepdims=True))
    normed = low(centred * lax.rsqrt(variance + norm_eps) * ln_gain + ln_bias)
    packed = low_back(matmul(normed, w_qkv) + b_qkv).reshape(length, HEADS, 3, HEAD)
    hidden = low_back(matmul(normed, w_up) + b_up)
    cos_table, sin_table = rotary_tables(length, ROT)
    query_vecs = low(rotate(packed[:, :, 0], cos_table, sin_table, ROT))
    key_vecs = low(rotate(packed[:, :, 1], cos_table, sin_table, ROT))
    value_vecs = low(packed[:, :, 2])
    places = jnp.arange(length, dtype=jnp.int32)
    block_rows = min(512, length)
    block_count = length // block_rows
    score_scale = 1.0 / math.sqrt(HEAD)

    def attend(pieces):
        query_block, doc_block, place_block = pieces
        scores = low_back(jnp.einsum('qhd,khd->hqk', query_block, key_vecs, precision=precise) * score_scale)
        allowed = (doc_block[:, None] == doc_ids[None, :]) & (place_block[:, None] >= places[None, :])
        scores = jnp.where(allowed[None], scores, -1e+30)
        probs = jax.nn.softmax(scores, axis=-1)
        return jnp.einsum('hqk,khd->qhd', low(probs), value_vecs, precision=precise)
    attended = lax.map(jax.checkpoint(attend), (query_vecs.reshape(block_count, block_rows, HEADS, HEAD), doc_ids.reshape(block_count, block_rows), places.reshape(block_count, block_rows)))
    attn_out = low(low_back(attended.reshape(length, HEADS * HEAD)))
    activated = low(jax.nn.gelu(hidden, approximate=False))
    return inputs + matmul(attn_out, w_dense) + b_dense + matmul(activated, w_down) + b_down

def reference(tokens, cotangent, segments, ln_gain, ln_bias, w_qkv, b_qkv, w_dense, b_dense, w_up, b_up, w_down, b_down):
    params = tuple((weight.astype(jnp.float32) for weight in (ln_gain, ln_bias, w_qkv, b_qkv, w_dense, b_dense, w_up, b_up, w_down, b_down)))
    inputs = tokens.astype(jnp.float32).reshape(N_DP, SEQ, D)
    upstream = cotangent.astype(jnp.float32).reshape(N_DP, SEQ, D)

    def one_sequence(totals, pieces):
        seq_in, seq_up, seq_doc = pieces

        def forward(layer_in, *weights):
            return layer(layer_in, seq_doc, *weights)
        result, pullback = jax.vjp(forward, seq_in, *params)
        gradients = pullback(seq_up)
        totals = tuple((total + gradient for total, gradient in zip(totals, gradients[1:])))
        return (totals, (result.astype(jnp.bfloat16), gradients[0]))
    starting = tuple((jnp.zeros_like(param) for param in params))
    totals, (outputs, input_grads) = lax.scan(one_sequence, starting, (inputs, upstream, segments))
    return (outputs.reshape(TOKENS, D), input_grads.reshape(TOKENS, D), totals[0], totals[1], totals[2], totals[3], totals[4], totals[5], totals[6], totals[7], totals[8], totals[9])
```

```python
import functools

import jax
import jax.numpy as jnp
import numpy as np
from jax import lax
from jax.experimental import pallas as pl
from jax.experimental.pallas import tpu as pltpu
from jax.sharding import PartitionSpec as P

HEAD = 64
ROT = 16
NORM_EPS = 1e-05
ROTARY_BASE = 10000.0
MESH = pl.DeviceIdType.MESH
F32 = jnp.float32
BF16 = jnp.bfloat16


def dot(left, right, over_left, over_right):
    return lax.dot_general(
        left, right, (((over_left,), (over_right,)), ((), ())), preferred_element_type=F32
    )


def normalize(rows):
    centred = rows - jnp.mean(rows, axis=-1, keepdims=True)
    inverse = lax.rsqrt(jnp.mean(centred * centred, axis=-1, keepdims=True) + NORM_EPS)
    return centred * inverse, inverse


def kernel(
    sizes,
    tokens,
    cotangent,
    segments,
    gain,
    shift,
    w_qkv,
    b_qkv,
    w_dense,
    b_dense,
    w_up,
    b_up,
    w_down,
    b_down,
    output,
    input_grad,
    gain_grad,
    shift_grad,
    qkv_grad,
    qkv_bias,
    dense_grad,
    dense_bias,
    up_grad,
    up_bias,
    down_grad,
    wa_in,
    ba,
    cos_table,
    sin_table,
    docs,
    doc_column,
    wa,
    wu,
    wd,
    normed,
    grads,
    query,
    key,
    value,
    grad_out,
    attended,
    grad_z,
    key_sum,
    value_sum,
    active,
    slope,
    grad_u,
    core_in,
    turn_in,
    own_rows,
    own_a,
    own_u,
    own_d,
    xs_a,
    xs_u,
    xs_d,
    xr_a,
    xr_u,
    xr_d,
    zs_a,
    zs_u,
    zs_d,
    zr_a,
    zr_u,
    zr_d,
    fs_a,
    fs_u,
    fs_d,
    keep_a,
    fr_a,
    vec,
    vec_in,
    vec_t,
    vec_z,
    local_sem,
    core_sem,
    up_send,
    down_send,
    x_send,
    z_recv,
    x_recv,
    act_send,
    act_recv,
    pass_send,
    pass_recv,
    rx_send,
    rx_recv,
    rz_send,
    rz_recv,
    fin_send,
    fin_recv,
    half_send,
    half_recv,
    turn_send,
    turn_recv,
    vec_send,
    vec_recv,
    credit,
):
    nt, nz, na, nm, hp, length, R, r, pw = (
        sizes[k] for k in ("nt", "nz", "na", "nm", "hp", "length", "R", "r", "pw")
    )
    D = tokens.shape[1]
    half = D // 2
    chip = 2 * r
    partials = (grads, normed)
    wide = hp * HEAD
    units = nm * pw
    dp, t = lax.axis_index("dp"), lax.axis_index("tensor")
    z, x, c = dp // 4, (dp // 2) % 2, dp % 2

    def device(zz, xx, cc, tt):
        return (zz * 4 + xx * 2 + cc, tt)

    partner = device(z, x, 1 - c, t)
    across = device(z, 1 - x, c, t)

    def along(zz):
        return device(zz, x, c, t)

    def turned(tt):
        return device(z, x, c, tt)

    def other_z(k):
        return lax.rem(z + k, nz)

    def other_t(k):
        return lax.rem(t + k, nt)

    def copy(src, dst, send, recv, to):
        return pltpu.make_async_remote_copy(
            src_ref=src, dst_ref=dst, send_sem=send, recv_sem=recv, device_id=to, device_id_type=MESH
        )

    pieces = (
        [(wa, k) for k in range(na)] + [(wu, k) for k in range(nm)] + [(wd, k) for k in range(nm)]
    )
    A = list(range(na))
    U = list(range(na, na + nm))
    Dn = list(range(na + nm, na + 2 * nm))
    own_of = [own_a.at[k] for k in range(na)] + [own_u.at[k] for k in range(nm)] + [own_d.at[k] for k in range(nm)]
    xs_of = [xs_a.at[k] for k in range(na)] + [xs_u.at[k] for k in range(nm)] + [xs_d.at[k] for k in range(nm)]
    xr_of = [xr_a.at[k] for k in range(na)] + [xr_u.at[k] for k in range(nm)] + [xr_d.at[k] for k in range(nm)]
    zs_of = [zs_a.at[k] for k in range(na)] + [zs_u.at[k] for k in range(nm)] + [zs_d.at[k] for k in range(nm)]
    zr_of = [zr_a.at[k] for k in range(na)] + [zr_u.at[k] for k in range(nm)] + [zr_d.at[k] for k in range(nm)]
    fs_of = [fs_a.at[k] for k in range(na)] + [fs_u.at[k] for k in range(nm)] + [fs_d.at[k] for k in range(nm)]

    def chip_rows(xx, zz):
        return pl.ds(pl.multiple_of((xx * nz + zz) * chip, chip), chip)

    own_block = pl.ds(pl.multiple_of((x * nz + z) * chip + c * r, r), r)

    barrier = pltpu.get_barrier_semaphore()
    greeted = [partner, across] + [along(other_z(k)) for k in range(1, nz)] + [turned(other_t(k)) for k in range(1, nt)]
    for other in greeted:
        pl.semaphore_signal(barrier, inc=1, device_id=other, device_id_type=MESH)
    pl.semaphore_wait(barrier, len(greeted))

    def half_of(i, cc):
        if i in A:
            return wa_in.at[cc, i]
        if i in U:
            return w_up.at[:, pl.ds(pl.multiple_of(cc * units + (i - na) * pw, pw), pw)]
        return w_down.at[:, pl.ds(pl.multiple_of(cc * units + (i - na - nm) * pw, pw), pw)]

    def local_copy(i):
        ref, k = pieces[i]
        return pltpu.make_async_copy(half_of(i, c), ref.at[k, own_block], local_sem.at[i])

    def core_copy(i):
        ref, k = pieces[i]
        return copy(half_of(i, 1 - c), ref.at[k, own_block], core_sem.at[0, i], core_sem.at[1, i], partner)

    def share(i):
        local_copy(i).start()
        core_copy(i).start()

    def padded(array):
        rest = -array.shape[1] % 128
        return jnp.concatenate([array, jnp.zeros((array.shape[0], rest), array.dtype)], axis=1) if rest else array

    def head_part(array, cc, k, part):
        at = [((cc * na + k) * hp + h) * 3 * HEAD + part * HEAD for h in range(hp)]
        return padded(jnp.concatenate([array[:, a : a + HEAD] for a in at], axis=1))

    for cc in range(2):
        for k in range(na):
            for part in range(3):
                wa_in[cc, k, :, part * 128 : (part + 1) * 128] = head_part(w_qkv[...], cc, k, part)
            at = (cc * na + k) * wide
            wa_in[cc, k, :, 384:512] = padded(w_dense[:, at : at + wide])
    for i in A:
        share(i)
    for i in U + Dn:
        share(i)
    docs[c] = jnp.broadcast_to(segments[...].astype(F32), docs.shape[1:])
    docs_core = copy(
        docs.at[c], docs.at[c], core_sem.at[0, len(pieces)], core_sem.at[1, len(pieces)], partner
    )
    docs_core.start()

    def permute(rows):
        return jnp.concatenate(
            [rows[:, (zz * 2 + xx) * chip : (zz * 2 + xx + 1) * chip] for xx in range(2) for zz in range(nz)],
            axis=1,
        )

    def restore(rows):
        return jnp.concatenate(
            [rows[:, (xx * nz + zz) * chip : (xx * nz + zz + 1) * chip] for zz in range(nz) for xx in range(2)],
            axis=1,
        )

    def act_rows(cc, tt):
        return pl.ds(pl.multiple_of((cc * nt + tt) * R, R), R)

    tile = min(64, R)

    def norm_rows(j, carry):
        rows = pl.ds(pl.multiple_of(j * tile, tile), tile)
        normal, _ = normalize(tokens[rows, :].astype(F32))
        to = pl.ds(pl.multiple_of((c * nt + t) * R + j * tile, tile), tile)
        normed[to, :] = permute((normal * gain[...] + shift[...]).astype(BF16))
        grads[to, :] = permute(cotangent[rows, :])
        return carry

    lax.fori_loop(0, R // tile, norm_rows, 0)

    acts = (normed, grads)

    def prepare():
        for k in range(na):
            for part in range(3):
                ba[k, :, part * 128 : (part + 1) * 128] = jnp.where(
                    c == 0, head_part(b_qkv[...], 0, k, part), head_part(b_qkv[...], 1, k, part)
                )
        inverse = np.float32(ROTARY_BASE) ** (-(np.arange(ROT // 2, dtype=np.float32) * 2.0 / ROT)).astype(np.float32)
        lane = lax.broadcasted_iota(jnp.int32, (128, 128), 1) % HEAD
        scale = jnp.zeros((128, 128), F32)
        for j in range(ROT):
            scale = jnp.where(lane == j, inverse[j % (ROT // 2)], scale)

        def table(j, carry):
            rows = pl.ds(pl.multiple_of(j * 128, 128), 128)
            place = (j * 128 + lax.broadcasted_iota(jnp.int32, (128, 128), 0)).astype(F32)
            cos, sin = jnp.cos(place * scale), jnp.sin(place * scale)
            cos_table[rows, :] = cos
            sin_table[rows, :] = jnp.where(lane < ROT // 2, -sin, sin)
            return carry

        lax.fori_loop(0, length // 128, table, 0)

    def prepare_docs():
        docs_core.wait_recv()
        for j in range(length // 128):
            cut = slice(j * 128, (j + 1) * 128)
            both = [jnp.broadcast_to(docs[s, 0:1, cut], (HEAD, 128)) for s in range(2)]
            doc_column[cut, :] = jnp.transpose(jnp.concatenate(both, axis=0))

    def act_turn(a, tt, src_t):
        blk = acts[a].at[act_rows(c, src_t)]
        return copy(blk, blk, act_send.at[a, tt], act_recv.at[a, src_t], turned(tt))

    def act_core(a, src_t, cc):
        blk = acts[a].at[act_rows(cc, src_t)]
        return copy(blk, blk, pass_send.at[a, src_t], pass_recv.at[a, src_t], partner)

    for a in range(2):
        for k in range(1, nt):
            act_turn(a, other_t(k), t).start()
        act_core(a, t, c).start()

    def act_forward(a):
        for k in range(1, nt):
            src = other_t(k)
            act_turn(a, t, src).wait_recv()
            act_core(a, src, c).start()

    def act_sent(a):
        for k in range(nt):
            act_core(a, k, c).wait_send()
        for k in range(1, nt):
            act_turn(a, other_t(k), t).wait_send()

    def act_wait(a):
        for k in range(nt):
            act_core(a, k, 1 - c).wait_recv()

    def w_block(i, xx, zz):
        ref, k = pieces[i]
        return ref.at[k, chip_rows(xx, zz)]

    def send_up(i, src):
        b = w_block(i, x, src)
        return copy(b, b, up_send.at[i, src], z_recv.at[i, src], along(z + 1))

    def send_down(i, src):
        b = w_block(i, x, src)
        return copy(b, b, down_send.at[i, src], z_recv.at[i, src], along(z - 1))

    def send_across(i, src, xx):
        b = w_block(i, xx, src)
        return copy(b, b, x_send.at[i, src], x_recv.at[i, src], across)

    def send_own(i):
        local_copy(i).wait()
        core_copy(i).wait_recv()
        pl.when(z < nz - 1)(lambda: send_up(i, z).start())
        pl.when(z > 0)(lambda: send_down(i, z).start())
        send_across(i, z, x).start()

    def forward(i, d):
        @pl.when(z >= d)
        def _():
            send_up(i, z - d).wait_recv()
            pl.when(z < nz - 1)(lambda: send_up(i, z - d).start())
            send_across(i, z - d, x).start()

        @pl.when(z + d <= nz - 1)
        def _():
            send_down(i, z + d).wait_recv()
            pl.when(z > 0)(lambda: send_down(i, z + d).start())
            send_across(i, z + d, x).start()

    def gathered(i):
        for src in range(nz):
            send_across(i, src, 1 - x).wait_recv()

    def g_across(i, to_z):
        blk = pl.ds(to_z * chip, chip)
        return copy(xs_of[i].at[blk], xr_of[i].at[blk], rx_send.at[i, to_z], rx_recv.at[i, to_z], across)

    def g_along(i, to_z, src_z):
        blk = pl.ds(pl.multiple_of(to_z * chip, chip), chip)
        src = pl.ds(pl.multiple_of(src_z * chip, chip), chip)
        return copy(zs_of[i].at[blk], zr_of[i].at[src], rz_send.at[i, to_z], rz_recv.at[i, src_z], along(to_z))

    def g_final(i, cc):
        if i in A:
            dst = fr_a.at[i]
        elif i in U:
            dst = up_grad.at[:, pl.ds(pl.multiple_of(cc * units + (i - na) * pw, pw), pw)]
        else:
            dst = down_grad.at[:, pl.ds(pl.multiple_of(cc * units + (i - na - nm) * pw, pw), pw)]
        return copy(fs_of[i], dst, fin_send.at[i], fin_recv.at[i], partner)

    def columns(xx):
        return pl.ds(pl.multiple_of(xx * half, half), half)

    def products(i, xx):
        if i in A:
            k = i
            return [
                (0, 384, dot(normed[:, columns(xx)], grad_z[k], 0, 0)),
                (384, 512, dot(grads[:, columns(xx)], attended[k], 0, 0)),
            ]
        if i in U:
            k = i - na
            return [(0, pw, dot(normed[:, columns(xx)], grad_u[k], 0, 0))]
        k = i - na - nm
        return [(0, pw, dot(grads[:, columns(xx)], active[k], 0, 0))]

    def weight_grad(i):
        for lo, hi, part in products(i, 1 - x):
            xs_of[i][:, lo:hi] = part.astype(BF16)
        for to_z in range(nz):
            g_across(i, to_z).start()
        for lo, hi, part in products(i, x):
            own_of[i][:, lo:hi] = part

    def scatter_x(i):
        for to_z in range(nz):
            g_across(i, to_z).wait_recv()
            blk = slice(to_z * chip, (to_z + 1) * chip)
            both = own_of[i][blk, :] + xr_of[i][blk, :].astype(F32)

            @pl.when(to_z != z)
            def _():
                zs_of[i][blk, :] = both.astype(BF16)
                g_along(i, to_z, z).start()

            @pl.when(to_z == z)
            def _():
                own_of[i][blk, :] = both

    def scatter_z(i):
        total = own_of[i][pl.ds(pl.multiple_of(z * chip, chip), chip), :]
        for k in range(1, nz):
            src = other_z(k)
            g_along(i, z, src).wait_recv()
            total = total + zr_of[i][pl.ds(pl.multiple_of(src * chip, chip), chip), :].astype(F32)
        keep = jnp.where(c == 0, total[:r, :], total[r:, :])
        give = jnp.where(c == 0, total[r:, :], total[:r, :])
        if i in A:
            keep_a[i] = keep
        elif i in U:
            up_grad[:, pl.ds(pl.multiple_of(c * units + (i - na) * pw, pw), pw)] = keep
        else:
            down_grad[:, pl.ds(pl.multiple_of(c * units + (i - na - nm) * pw, pw), pw)] = keep
        fs_of[i][...] = give
        g_final(i, c).start()

    def finish_attention():
        for k in range(na):
            g_final(k, 1 - c).wait_recv()
            for cc in range(2):
                part = jnp.where(c == cc, keep_a[k], fr_a[k])
                heads = [
                    part[:, p * 128 + h * HEAD : p * 128 + (h + 1) * HEAD] for h in range(hp) for p in range(3)
                ]
                at = (cc * na + k) * wide
                qkv_grad[:, 3 * at : 3 * (at + wide)] = jnp.concatenate(heads, axis=1)
                dense_grad[:, at : at + wide] = part[:, 384 : 384 + wide]

    RT = min(512, 2 * length)
    tiles = 2 * length // RT
    lanes = lax.broadcasted_iota(jnp.int32, (1, 128), 1)
    first = lanes < HEAD

    low = lanes % HEAD < ROT // 2
    turning = lanes % HEAD < ROT

    def rotated(rows, places, sign):
        near = jnp.where(low, pltpu.roll(rows, 128 - ROT // 2, 1), pltpu.roll(rows, ROT // 2, 1))
        return rows * cos_table[places, :] + jnp.where(turning, sign * near * sin_table[places, :], 0.0)

    def project(k):
        def body(j, carry):
            rows = pl.ds(pl.multiple_of(j * RT, RT), RT)
            places = pl.ds(pl.multiple_of(lax.rem(j * RT, length), RT), RT)
            packed = dot(normed[rows, :], wa[k, :, 0:384], 1, 0) + ba[k]
            query[rows, :] = (rotated(packed[:, 0:128], places, 1.0) * (HEAD**-0.5)).astype(BF16)
            key[rows, :] = rotated(packed[:, 128:256], places, 1.0).astype(BF16)
            value[rows, :] = packed[:, 256:384].astype(BF16)
            grad_out[rows, :] = dot(grads[rows, :], wa[k, :, 384:512], 1, 0).astype(BF16)
            return carry

        lax.fori_loop(0, tiles, body, 0)

    block = min(128, length // 4)
    window = length // 4 + block

    def stacked(rows):
        if hp == 1:
            return rows
        zero = jnp.zeros_like(rows)
        return jnp.concatenate([jnp.where(first, rows, zero), jnp.where(first, zero, rows)], axis=0)

    def unstacked(rows):
        if hp == 1:
            return rows
        return jnp.where(first, rows[: window], rows[window :])

    def attend(k, s):
        key_sum[...] = jnp.zeros_like(key_sum)
        value_sum[...] = jnp.zeros_like(value_sum)

        def body(i, carry):
            q_at = pl.multiple_of(i * block, block)
            k_at = pl.multiple_of(jnp.maximum(q_at - length // 4, 0), block)
            q_rows = pl.ds(pl.multiple_of(s * length + q_at, block), block)
            k_rows = pl.ds(pl.multiple_of(s * length + k_at, block), window)
            q = query[q_rows, :]
            g = grad_out[q_rows, :]
            keys, values = stacked(key[k_rows, :]), stacked(value[k_rows, :])
            scores = dot(q, keys, 1, 1)
            grad_p = dot(g, values, 1, 1)
            at = k_at + lax.broadcasted_iota(jnp.int32, (block, window), 1)
            here = q_at + lax.broadcasted_iota(jnp.int32, (block, window), 0)
            allowed = (doc_column[pl.ds(q_at, block), s * HEAD : s * HEAD + 1] == docs[s, 0:1, pl.ds(k_at, window)]) & (at <= here)
            probs, grad_s = [], []
            for h in range(hp):
                cut = slice(h * window, (h + 1) * window)
                sc = jnp.where(allowed, scores[:, cut], -1e30)
                expos = jnp.exp(sc - jnp.max(sc, axis=-1, keepdims=True))
                p = expos / jnp.sum(expos, axis=-1, keepdims=True)
                gp = grad_p[:, cut]
                inner = jnp.sum(p * gp, axis=-1, keepdims=True)
                probs.append(p.astype(BF16))
                grad_s.append((p * (gp - inner)).astype(BF16))
            p = jnp.concatenate(probs, axis=1) if hp > 1 else probs[0]
            gs = jnp.concatenate(grad_s, axis=1) if hp > 1 else grad_s[0]
            attended[k, q_rows, :] = dot(p, values, 1, 0).astype(BF16)
            places = pl.ds(q_at, block)
            back = rotated(dot(gs, keys, 1, 0) * (HEAD**-0.5), places, -1.0)
            grad_z[k, q_rows, 0:128] = back.astype(BF16)
            here_rows = pl.ds(k_at, window)
            key_sum[here_rows, :] += unstacked(dot(gs, q, 0, 0))
            value_sum[here_rows, :] += unstacked(dot(p, g, 0, 0))
            return carry

        lax.fori_loop(0, length // block, body, 0)
        rows = pl.ds(pl.multiple_of(s * length, length), length)
        grad_z[k, rows, 128:256] = rotated(key_sum[...], slice(None), -1.0).astype(BF16)
        grad_z[k, rows, 256:384] = value_sum[...].astype(BF16)

    def hidden(k):
        def body(j, carry):
            rows = pl.ds(pl.multiple_of(j * RT, RT), RT)
            u = dot(normed[rows, :], wu[k], 1, 0) + b_up[:, pl.ds(pl.multiple_of(c * units + k * pw, pw), pw)]
            phi = 0.5 * (1.0 + lax.erf(u * np.float32(0.5**0.5)))
            active[k, rows, :] = (u * phi).astype(BF16)
            slope[k, rows, :] = phi + u * (jnp.exp(-0.5 * u * u) * np.float32((2 * np.pi) ** -0.5))
            return carry

        lax.fori_loop(0, tiles, body, 0)

    def hidden_back(k):
        def body(j, carry):
            rows = pl.ds(pl.multiple_of(j * RT, RT), RT)
            grad_u[k, rows, :] = (dot(grads[rows, :], wd[k], 1, 0) * slope[k, rows, :]).astype(BF16)
            return carry

        lax.fori_loop(0, tiles, body, 0)

    HT = min(512, length)

    def branch_rows(a, cc):
        def body(j, carry):
            rows = pl.ds(pl.multiple_of(cc * length + j * HT, HT), HT)
            total = None
            for k in range(na):
                if a == 0:
                    part = dot(attended[k, rows, :], wa[k, :, 384:512], 1, 1)
                else:
                    part = dot(grad_z[k, rows, :], wa[k, :, 0:384], 1, 1)
                total = part if total is None else total + part
            for k in range(nm):
                if a == 0:
                    part = dot(active[k, rows, :], wd[k], 1, 1)
                else:
                    part = dot(grad_u[k, rows, :], wu[k], 1, 1)
                total = total + part
            partials[a][rows, :] = total.astype(BF16)
            return carry

        lax.fori_loop(0, length // HT, body, 0)

    def half_copy(a, cc):
        rows = pl.ds(pl.multiple_of(cc * length, length), length)
        return copy(partials[a].at[rows], core_in, half_send.at[a], half_recv.at[a], partner)

    def branches(a):
        branch_rows(a, 1 - c)
        if a == 1:
            pl.semaphore_wait(credit.at[0], 1)
        half_copy(a, 1 - c).start()
        branch_rows(a, c)

    def turn_copy(a, tt, src):
        rows = pl.ds(pl.multiple_of(c * length + tt * R, R), R)
        return copy(
            partials[a].at[rows], turn_in.at[src], turn_send.at[a, tt], turn_recv.at[a, src], turned(tt)
        )

    def reduce_core(a):
        half_copy(a, 1 - c).wait()
        if a == 1 and nt > 1:
            pl.semaphore_wait(credit.at[1], nt - 1)
        for k in range(nt):
            tt = other_t(k)
            rows = pl.ds(pl.multiple_of(c * length + tt * R, R), R)
            mine = pl.ds(pl.multiple_of(tt * R, R), R)
            both = partials[a][rows, :].astype(F32) + core_in[mine, :].astype(F32)
            if k == 0:
                own_rows[...] = both
            else:
                partials[a][rows, :] = both.astype(BF16)
                turn_copy(a, tt, t).start()
        if a == 0:
            pl.semaphore_signal(credit.at[0], inc=1, device_id=partner, device_id_type=MESH)

    def reduced(a, rows):
        total = own_rows[rows, :]
        for k in range(1, nt):
            total = total + turn_in[other_t(k), rows, :].astype(F32)
        return restore(total)

    def reduce_turn(a):
        for k in range(1, nt):
            turn_copy(a, t, other_t(k)).wait_recv()

    def write_output():
        def body(j, carry):
            rows = pl.ds(pl.multiple_of(j * tile, tile), tile)
            total = tokens[rows, :].astype(F32) + reduced(0, rows) + b_dense[...] + b_down[...]
            output[rows, :] = total.astype(BF16)
            return carry

        lax.fori_loop(0, R // tile, body, 0)
        for k in range(1, nt):
            pl.semaphore_signal(credit.at[1], inc=1, device_id=turned(other_t(k)), device_id_type=MESH)

    def write_input_grad():
        vec[0] = jnp.zeros_like(vec[0])

        def body(j, carry):
            rows = pl.ds(pl.multiple_of(j * tile, tile), tile)
            normal, inverse = normalize(tokens[rows, :].astype(F32))
            up = cotangent[rows, :].astype(F32)
            grad = reduced(1, rows)
            vec[0, 0:1, :] += jnp.sum(grad * normal, axis=0, keepdims=True)
            vec[0, 1:2, :] += jnp.sum(grad, axis=0, keepdims=True)
            vec[0, 2:3, :] += jnp.sum(up, axis=0, keepdims=True)
            scaled = grad * gain[...]
            input_grad[rows, :] = up + inverse * (
                scaled
                - jnp.mean(scaled, axis=-1, keepdims=True)
                - normal * jnp.mean(scaled * normal, axis=-1, keepdims=True)
            )
            return carry

        lax.fori_loop(0, R // tile, body, 0)
        for k in range(nm):
            vec[0, 8:9, k * pw : (k + 1) * pw] = jnp.sum(grad_u[k].astype(F32), axis=0, keepdims=True)
        for k in range(na):
            vec[0, 9:10, k * 512 : k * 512 + 384] = jnp.sum(grad_z[k].astype(F32), axis=0, keepdims=True)

    top, bottom, whole = pl.ds(0, 8), pl.ds(8, 8), pl.ds(0, 16)

    def vec_copy(stage, rows, dst, slot, sem, to):
        return copy(
            vec.at[stage, rows], dst, vec_send.at[stage, slot], vec_recv.at[stage, sem], to
        )

    def small_sums():
        def add(first_sum, second_sum):
            return first_sum + second_sum

        core = vec_copy(0, top, vec_in.at[0, top], 0, 0, partner)
        core.start()
        core.wait_recv()
        vec[1, 0:8] = add(vec[0, 0:8], vec_in[0, 0:8])
        vec[1, 8:16] = vec[0, 8:16]
        vec_t[t] = vec[1, 0:8]
        for k in range(1, nt):
            vec_copy(1, top, vec_t.at[t], other_t(k), t, turned(other_t(k))).start()
        for k in range(1, nt):
            src = other_t(k)
            vec_copy(1, top, vec_t.at[src], t, src, turned(src)).wait_recv()
        total = vec_t[0]
        for k in range(1, nt):
            total = total + vec_t[k]
        vec[2, 0:8] = total
        vec[2, 8:16] = vec[1, 8:16]
        cross = vec_copy(2, whole, vec_in.at[1], 0, 0, across)
        cross.start()
        cross.wait_recv()
        vec[3] = add(vec[2], vec_in[1])
        vec_z[z] = vec[3]
        for k in range(1, nz):
            vec_copy(3, whole, vec_z.at[z], other_z(k), z, along(other_z(k))).start()
        for k in range(1, nz):
            src = other_z(k)
            vec_copy(3, whole, vec_z.at[src], z, src, along(src)).wait_recv()
        total = vec_z[0]
        for k in range(1, nz):
            total = total + vec_z[k]
        vec[4] = total
        last = vec_copy(4, bottom, vec_in.at[2, bottom], 0, 0, partner)
        last.start()
        gain_grad[...] = vec[4, 0:1]
        shift_grad[...] = vec[4, 1:2]
        dense_bias[...] = vec[4, 2:3]
        last.wait_recv()
        for cc in range(2):
            part = jnp.where(c == cc, vec[4, 8:10], vec_in[2, 8:10])
            up_bias[:, cc * units : (cc + 1) * units] = part[0:1, :units]
            for k in range(na):
                row = part[1:2, k * 512 : k * 512 + 384]
                heads = [row[:, p * 128 + h * HEAD : p * 128 + (h + 1) * HEAD] for h in range(hp) for p in range(3)]
                at = (cc * na + k) * wide
                qkv_bias[:, 3 * at : 3 * (at + wide)] = jnp.concatenate(heads, axis=1)
        core.wait_send()
        for k in range(1, nt):
            vec_copy(1, top, vec_t.at[t], other_t(k), t, turned(other_t(k))).wait_send()
        cross.wait_send()
        for k in range(1, nz):
            vec_copy(3, whole, vec_z.at[z], other_z(k), z, along(other_z(k))).wait_send()
        last.wait_send()

    steps = []

    def lead(i, n):
        for d in range(1, nz):
            for j in range(i, min(i + n, len(pieces))):
                steps.append(functools.partial(forward, j, d))
            if d == min(2, nz - 1):
                for j in range(i + n, min(i + 2 * n, len(pieces))):
                    steps.append(functools.partial(send_own, j))

    for i in range(0, len(pieces), 2):
        lead(i, 2)
    steps.reverse()

    def advance(n):
        for _ in range(n):
            if steps:
                steps.pop()()

    per = nz + 1
    send_own(0)
    if len(pieces) > 1:
        send_own(1)
    prepare()
    prepare_docs()
    advance(2)
    act_forward(0)
    advance(len(range(1, nz)) * 2 + 2 - 2)
    act_forward(1)
    act_wait(0)
    act_wait(1)
    for k in range(na):
        gathered(A[k])
        project(k)
        advance(per // 2)
        for s in range(2):
            attend(k, s)
            advance(per // 2)
        weight_grad(A[k])
        advance(1)
    for k in range(nm):
        if k == 0:
            advance(per * 2)
        gathered(U[k])
        hidden(k)
        advance(per)
        weight_grad(Dn[k])
        if k < na:
            scatter_x(A[k])
        advance(per)
    advance(len(steps))
    for k in range(na):
        if k >= nm:
            scatter_x(A[k])
        scatter_z(A[k])
    for k in range(nm):
        gathered(Dn[k])
        hidden_back(k)
        weight_grad(U[k])
        scatter_x(Dn[k])
    act_sent(1)
    act_sent(0)
    branches(0)
    reduce_core(0)
    branches(1)
    for k in range(nm):
        scatter_x(U[k])
    reduce_turn(0)
    write_output()
    reduce_core(1)
    for k in range(nm):
        scatter_z(Dn[k])
    reduce_turn(1)
    write_input_grad()
    small_sums()
    for k in range(nm):
        scatter_z(U[k])
    finish_attention()

    for i in range(len(pieces)):
        if i not in A:
            g_final(i, 1 - c).wait_recv()
        g_final(i, c).wait_send()
        core_copy(i).wait_send()
        for src in range(nz):
            pl.when((z < nz - 1) & (src <= z))(lambda: send_up(i, src).wait_send())
            pl.when((z > 0) & (src >= z))(lambda: send_down(i, src).wait_send())
            send_across(i, src, x).wait_send()
            g_across(i, src).wait_send()
            pl.when(src != z)(lambda: g_along(i, src, z).wait_send())
    for a in range(2):
        for k in range(1, nt):
            turn_copy(a, other_t(k), t).wait_send()
    docs_core.wait_send()


def on_device(
    nt,
    n_dp,
    tokens,
    cotangent,
    segments,
    ln_gain,
    ln_bias,
    w_qkv,
    b_qkv,
    w_dense,
    b_dense,
    w_up,
    b_up,
    w_down,
    b_down,
):
    R, D = tokens.shape
    length = segments.shape[1]
    r = w_qkv.shape[0]
    nz = n_dp // 4
    heads = w_qkv.shape[1] // (3 * HEAD) // 2
    hp = 2 if heads % 2 == 0 else 1
    na = heads // hp
    units = w_up.shape[1] // 2
    pw = 512 if units % 512 == 0 else units
    nm = units // pw
    wide = hp * HEAD
    sizes = dict(nt=nt, nz=nz, na=na, nm=nm, hp=hp, length=length, R=R, r=r, pw=pw)

    widths = ((na, 512), (nm, pw), (nm, pw))
    count = na + 2 * nm
    rows = 2 * length
    half = D // 2
    chip = 2 * r
    V = pltpu.VMEM
    DMA = pltpu.SemaphoreType.DMA
    scratch = (
        [V((2, na, r, 512), BF16), V((na, 1, 384), F32)]
        + [V((length, 128), F32)] * 2
        + [V((2, 8, length), F32), V((length, 128), F32)]
        + [V((n, D, w), BF16) for n, w in widths]
        + [V((rows, D), BF16), V((rows, D), BF16)]
        + [V((rows, 128), BF16)] * 4
        + [V((na, rows, 128), BF16), V((na, rows, 384), BF16)]
        + [V((length, 128), F32)] * 2
        + [V((nm, rows, pw), BF16), V((nm, rows, pw), F32), V((nm, rows, pw), BF16)]
        + [V((length, D), BF16), V((nt, R, D), BF16)]
        + [V((R, D), F32)]
        + [V((n, half, w), F32) for n, w in widths]
        + [V((n, half, w), BF16) for _ in range(4) for n, w in widths]
        + [V((na, r, 512), F32), V((nm, r, pw), F32), V((nm, r, pw), F32)]
        + [V((na, r, 512), F32)] * 2
        + [V((5, 16, D), F32), V((3, 16, D), F32), V((nt, 8, D), F32), V((nz, 16, D), F32)]
        + [DMA((count + 1,)), DMA((2, count + 1))]
        + [DMA((count, nz))] * 5
        + [DMA((2, nt))] * 4
        + [DMA((count, nz))] * 4
        + [DMA((count,))] * 2
        + [DMA((2,))] * 2
        + [DMA((2, nt))] * 2
        + [DMA((5, max(nt, nz)))] * 2
        + [pltpu.SemaphoreType.REGULAR((2,))]
    )
    space = pl.BlockSpec(memory_space=pltpu.VMEM)

    def row(vector):
        return vector.reshape(1, -1)

    args = (
        tokens,
        cotangent,
        segments,
        row(ln_gain),
        row(ln_bias),
        w_qkv,
        row(b_qkv),
        w_dense.T,
        row(b_dense),
        w_up,
        row(b_up),
        w_down.T,
        row(b_down),
    )
    shapes = (
        jax.ShapeDtypeStruct((R, D), BF16),
        jax.ShapeDtypeStruct((R, D), F32),
        jax.ShapeDtypeStruct((1, D), F32),
        jax.ShapeDtypeStruct((1, D), F32),
        jax.ShapeDtypeStruct(w_qkv.shape, F32),
        jax.ShapeDtypeStruct((1, w_qkv.shape[1]), F32),
        jax.ShapeDtypeStruct(w_dense.shape[::-1], F32),
        jax.ShapeDtypeStruct((1, D), F32),
        jax.ShapeDtypeStruct(w_up.shape, F32),
        jax.ShapeDtypeStruct((1, w_up.shape[1]), F32),
        jax.ShapeDtypeStruct(w_down.shape[::-1], F32),
    )
    out = pl.pallas_call(
        functools.partial(kernel, sizes),
        out_shape=shapes,
        in_specs=[space] * len(args),
        out_specs=[space] * len(shapes),
        scratch_shapes=scratch,
        compiler_params=pltpu.CompilerParams(
            collective_id=0, has_side_effects=True, vmem_limit_bytes=67043328
        ),
        name="layer",
    )(*args)
    out = [part.reshape(-1) if part.shape[0] == 1 else part for part in out]
    out[6], out[10] = out[6].T, out[10].T
    return (*out, out[7])


def solution(mesh):
    return jax.shard_map(
        functools.partial(on_device, mesh.shape["tensor"], mesh.shape["dp"]),
        mesh=mesh,
        in_specs=(
            P(("dp", "tensor"), None),
            P(("dp", "tensor"), None),
            P("dp", None),
            P(),
            P(),
            P("dp", "tensor"),
            P("tensor"),
            P("tensor", "dp"),
            P(),
            P("dp", "tensor"),
            P("tensor"),
            P("tensor", "dp"),
            P(),
        ),
        out_specs=(
            P(("dp", "tensor"), None),
            P(("dp", "tensor"), None),
            P(),
            P(),
            P("dp", "tensor"),
            P("tensor"),
            P("tensor", "dp"),
            P(),
            P("dp", "tensor"),
            P("tensor"),
            P("tensor", "dp"),
            P(),
        ),
        check_vma=False,
    )
```

```python
import functools

import jax
import jax.numpy as jnp
import numpy as np
from jax import lax
from jax.experimental import pallas as pl
from jax.experimental.pallas import tpu as pltpu
from jax.sharding import PartitionSpec as P

HEAD = 64
ROT = 16
NORM_EPS = 1e-05
ROTARY_BASE = 10000.0
MESH = pl.DeviceIdType.MESH
F32 = jnp.float32
BF16 = jnp.bfloat16


def dot(left, right, over_left, over_right):
    return lax.dot_general(
        left, right, (((over_left,), (over_right,)), ((), ())), preferred_element_type=F32
    )


def normalize(rows):
    centred = rows - jnp.mean(rows, axis=-1, keepdims=True)
    inverse = lax.rsqrt(jnp.mean(centred * centred, axis=-1, keepdims=True) + NORM_EPS)
    return centred * inverse, inverse


def padded(array):
    rest = -array.shape[1] % 128
    return jnp.concatenate([array, jnp.zeros((array.shape[0], rest), array.dtype)], axis=1) if rest else array


def kernel(
    sizes,
    tokens,
    cotangent,
    segments,
    gain,
    shift,
    w_qkv,
    b_qkv,
    w_dense,
    b_dense,
    w_up,
    b_up,
    w_down,
    b_down,
    output,
    input_grad,
    gain_grad,
    shift_grad,
    qkv_grad,
    qkv_bias,
    dense_grad,
    dense_bias,
    up_grad,
    up_bias,
    down_grad,
    wa_in,
    ba,
    cos_table,
    sin_table,
    docs,
    doc_column,
    wa,
    wu,
    wd,
    normed,
    grads,
    query,
    key,
    value,
    grad_out,
    attended,
    grad_z,
    key_sum,
    value_sum,
    active,
    slope,
    grad_u,
    late,
    core_in,
    corner_x,
    corner_t,
    side_x,
    side_t,
    own_a,
    own_u,
    own_d,
    xs_a,
    xs_u,
    xs_d,
    xr_a,
    xr_u,
    xr_d,
    zs_a,
    zs_u,
    zs_d,
    zu_a,
    zu_u,
    zu_d,
    zd_a,
    zd_u,
    zd_d,
    fs_a,
    fs_u,
    fs_d,
    fr_a,
    fr_u,
    fr_d,
    vec,
    vec_z,
    vec_m,
    local_sem,
    share_send,
    share_recv,
    up_send,
    down_send,
    z_recv,
    x_send,
    x_recv,
    turn_send,
    turn_recv,
    side_send,
    side_recv,
    corner_x_send,
    corner_x_recv,
    corner_t_send,
    corner_t_recv,
    pass_send,
    pass_recv,
    gx_send,
    gx_recv,
    gu_send,
    gu_recv,
    gd_send,
    gd_recv,
    fin_send,
    fin_recv,
    half_send,
    half_recv,
    peer_send,
    peer_recv,
    mate_send,
    mate_recv,
    credit,
):
    nt, nz, gx, na, nm, hp, length, R, r, pw, nbuf = (
        sizes[k] for k in ("nt", "nz", "gx", "na", "nm", "hp", "length", "R", "r", "pw", "nbuf")
    )
    D = tokens.shape[1]
    chip = 2 * r
    zb = gx * chip
    own = D if gx == 2 else D // 2
    members = 2 * gx
    wide = hp * HEAD
    units = nm * pw
    total_rows = members * length
    partials = (grads, late if gx == 2 else normed)
    dp, t = lax.axis_index("dp"), lax.axis_index("tensor")
    z, x, c = dp // 4, (dp // 2) % 2, dp % 2
    j = c * gx + x if gx == 2 else c

    def device(zz, xx, cc, tt):
        return (zz * 4 + xx * 2 + cc, tt)

    partner = device(z, x, 1 - c, t)
    across = device(z, 1 - x, c, t)

    def member(jj):
        return device(z, jj % 2, jj // 2, t) if gx == 2 else device(z, x, jj, t)

    def along(zz):
        return device(zz, x, c, t)

    def turned(tt):
        return device(z, x, c, tt)

    def other_j(k):
        return lax.rem(j + k, members)

    def other_z(k):
        return lax.rem(z + k, nz)

    def other_t(k):
        return lax.rem(t + k, nt)

    def rows_at(start, size):
        return pl.ds(pl.multiple_of(start, size), size)

    def copy(src, dst, send, recv, to):
        return pltpu.make_async_remote_copy(
            src_ref=src, dst_ref=dst, send_sem=send, recv_sem=recv, device_id=to, device_id_type=MESH
        )

    A = list(range(na))
    U = list(range(na, na + nm))
    Dn = list(range(na + nm, na + 2 * nm))
    count = na + 2 * nm

    def of(a, u, d, i):
        if i in A:
            return a.at[i]
        return u.at[i - na] if i in U else d.at[i - na - nm]

    def weights(i):
        return of(wa, wu, wd, i)

    def z_rows(zz):
        return rows_at(zz * zb if gx == 2 else (x * nz + zz) * chip, zb)

    own_rows = rows_at(z * zb + (x * 2 + c) * r if gx == 2 else (x * nz + z) * chip + c * r, r)

    barrier = pltpu.get_barrier_semaphore()
    greeted = [member(other_j(k)) for k in range(1, members)] + ([] if gx == 2 else [across])
    if gx == 1:
        greeted += [device(other_z(k), 1 - x, c, t) for k in range(1, nz)]
    if nt > 1:
        greeted += [
            device(z, jj % 2 if gx == 2 else x, jj // 2 if gx == 2 else jj, other_t(k))
            for k in range(1, nt)
            for jj in [other_j(n) for n in range(1, members)]
        ]
    greeted += [along(other_z(k)) for k in range(1, nz)] + [turned(other_t(k)) for k in range(1, nt)]
    for other in greeted:
        pl.semaphore_signal(barrier, inc=1, device_id=other, device_id_type=MESH)

    def enter():
        pl.semaphore_wait(barrier, len(greeted))

    def part_of(i, jj):
        if i in A:
            return wa_in.at[jj, i]
        ref, k = (w_up, i - na) if i in U else (w_down, i - na - nm)
        return ref.at[:, rows_at(jj * units + k * pw, pw)]

    def local_copy(i):
        return pltpu.make_async_copy(part_of(i, j), weights(i).at[own_rows], local_sem.at[i])

    def give_part(i, jj):
        dst = weights(i).at[own_rows]
        return copy(part_of(i, jj), dst, share_send.at[i, jj], share_recv.at[i, j], member(jj))

    def take_part(i, jj):
        at = z * zb + (jj % 2 * 2 + jj // 2) * r if gx == 2 else (x * nz + z) * chip + jj * r
        dst = weights(i).at[rows_at(at, r)]
        return copy(part_of(i, j), dst, share_send.at[i, jj], share_recv.at[i, jj], member(jj))

    def share(i):
        local_copy(i).start()
        for k in range(1, members):
            give_part(i, other_j(k)).start()

    def head_part(array, jj, k, part):
        at = [((jj * na + k) * hp + h) * 3 * HEAD + part * HEAD for h in range(hp)]
        return padded(jnp.concatenate([array[:, a : a + HEAD] for a in at], axis=1))

    def own_doc(jj):
        return copy(docs.at[j], docs.at[j], share_send.at[count, jj], share_recv.at[count, j], member(jj))

    def doc_of(jj):
        return copy(docs.at[jj], docs.at[jj], share_send.at[count, jj], share_recv.at[count, jj], member(jj))

    def stage():
        for jj in range(members):
            for k in range(na):
                for part in range(3):
                    wa_in[jj, k, :, part * 128 : (part + 1) * 128] = head_part(w_qkv[...], jj, k, part)
                at = (jj * na + k) * wide
                wa_in[jj, k, :, 384:512] = padded(w_dense[:, at : at + wide])
        docs[j] = jnp.broadcast_to(segments[...].astype(F32), docs.shape[1:])

    def give_docs():
        for k in range(1, members):
            own_doc(other_j(k)).start()

    def permute(rows):
        if gx == 2:
            return rows
        return jnp.concatenate(
            [rows[:, (zz * 2 + xx) * chip : (zz * 2 + xx + 1) * chip] for xx in range(2) for zz in range(nz)],
            axis=1,
        )

    def restore(rows):
        if gx == 2:
            return rows
        return jnp.concatenate(
            [rows[:, (xx * nz + zz) * chip : (xx * nz + zz + 1) * chip] for zz in range(nz) for xx in range(2)],
            axis=1,
        )

    acts = (normed, grads)
    tile = min(64, R)
    split = D * 3 // 8
    left, right = slice(0, split), slice(split, D)

    def act_rows(jj, tt):
        return rows_at((jj * nt + tt) * R, R)

    across_j = c * gx + 1 - x if gx == 2 else c

    def fill_normed():
        def body(n, carry):
            rows = rows_at(n * tile, tile)
            normal, _ = normalize(tokens[rows, :].astype(F32))
            normed[rows_at((j * nt + t) * R + n * tile, tile), :] = permute(
                (normal * gain[...] + shift[...]).astype(BF16)
            )
            return carry

        lax.fori_loop(0, R // tile, body, 0)

    def fill_grads():
        def body(n, carry):
            grads[rows_at((j * nt + t) * R + n * tile, tile), :] = permute(cotangent[rows_at(n * tile, tile), :])
            return carry

        lax.fori_loop(0, R // tile, body, 0)

    def act_turn(a, tt, src):
        b = acts[a].at[act_rows(j, src)]
        return copy(b, b, turn_send.at[a, tt], turn_recv.at[a, src], turned(tt))

    def act_side(a, jj):
        b = acts[a].at[act_rows(jj, t)]
        return copy(b, b, side_send.at[a], side_recv.at[a], across)

    def act_corner_x(a, jj, tt):
        b = acts[a].at[act_rows(jj, tt), left]
        return copy(b, b, corner_x_send.at[a, tt], corner_x_recv.at[a, tt], across)

    def act_corner_t(a, tt, src):
        b = acts[a].at[act_rows(across_j, src), right]
        return copy(b, b, corner_t_send.at[a, tt], corner_t_recv.at[a, src], turned(tt))

    def act_pass(a, jj, tt):
        b = acts[a].at[act_rows(jj, tt)]
        return copy(b, b, pass_send.at[a, jj, tt], pass_recv.at[a, jj, tt], partner)

    def act_start(a):
        if gx == 2:
            act_side(a, j).start()
        for k in range(1, nt):
            act_turn(a, other_t(k), t).start()
        act_pass(a, j, t).start()

    def act_from_turn(a):
        for k in range(1, nt):
            src = other_t(k)
            act_turn(a, t, src).wait_recv()
            if gx == 2:
                act_corner_x(a, j, src).start()
            act_pass(a, j, src).start()

    def act_from_side(a):
        if gx == 2:
            act_side(a, across_j).wait_recv()
            for k in range(1, nt):
                act_corner_t(a, other_t(k), t).start()
            act_pass(a, across_j, t).start()

    def act_finish(a):
        if gx == 2:
            for k in range(1, nt):
                src = other_t(k)
                act_corner_x(a, across_j, src).wait_recv()
                act_corner_t(a, t, src).wait_recv()
                act_pass(a, across_j, src).start()

    def act_wait(a):
        for xx in range(gx):
            for k in range(nt):
                act_pass(a, (1 - c) * gx + xx, k).wait_recv()

    def act_sent(a):
        if gx == 2:
            act_side(a, j).wait_send()
        for k in range(1, nt):
            act_turn(a, other_t(k), t).wait_send()
            if gx == 2:
                act_corner_x(a, j, other_t(k)).wait_send()
                act_corner_t(a, other_t(k), t).wait_send()
        for xx in range(gx):
            for k in range(nt):
                act_pass(a, c * gx + xx, k).wait_send()

    def w_block(i, zz):
        return weights(i).at[z_rows(zz)]

    def send_up(i, src):
        b = w_block(i, src)
        return copy(b, b, up_send.at[i, src], z_recv.at[i, src], along(z + 1))

    def send_down(i, src):
        b = w_block(i, src)
        return copy(b, b, down_send.at[i, src], z_recv.at[i, src], along(z - 1))

    def send_across(i, src, xx):
        b = weights(i).at[rows_at((xx * nz + src) * chip, chip)]
        return copy(b, b, x_send.at[i, src], x_recv.at[i, src], across)

    def send_own(i):
        local_copy(i).wait()
        for k in range(1, members):
            take_part(i, other_j(k)).wait_recv()
        pl.when(z < nz - 1)(lambda: send_up(i, z).start())
        pl.when(z > 0)(lambda: send_down(i, z).start())
        if gx == 1:
            send_across(i, z, x).start()

    def forward_up(i, d):
        @pl.when(z >= d)
        def _():
            send_up(i, z - d).wait_recv()
            pl.when(z < nz - 1)(lambda: send_up(i, z - d).start())
            if gx == 1:
                send_across(i, z - d, x).start()

    def forward_down(i, d):
        @pl.when(z + d <= nz - 1)
        def _():
            send_down(i, z + d).wait_recv()
            pl.when(z > 0)(lambda: send_down(i, z + d).start())
            if gx == 1:
                send_across(i, z + d, x).start()

    def gathered(i):
        if gx == 1:
            for src in range(nz):
                send_across(i, src, 1 - x).wait_recv()

    def own_of(i):
        return of(own_a, own_u, own_d, i)

    def g_across(i, to_z):
        b = pl.ds(to_z * chip, chip)
        return copy(
            of(xs_a, xs_u, xs_d, i).at[b],
            of(xr_a, xr_u, xr_d, i).at[b],
            gx_send.at[i, to_z],
            gx_recv.at[i, to_z],
            across,
        )

    def g_up(i, to_z):
        b = rows_at(to_z * zb, zb)
        return copy(
            of(zs_a, zs_u, zs_d, i).at[b],
            of(zu_a, zu_u, zu_d, i).at[b],
            gu_send.at[i, to_z],
            gu_recv.at[i, to_z],
            along(z + 1),
        )

    def g_down(i, to_z):
        b = rows_at(to_z * zb, zb)
        return copy(
            of(zs_a, zs_u, zs_d, i).at[b],
            of(zd_a, zd_u, zd_d, i).at[b],
            gd_send.at[i, to_z],
            gd_recv.at[i, to_z],
            along(z - 1),
        )

    def g_final(i, jj, src):
        at = (jj % 2 * 2 + jj // 2) * r if gx == 2 else jj * r
        return copy(
            of(fs_a, fs_u, fs_d, i).at[rows_at(at, r)],
            of(fr_a, fr_u, fr_d, i).at[src],
            fin_send.at[i, jj],
            fin_recv.at[i, src],
            member(jj),
        )

    def products(i, columns):
        if i in A:
            return [
                (0, 384, dot(normed[:, columns], grad_z[i], 0, 0)),
                (384, 512, dot(grads[:, columns], attended[i], 0, 0)),
            ]
        if i in U:
            return [(0, pw, dot(normed[:, columns], grad_u[i - na], 0, 0))]
        return [(0, pw, dot(grads[:, columns], active[i - na - nm], 0, 0))]

    def weight_grad(i):
        cut = min(512, own)
        if gx == 1:
            xs = of(xs_a, xs_u, xs_d, i)
            for n in range(own // cut):
                for lo, hi, part in products(i, rows_at((1 - x) * own + n * cut, cut)):
                    xs[n * cut : (n + 1) * cut, lo:hi] = part.astype(BF16)
            for to_z in range(nz):
                g_across(i, to_z).start()
        for n in range(own // cut):
            at = n * cut if gx == 2 else x * own + n * cut
            for lo, hi, part in products(i, rows_at(at, cut)):
                own_of(i)[n * cut : (n + 1) * cut, lo:hi] = part

    def sum_x(i):
        if gx == 1:
            xr = of(xr_a, xr_u, xr_d, i)
            for to_z in range(nz):
                g_across(i, to_z).wait_recv()
                b = slice(to_z * chip, (to_z + 1) * chip)
                own_of(i)[b, :] += xr[b, :].astype(F32)

    def chain_step(i, to_z, last, came, buffer, send):
        b = rows_at(to_z * zb, zb)
        zs = of(zs_a, zs_u, zs_d, i)

        @pl.when(last)
        def _():
            zs[b, :] = own_of(i)[b, :].astype(BF16)

        @pl.when(jnp.logical_not(last))
        def _():
            came.wait_recv()
            zs[b, :] = (own_of(i)[b, :] + buffer[b, :].astype(F32)).astype(BF16)

        send.start()

    def chain_up(i, n):
        @pl.when(z <= n)
        def _():
            to_z = nz - 1 - n + z
            chain_step(i, to_z, z == 0, g_up(i, to_z), of(zu_a, zu_u, zu_d, i), g_up(i, to_z))

    def chain_down(i, n):
        @pl.when(nz - 1 - z <= n)
        def _():
            to_z = n - (nz - 1 - z)
            chain_step(i, to_z, z == nz - 1, g_down(i, to_z), of(zd_a, zd_u, zd_d, i), g_down(i, to_z))

    def own_index():
        return x * 2 + c if gx == 2 else c

    def chain_end(i):
        b = rows_at(z * zb, zb)

        @pl.when(z > 0)
        def _():
            g_up(i, z).wait_recv()
            own_of(i)[b, :] += of(zu_a, zu_u, zu_d, i)[b, :].astype(F32)

        @pl.when(z < nz - 1)
        def _():
            g_down(i, z).wait_recv()
            own_of(i)[b, :] += of(zd_a, zd_u, zd_d, i)[b, :].astype(F32)

        of(fs_a, fs_u, fs_d, i)[...] = own_of(i)[b, :].astype(BF16)
        for k in range(1, members):
            g_final(i, other_j(k), j).start()

    def finish(i):
        for k in range(1, members):
            g_final(i, j, other_j(k)).wait_recv()
        keep = own_of(i)[rows_at(z * zb + own_index() * r, r), :]
        came = of(fr_a, fr_u, fr_d, i)
        for jj in range(members):
            part = jnp.where(j == jj, keep, came[jj].astype(F32))
            if i in A:
                heads = [
                    part[:, p * 128 + h * HEAD : p * 128 + (h + 1) * HEAD] for h in range(hp) for p in range(3)
                ]
                at = (jj * na + i) * wide
                qkv_grad[:, 3 * at : 3 * (at + wide)] = jnp.concatenate(heads, axis=1)
                dense_grad[:, at : at + wide] = part[:, 384 : 384 + wide]
            else:
                out, k = (up_grad, i - na) if i in U else (down_grad, i - na - nm)
                out[:, jj * units + k * pw : jj * units + (k + 1) * pw] = part

    def pick(parts):
        total = parts[0]
        for jj in range(1, members):
            total = jnp.where(j == jj, parts[jj], total)
        return total

    def prepare():
        for k in range(na):
            for part in range(3):
                ba[k, :, part * 128 : (part + 1) * 128] = pick(
                    [head_part(b_qkv[...], jj, k, part) for jj in range(members)]
                )
        steps = np.arange(ROT // 2, dtype=np.float32) * 2.0 / ROT
        inverse = (np.float32(ROTARY_BASE) ** -steps).astype(np.float32)
        lane = lax.broadcasted_iota(jnp.int32, (128, 128), 1) % HEAD
        scale = jnp.zeros((128, 128), F32)
        for n in range(ROT):
            scale = jnp.where(lane == n, inverse[n % (ROT // 2)], scale)

        def table(n, carry):
            rows = rows_at(n * 128, 128)
            place = (n * 128 + lax.broadcasted_iota(jnp.int32, (128, 128), 0)).astype(F32)
            cos, sin = jnp.cos(place * scale), jnp.sin(place * scale)
            cos_table[rows, :] = cos
            sin_table[rows, :] = jnp.where(lane < ROT // 2, -sin, sin)
            return carry

        lax.fori_loop(0, length // 128, table, 0)

    lanes_of_doc = 128 // members

    def prepare_docs():
        for k in range(1, members):
            doc_of(other_j(k)).wait_recv()
        for n in range(length // 128):
            cut = slice(n * 128, (n + 1) * 128)
            rows = [jnp.broadcast_to(docs[s, 0:1, cut], (lanes_of_doc, 128)) for s in range(members)]
            doc_column[cut, :] = jnp.transpose(jnp.concatenate(rows, axis=0))

    RT = min(512, total_rows)
    tiles = total_rows // RT
    lanes = lax.broadcasted_iota(jnp.int32, (1, 128), 1)
    first = lanes < HEAD
    low = lanes % HEAD < ROT // 2
    turning = lanes % HEAD < ROT

    def rotated(rows, places, sign):
        near = jnp.where(low, pltpu.roll(rows, 128 - ROT // 2, 1), pltpu.roll(rows, ROT // 2, 1))
        return rows * cos_table[places, :] + jnp.where(turning, sign * near * sin_table[places, :], 0.0)

    def project(k, n):
        rows = rows_at(n * RT, RT)
        places = rows_at(lax.rem(n * RT, length), RT)
        packed = dot(normed[rows, :], wa[k, :, 0:384], 1, 0) + ba[k]
        query[rows, :] = (rotated(packed[:, 0:128], places, 1.0) * (HEAD**-0.5)).astype(BF16)
        key[rows, :] = rotated(packed[:, 128:256], places, 1.0).astype(BF16)
        value[rows, :] = packed[:, 256:384].astype(BF16)

    def project_back(k, n):
        rows = rows_at(n * RT, RT)
        grad_out[rows, :] = dot(grads[rows, :], wa[k, :, 384:512], 1, 0).astype(BF16)

    def each_tile(step, k):
        def body(n, carry):
            step(k, n)
            return carry

        lax.fori_loop(0, tiles, body, 0)

    block = min(128, length // 4)
    window = length // 4 + block

    def stacked(rows):
        if hp == 1:
            return rows
        zero = jnp.zeros_like(rows)
        return jnp.concatenate([jnp.where(first, rows, zero), jnp.where(first, zero, rows)], axis=0)

    def unstacked(rows):
        if hp == 1:
            return rows
        return jnp.where(first, rows[:window], rows[window:])

    def attend(k, s):
        key_sum[...] = jnp.zeros_like(key_sum)
        value_sum[...] = jnp.zeros_like(value_sum)

        def body(n, carry):
            q_at = pl.multiple_of(n * block, block)
            k_at = pl.multiple_of(jnp.maximum(q_at - length // 4, 0), block)
            q_rows = rows_at(s * length + q_at, block)
            k_rows = pl.ds(pl.multiple_of(s * length + k_at, block), window)
            q = query[q_rows, :]
            g = grad_out[q_rows, :]
            keys, values = stacked(key[k_rows, :]), stacked(value[k_rows, :])
            scores = dot(q, keys, 1, 1)
            grad_p = dot(g, values, 1, 1)
            at = k_at + lax.broadcasted_iota(jnp.int32, (block, window), 1)
            here = q_at + lax.broadcasted_iota(jnp.int32, (block, window), 0)
            lane = s * lanes_of_doc
            same = doc_column[pl.ds(q_at, block), lane : lane + 1] == docs[s, 0:1, pl.ds(k_at, window)]
            allowed = same & (at <= here)
            probs, grad_s = [], []
            for h in range(hp):
                cut = slice(h * window, (h + 1) * window)
                sc = jnp.where(allowed, scores[:, cut], -1e30)
                expos = jnp.exp(sc - jnp.max(sc, axis=-1, keepdims=True))
                p = expos / jnp.sum(expos, axis=-1, keepdims=True)
                gp = grad_p[:, cut]
                inner = jnp.sum(p * gp, axis=-1, keepdims=True)
                probs.append(p.astype(BF16))
                grad_s.append((p * (gp - inner)).astype(BF16))
            p = jnp.concatenate(probs, axis=1) if hp > 1 else probs[0]
            gs = jnp.concatenate(grad_s, axis=1) if hp > 1 else grad_s[0]
            attended[k, q_rows, :] = dot(p, values, 1, 0).astype(BF16)
            places = pl.ds(q_at, block)
            back = rotated(dot(gs, keys, 1, 0) * (HEAD**-0.5), places, -1.0)
            grad_z[k, q_rows, 0:128] = back.astype(BF16)
            here_rows = pl.ds(k_at, window)
            key_sum[here_rows, :] += unstacked(dot(gs, q, 0, 0))
            value_sum[here_rows, :] += unstacked(dot(p, g, 0, 0))
            return carry

        lax.fori_loop(0, length // block, body, 0)
        rows = rows_at(s * length, length)
        grad_z[k, rows, 128:256] = rotated(key_sum[...], slice(None), -1.0).astype(BF16)
        grad_z[k, rows, 256:384] = value_sum[...].astype(BF16)

    def hidden(k, n):
        rows = rows_at(n * RT, RT)
        u = dot(normed[rows, :], wu[k], 1, 0) + b_up[:, rows_at(j * units + k * pw, pw)]
        phi = 0.5 * (1.0 + lax.erf(u * np.float32(0.5**0.5)))
        active[k, rows, :] = (u * phi).astype(BF16)
        slope[k, rows, :] = phi + u * (jnp.exp(-0.5 * u * u) * np.float32((2 * np.pi) ** -0.5))

    def hidden_back(k, n):
        rows = rows_at(n * RT, RT)
        grad_u[k, rows, :] = (dot(grads[rows, :], wd[k], 1, 0) * slope[k, rows, :]).astype(BF16)

    per_core = gx * length
    HT = min(512, per_core)

    def branch_rows(a, cc):
        def body(n, carry):
            rows = rows_at(cc * per_core + n * HT, HT)
            total = None
            for k in range(na):
                if a == 0:
                    part = dot(attended[k, rows, :], wa[k, :, 384:512], 1, 1)
                else:
                    part = dot(grad_z[k, rows, :], wa[k, :, 0:384], 1, 1)
                total = part if total is None else total + part
            for k in range(nm):
                if a == 0:
                    part = dot(active[k, rows, :], wd[k], 1, 1)
                else:
                    part = dot(grad_u[k, rows, :], wu[k], 1, 1)
                total = total + part
            partials[a][rows, :] = total.astype(BF16)
            return carry

        lax.fori_loop(0, per_core // HT, body, 0)

    def half_copy(a, cc):
        rows = rows_at(cc * per_core, per_core)
        return copy(partials[a].at[rows], core_in.at[a % nbuf], half_send.at[a], half_recv.at[a], partner)

    def branches_give(a):
        branch_rows(a, 1 - c)
        if nbuf == 1 and a == second:
            pl.semaphore_wait(credit.at[0], 1)
        half_copy(a, 1 - c).start()

    def branches_keep(a):
        branch_rows(a, c)

    def block_rows(jj, tt):
        return rows_at((jj * nt + tt) * R, R)

    def in_rows(jj, tt):
        return rows_at(((jj - c * gx) * nt + tt) * R, R)

    def both_cores(a, jj, tt, columns=slice(None)):
        return (
            partials[a][block_rows(jj, tt), columns].astype(F32)
            + core_in[a % nbuf, in_rows(jj, tt), columns].astype(F32)
        )

    def corner_t_copy(a, tt, src):
        b = partials[a].at[block_rows(across_j, tt), left]
        return copy(b, corner_t.at[a % nbuf, src], corner_t_send.at[2 + a, tt], corner_t_recv.at[2 + a, src], turned(tt))

    def corner_x_copy(a, jj, tt):
        b = partials[a].at[block_rows(jj, tt), right]
        return copy(b, corner_x.at[a % nbuf, tt], corner_x_send.at[2 + a, tt], corner_x_recv.at[2 + a, tt], across)

    def side_copy(a, jj):
        b = partials[a].at[block_rows(jj, t)]
        return copy(b, side_x.at[a % nbuf], side_send.at[2 + a], side_recv.at[2 + a], across)

    def turn_copy(a, tt, src):
        b = partials[a].at[block_rows(j, tt)]
        return copy(b, side_t.at[a % nbuf, src], turn_send.at[2 + a, tt], turn_recv.at[2 + a, src], turned(tt))

    def reduce_corner(a):
        half_copy(a, 1 - c).wait_recv()
        if gx == 2:
            for k in range(1, nt):
                tt = other_t(k)
                partials[a][block_rows(across_j, tt), :] = both_cores(a, across_j, tt).astype(BF16)
                corner_t_copy(a, tt, t).start()
                corner_x_copy(a, across_j, tt).start()

    def reduce_side(a):
        if gx == 2:
            total = both_cores(a, across_j, t, left)
            for k in range(1, nt):
                corner_t_copy(a, t, other_t(k)).wait_recv()
                total = total + corner_t[a % nbuf, other_t(k)].astype(F32)
            partials[a][block_rows(across_j, t), left] = total.astype(BF16)
            partials[a][block_rows(across_j, t), right] = both_cores(a, across_j, t, right).astype(BF16)
            side_copy(a, across_j).start()

    def reduce_turn(a):
        if nbuf == 1 and a == second and nt > 1:
            pl.semaphore_wait(credit.at[1], nt - 1)
        for k in range(1, nt):
            tt = other_t(k)
            if gx == 2:
                corner_x_copy(a, j, tt).wait_recv()
                total = both_cores(a, j, tt, right) + corner_x[a % nbuf, tt].astype(F32)
                partials[a][block_rows(j, tt), right] = total.astype(BF16)
                partials[a][block_rows(j, tt), left] = both_cores(a, j, tt, left).astype(BF16)
            else:
                partials[a][block_rows(j, tt), :] = both_cores(a, j, tt).astype(BF16)
            turn_copy(a, tt, t).start()

    def reduce_wait(a):
        if gx == 2:
            side_copy(a, across_j).wait_recv()
        for k in range(1, nt):
            turn_copy(a, t, other_t(k)).wait_recv()

    def reduced(a, n):
        mine = rows_at((j * nt + t) * R + n * tile, tile)
        came = rows_at(((j - c * gx) * nt + t) * R + n * tile, tile)
        rows = rows_at(n * tile, tile)
        total = partials[a][mine, :].astype(F32) + core_in[a % nbuf, came, :].astype(F32)
        if gx == 2:
            total = total + side_x[a % nbuf, rows, :].astype(F32)
        for k in range(1, nt):
            total = total + side_t[a % nbuf, other_t(k), rows, :].astype(F32)
        return restore(total)

    def reduce_sent(a):
        half_copy(a, 1 - c).wait_send()
        if gx == 2:
            side_copy(a, across_j).wait_send()
        for k in range(1, nt):
            tt = other_t(k)
            turn_copy(a, tt, t).wait_send()
            if gx == 2:
                corner_t_copy(a, tt, t).wait_send()
                corner_x_copy(a, across_j, tt).wait_send()

    def free_buffers():
        if nbuf == 1:
            pl.semaphore_signal(credit.at[0], inc=1, device_id=partner, device_id_type=MESH)
            for k in range(1, nt):
                pl.semaphore_signal(credit.at[1], inc=1, device_id=turned(other_t(k)), device_id_type=MESH)

    def write_output():
        def body(n, carry):
            rows = rows_at(n * tile, tile)
            total = tokens[rows, :].astype(F32) + reduced(0, n) + b_dense[...] + b_down[...]
            output[rows, :] = total.astype(BF16)
            return carry

        lax.fori_loop(0, R // tile, body, 0)

    def sum_biases():
        vec[...] = jnp.zeros_like(vec)
        for k in range(nm):
            vec[3:4, k * pw : (k + 1) * pw] = jnp.sum(grad_u[k].astype(F32), axis=0, keepdims=True)
        for k in range(na):
            at = units + k * 384
            vec[3:4, at : at + 384] = jnp.sum(grad_z[k].astype(F32), axis=0, keepdims=True)

    def write_input_grad():
        def body(n, carry):
            rows = rows_at(n * tile, tile)
            normal, inverse = normalize(tokens[rows, :].astype(F32))
            up = cotangent[rows, :].astype(F32)
            grad = reduced(1, n)
            vec[0:1, :] += jnp.sum(grad * normal, axis=0, keepdims=True)
            vec[1:2, :] += jnp.sum(grad, axis=0, keepdims=True)
            vec[2:3, :] += jnp.sum(up, axis=0, keepdims=True)
            scaled = grad * gain[...]
            input_grad[rows, :] = up + inverse * (
                scaled
                - jnp.mean(scaled, axis=-1, keepdims=True)
                - normal * jnp.mean(scaled * normal, axis=-1, keepdims=True)
            )
            return carry

        lax.fori_loop(0, R // tile, body, 0)

    peers = nz if gx == 2 else 2 * nz
    mates = members * nt
    peer = z if gx == 2 else z * 2 + x
    mate = j * nt + t

    def peer_copy(to, src):
        device_to = device(to, x, c, t) if gx == 2 else device(to // 2, to % 2, c, t)
        return copy(vec_z.at[peer], vec_z.at[src], peer_send.at[to], peer_recv.at[src], device_to)

    def mate_copy(to, src):
        jj, tt = to // nt, to % nt
        device_to = device(z, jj % 2, jj // 2, tt) if gx == 2 else device(z, x, jj, tt)
        return copy(vec_m.at[mate], vec_m.at[src], mate_send.at[to], mate_recv.at[src], device_to)

    def sums_start():
        vec_z[peer] = vec[...]
        for k in range(1, peers):
            peer_copy(lax.rem(peer + k, peers), peer).start()

    def sums_group():
        for k in range(1, peers):
            peer_copy(peer, lax.rem(peer + k, peers)).wait_recv()
        total = vec_z[0]
        for k in range(1, peers):
            total = total + vec_z[k]
        vec_m[mate] = total
        for k in range(1, mates):
            mate_copy(lax.rem(mate + k, mates), mate).start()

    def sums_end():
        for k in range(1, mates):
            mate_copy(mate, lax.rem(mate + k, mates)).wait_recv()
        total = vec_m[0]
        for k in range(1, mates):
            total = total + vec_m[k]
        gain_grad[...] = total[0:1]
        shift_grad[...] = total[1:2]
        dense_bias[...] = total[2:3]
        for jj in range(members):
            row = vec_m[jj * nt + t][3:4]
            up_bias[:, jj * units : (jj + 1) * units] = row[:, :units]
            for k in range(na):
                part = row[:, units + k * 384 : units + (k + 1) * 384]
                heads = [part[:, p * 128 + h * HEAD : p * 128 + (h + 1) * HEAD] for h in range(hp) for p in range(3)]
                at = (jj * na + k) * wide
                qkv_bias[:, 3 * at : 3 * (at + wide)] = jnp.concatenate(heads, axis=1)

    def sums_sent():
        for k in range(1, peers):
            peer_copy(lax.rem(peer + k, peers), peer).wait_send()
        for k in range(1, mates):
            mate_copy(lax.rem(mate + k, mates), mate).wait_send()

    def forwards(some, lo, hi):
        for d in range(lo, hi):
            for i in some:
                forward_up(i, d)
                forward_down(i, d)

    def chains(some, lo, hi):
        for n in range(lo, hi):
            for i in some:
                chain_up(i, n)
                chain_down(i, n)

    second = 0 if gx == 2 else 1

    def any_order():
        stage()
        fill_normed()
        enter()
        for i in U + A + Dn:
            share(i)
        give_docs()
        act_start(0)
        fill_grads()
        act_start(1)
        for i in U + A:
            send_own(i)
        prepare()
        prepare_docs()
        forwards(U + A, 1, 2)
        act_from_turn(0)
        act_from_side(0)
        for i in Dn:
            send_own(i)
        forwards(U, 2, nz)
        act_finish(0)
        act_wait(0)
        for i in U:
            gathered(i)
            each_tile(hidden, i - na)
        act_from_turn(1)
        act_from_side(1)
        forwards(A, 2, nz)
        forwards(Dn, 1, nz)
        act_finish(1)
        act_wait(1)
        for i in Dn:
            weight_grad(i)
            sum_x(i)
        chains(Dn, 0, nz - 1)
        for i in A:
            gathered(i)
            each_tile(project, i)
            each_tile(project_back, i)
            for s in range(members):
                attend(i, s)
            weight_grad(i)
            sum_x(i)
        chains(A, 0, nz - 1)
        for i in Dn:
            gathered(i)
            each_tile(hidden_back, i - na - nm)
        for i in U:
            weight_grad(i)
            sum_x(i)
        act_sent(0)
        act_sent(1)
        sum_biases()
        for a in (1, 0) if gx == 2 else (0, 1):
            branches_give(a)
            branches_keep(a)
            reduce_corner(a)
            if a != second:
                chains(U, 0, nz - 1)
            reduce_side(a)
            reduce_turn(a)
            if a != second:
                for i in Dn + A:
                    chain_end(i)
            reduce_wait(a)
            if a == 0:
                write_output()
            else:
                write_input_grad()
                sums_start()
            if a != second:
                free_buffers()
        for i in U:
            chain_end(i)
        sums_group()
        for i in Dn + A + U:
            finish(i)
        sums_end()

    def tuned_order():
        (a,), (u,), (d,) = A, U, Dn
        fill_normed()
        stage()
        enter()
        share(u)
        share(a)
        give_docs()
        fill_grads()
        send_own(u)
        act_start(0)
        send_own(a)
        forward_up(u, 1)
        forward_down(u, 1)
        act_start(1)
        act_from_side(0)
        forward_down(a, 1)
        act_from_turn(0)
        forward_up(a, 1)
        share(d)
        forward_down(u, 2)
        forward_down(a, 2)
        forward_up(u, 2)
        act_from_side(1)
        act_from_turn(1)
        forward_up(a, 2)
        prepare_docs()
        act_finish(0)
        forward_up(u, 3)
        act_wait(0)
        forward_down(u, 3)
        hidden(0, 1)
        prepare()
        send_own(d)
        hidden(0, 2)
        forward_down(a, 3)
        forward_up(a, 3)
        project(0, 0)
        hidden(0, 3)
        project(0, 2)
        project(0, 3)
        hidden(0, 0)
        act_finish(1)
        project(0, 1)
        act_wait(1)
        weight_grad(d)
        chain_up(d, 0)
        chain_down(d, 0)
        forward_up(d, 1)
        forward_down(d, 1)
        each_tile(project_back, 0)
        attend(0, 0)
        attend(0, 1)
        forward_up(d, 2)
        chain_down(d, 1)
        forward_down(d, 2)
        chain_up(d, 1)
        attend(0, 3)
        attend(0, 2)
        weight_grad(a)
        forward_down(d, 3)
        forward_up(d, 3)
        chain_down(d, 2)
        chain_up(d, 2)
        hidden_back(0, 2)
        hidden_back(0, 0)
        hidden_back(0, 3)
        hidden_back(0, 1)
        weight_grad(u)
        chain_up(a, 0)
        branches_give(1)
        chain_down(a, 0)
        act_sent(0)
        act_sent(1)
        branches_give(0)
        chain_end(d)
        branches_keep(1)
        reduce_corner(1)
        chain_down(u, 0)
        branches_keep(0)
        chain_up(u, 0)
        reduce_corner(0)
        finish(d)
        reduce_side(1)
        chain_up(u, 1)
        chain_down(a, 1)
        chain_up(a, 1)
        reduce_turn(1)
        chain_down(u, 1)
        sum_biases()
        reduce_side(0)
        chain_up(u, 2)
        reduce_turn(0)
        chain_down(u, 2)
        reduce_wait(1)
        write_input_grad()
        chain_end(u)
        sums_start()
        chain_down(a, 2)
        chain_up(a, 2)
        sums_group()
        chain_end(a)
        sums_end()
        reduce_wait(0)
        write_output()
        finish(u)
        finish(a)

    if (gx, na, nm, nz, tiles) == (2, 1, 1, 4, 4):
        tuned_order()
    else:
        any_order()

    for i in range(count):
        for k in range(1, members):
            g_final(i, other_j(k), j).wait_send()
            give_part(i, other_j(k)).wait_send()
        for src in range(nz):
            pl.when((z < nz - 1) & (src <= z))(lambda: send_up(i, src).wait_send())
            pl.when((z > 0) & (src >= z))(lambda: send_down(i, src).wait_send())
            pl.when(src > z)(lambda: g_up(i, src).wait_send())
            pl.when(src < z)(lambda: g_down(i, src).wait_send())
            if gx == 1:
                send_across(i, src, x).wait_send()
                g_across(i, src).wait_send()
    for k in range(1, members):
        own_doc(other_j(k)).wait_send()
    reduce_sent(0)
    reduce_sent(1)
    sums_sent()


def on_device(
    nt,
    n_dp,
    tokens,
    cotangent,
    segments,
    ln_gain,
    ln_bias,
    w_qkv,
    b_qkv,
    w_dense,
    b_dense,
    w_up,
    b_up,
    w_down,
    b_down,
):
    R, D = tokens.shape
    length = segments.shape[1]
    r = w_qkv.shape[0]
    nz = n_dp // 4
    heads = w_qkv.shape[1] // (3 * HEAD)
    gx = 2 if heads % 4 == 0 and 4 * length * D <= 1 << 21 else 1
    members = 2 * gx
    heads = heads // members
    hp = 2 if heads % 2 == 0 else 1
    na = heads // hp
    units = w_up.shape[1] // members
    pw = 512 if units % 512 == 0 else units
    nm = units // pw
    nbuf = gx
    peers, mates = (nz if gx == 2 else 2 * nz), members * nt
    sizes = dict(nt=nt, nz=nz, gx=gx, na=na, nm=nm, hp=hp, length=length, R=R, r=r, pw=pw, nbuf=nbuf)

    widths = ((na, 512), (nm, pw), (nm, pw))
    count = na + 2 * nm
    rows = members * length
    own = D if gx == 2 else D // 2
    chip = 2 * r
    split = D * 3 // 8
    V = pltpu.VMEM
    DMA = pltpu.SemaphoreType.DMA

    def some(shape):
        return V(shape if gx == 2 else (1, 1, 8, 128)[-len(shape) :], BF16)

    scratch = (
        [V((members, na, r, 512), BF16), V((na, 1, 384), F32)]
        + [V((length, 128), F32)] * 2
        + [V((members, 8, length), F32), V((length, 128), F32)]
        + [V((n, D, w), BF16) for n, w in widths]
        + [V((rows, D), BF16), V((rows, D), BF16)]
        + [V((rows, 128), BF16)] * 4
        + [V((na, rows, 128), BF16), V((na, rows, 384), BF16)]
        + [V((length, 128), F32)] * 2
        + [V((nm, rows, pw), BF16), V((nm, rows, pw), F32), V((nm, rows, pw), BF16)]
        + [V((rows, D) if gx == 2 else (8, 128), BF16)]
        + [V((nbuf, gx * length, D), BF16), some((nbuf, nt, R, D - split)), some((nbuf, nt, R, split))]
        + [some((nbuf, R, D)), V((nbuf, nt, R, D), BF16)]
        + [V((n, own, w), F32) for n, w in widths]
        + [V((n, own, w) if gx == 1 else (n, 8, 128), BF16) for _ in range(2) for n, w in widths]
        + [V((n, own, w), BF16) for _ in range(3) for n, w in widths]
        + [V((n, gx * chip, w), BF16) for n, w in widths]
        + [V((n, members, r, w), BF16) for n, w in widths]
        + [V((8, D), F32), V((peers, 8, D), F32), V((mates, 8, D), F32)]
        + [DMA((count,)), DMA((count + 1, members)), DMA((count + 1, members))]
        + [DMA((count, nz))] * 5
        + [DMA((4, nt))] * 2
        + [DMA((4,))] * 2
        + [DMA((4, nt))] * 4
        + [DMA((2, members, nt))] * 2
        + [DMA((count, nz))] * 6
        + [DMA((count, members))] * 2
        + [DMA((2,))] * 2
        + [DMA((peers,))] * 2
        + [DMA((mates,))] * 2
        + [pltpu.SemaphoreType.REGULAR((2,))]
    )
    space = pl.BlockSpec(memory_space=pltpu.VMEM)

    def row(vector):
        return vector.reshape(1, -1)

    args = (
        tokens,
        cotangent,
        segments,
        row(ln_gain),
        row(ln_bias),
        w_qkv,
        row(b_qkv),
        w_dense.T,
        row(b_dense),
        w_up,
        row(b_up),
        w_down.T,
        row(b_down),
    )
    shapes = (
        jax.ShapeDtypeStruct((R, D), BF16),
        jax.ShapeDtypeStruct((R, D), F32),
        jax.ShapeDtypeStruct((1, D), F32),
        jax.ShapeDtypeStruct((1, D), F32),
        jax.ShapeDtypeStruct(w_qkv.shape, F32),
        jax.ShapeDtypeStruct((1, w_qkv.shape[1]), F32),
        jax.ShapeDtypeStruct(w_dense.shape[::-1], F32),
        jax.ShapeDtypeStruct((1, D), F32),
        jax.ShapeDtypeStruct(w_up.shape, F32),
        jax.ShapeDtypeStruct((1, w_up.shape[1]), F32),
        jax.ShapeDtypeStruct(w_down.shape[::-1], F32),
    )
    out = pl.pallas_call(
        functools.partial(kernel, sizes),
        out_shape=shapes,
        in_specs=[space] * len(args),
        out_specs=[space] * len(shapes),
        scratch_shapes=scratch,
        compiler_params=pltpu.CompilerParams(
            collective_id=0, has_side_effects=True, vmem_limit_bytes=67043328
        ),
        name="layer",
    )(*args)
    out = [part.reshape(-1) if part.shape[0] == 1 else part for part in out]
    out[6], out[10] = out[6].T, out[10].T
    return (*out, out[7])


def solution(mesh):
    return jax.shard_map(
        functools.partial(on_device, mesh.shape["tensor"], mesh.shape["dp"]),
        mesh=mesh,
        in_specs=(
            P(("dp", "tensor"), None),
            P(("dp", "tensor"), None),
            P("dp", None),
            P(),
            P(),
            P("dp", "tensor"),
            P("tensor"),
            P("tensor", "dp"),
            P(),
            P("dp", "tensor"),
            P("tensor"),
            P("tensor", "dp"),
            P(),
        ),
        out_specs=(
            P(("dp", "tensor"), None),
            P(("dp", "tensor"), None),
            P(),
            P(),
            P("dp", "tensor"),
            P("tensor"),
            P("tensor", "dp"),
            P(),
            P("dp", "tensor"),
            P("tensor"),
            P("tensor", "dp"),
            P(),
        ),
        check_vma=False,
    )
```

```python
import functools

import jax
import jax.numpy as jnp
import numpy as np
from jax import lax
from jax.experimental import pallas as pl
from jax.experimental.pallas import tpu as pltpu
from jax.sharding import PartitionSpec as P

HEAD = 64
ROT = 16
NORM_EPS = 1e-05
ROTARY_BASE = 10000.0
MESH = pl.DeviceIdType.MESH
F32 = jnp.float32
BF16 = jnp.bfloat16


def dot(left, right, over_left, over_right):
    return lax.dot_general(
        left, right, (((over_left,), (over_right,)), ((), ())), preferred_element_type=F32
    )


def normalize(rows):
    centred = rows - jnp.mean(rows, axis=-1, keepdims=True)
    inverse = lax.rsqrt(jnp.mean(centred * centred, axis=-1, keepdims=True) + NORM_EPS)
    return centred * inverse, inverse


def padded(array):
    rest = -array.shape[1] % 128
    return jnp.concatenate([array, jnp.zeros((array.shape[0], rest), array.dtype)], axis=1) if rest else array


def kernel(
    sizes,
    tokens,
    cotangent,
    segments,
    gain,
    shift,
    w_qkv,
    b_qkv,
    w_dense,
    b_dense,
    w_up,
    b_up,
    w_down,
    b_down,
    output,
    input_grad,
    gain_grad,
    shift_grad,
    qkv_grad,
    qkv_bias,
    dense_grad,
    dense_bias,
    up_grad,
    up_bias,
    down_grad,
    wa_in,
    ba,
    cos_table,
    sin_table,
    docs,
    doc_column,
    wa,
    wu,
    wd,
    normed,
    grads,
    query,
    key,
    value,
    grad_out,
    attended,
    grad_z,
    key_sum,
    value_sum,
    active,
    slope,
    grad_u,
    late,
    core_in,
    corner_x,
    corner_t,
    side_x,
    side_t,
    own_a,
    own_u,
    own_d,
    xs_a,
    xs_u,
    xs_d,
    xr_a,
    xr_u,
    xr_d,
    zs_a,
    zs_u,
    zs_d,
    zu_a,
    zu_u,
    zu_d,
    zd_a,
    zd_u,
    zd_d,
    fs_a,
    fs_u,
    fs_d,
    fr_a,
    fr_u,
    fr_d,
    vec,
    vec_z,
    vec_m,
    local_sem,
    share_send,
    share_recv,
    up_send,
    down_send,
    z_recv,
    x_send,
    x_recv,
    turn_send,
    turn_recv,
    side_send,
    side_recv,
    corner_x_send,
    corner_x_recv,
    corner_t_send,
    corner_t_recv,
    pass_send,
    pass_recv,
    gx_send,
    gx_recv,
    gu_send,
    gu_recv,
    gd_send,
    gd_recv,
    fin_send,
    fin_recv,
    half_send,
    half_recv,
    peer_send,
    peer_recv,
    mate_send,
    mate_recv,
    credit,
):
    nt, nz, gx, na, nm, hp, length, R, r, pw, nbuf = (
        sizes[k] for k in ("nt", "nz", "gx", "na", "nm", "hp", "length", "R", "r", "pw", "nbuf")
    )
    D = tokens.shape[1]
    chip = 2 * r
    zb = gx * chip
    own = D if gx == 2 else D // 2
    members = 2 * gx
    wide = hp * HEAD
    units = nm * pw
    total_rows = members * length
    partials = (grads, late if gx == 2 else normed)
    dp, t = lax.axis_index("dp"), lax.axis_index("tensor")
    z, x, c = dp // 4, (dp // 2) % 2, dp % 2
    j = c * gx + x if gx == 2 else c

    def device(zz, xx, cc, tt):
        return (zz * 4 + xx * 2 + cc, tt)

    partner = device(z, x, 1 - c, t)
    across = device(z, 1 - x, c, t)

    def member(jj):
        return device(z, jj % 2, jj // 2, t) if gx == 2 else device(z, x, jj, t)

    def along(zz):
        return device(zz, x, c, t)

    def turned(tt):
        return device(z, x, c, tt)

    def other_j(k):
        return lax.rem(j + k, members)

    def other_z(k):
        return lax.rem(z + k, nz)

    def other_t(k):
        return lax.rem(t + k, nt)

    def rows_at(start, size):
        return pl.ds(pl.multiple_of(start, size), size)

    def copy(src, dst, send, recv, to):
        return pltpu.make_async_remote_copy(
            src_ref=src, dst_ref=dst, send_sem=send, recv_sem=recv, device_id=to, device_id_type=MESH
        )

    A = list(range(na))
    U = list(range(na, na + nm))
    Dn = list(range(na + nm, na + 2 * nm))
    count = na + 2 * nm

    def of(a, u, d, i):
        if i in A:
            return a.at[i]
        return u.at[i - na] if i in U else d.at[i - na - nm]

    def weights(i):
        return of(wa, wu, wd, i)

    def z_rows(zz):
        return rows_at(zz * zb if gx == 2 else (x * nz + zz) * chip, zb)

    own_rows = rows_at(z * zb + (x * 2 + c) * r if gx == 2 else (x * nz + z) * chip + c * r, r)

    barrier = pltpu.get_barrier_semaphore()
    greeted = [member(other_j(k)) for k in range(1, members)] + ([] if gx == 2 else [across])
    if gx == 1:
        greeted += [device(other_z(k), 1 - x, c, t) for k in range(1, nz)]
    if nt > 1:
        greeted += [
            device(z, jj % 2 if gx == 2 else x, jj // 2 if gx == 2 else jj, other_t(k))
            for k in range(1, nt)
            for jj in [other_j(n) for n in range(1, members)]
        ]
    greeted += [along(other_z(k)) for k in range(1, nz)] + [turned(other_t(k)) for k in range(1, nt)]
    for other in greeted:
        pl.semaphore_signal(barrier, inc=1, device_id=other, device_id_type=MESH)

    def enter():
        pl.semaphore_wait(barrier, len(greeted))

    def part_of(i, jj):
        if i in A:
            return wa_in.at[jj, i]
        ref, k = (w_up, i - na) if i in U else (w_down, i - na - nm)
        return ref.at[:, rows_at(jj * units + k * pw, pw)]

    def local_copy(i):
        return pltpu.make_async_copy(part_of(i, j), weights(i).at[own_rows], local_sem.at[i])

    def give_part(i, jj):
        dst = weights(i).at[own_rows]
        return copy(part_of(i, jj), dst, share_send.at[i, jj], share_recv.at[i, j], member(jj))

    def take_part(i, jj):
        at = z * zb + (jj % 2 * 2 + jj // 2) * r if gx == 2 else (x * nz + z) * chip + jj * r
        dst = weights(i).at[rows_at(at, r)]
        return copy(part_of(i, j), dst, share_send.at[i, jj], share_recv.at[i, jj], member(jj))

    def share(i):
        local_copy(i).start()
        for k in range(1, members):
            give_part(i, other_j(k)).start()

    def head_part(array, jj, k, part):
        at = [((jj * na + k) * hp + h) * 3 * HEAD + part * HEAD for h in range(hp)]
        return padded(jnp.concatenate([array[:, a : a + HEAD] for a in at], axis=1))

    def own_doc(jj):
        return copy(docs.at[j], docs.at[j], share_send.at[count, jj], share_recv.at[count, j], member(jj))

    def doc_of(jj):
        return copy(docs.at[jj], docs.at[jj], share_send.at[count, jj], share_recv.at[count, jj], member(jj))

    def stage():
        for jj in range(members):
            for k in range(na):
                for part in range(3):
                    wa_in[jj, k, :, part * 128 : (part + 1) * 128] = head_part(w_qkv[...], jj, k, part)
                at = (jj * na + k) * wide
                wa_in[jj, k, :, 384:512] = padded(w_dense[:, at : at + wide])
        docs[j] = jnp.broadcast_to(segments[...].astype(F32), docs.shape[1:])

    def give_docs():
        for k in range(1, members):
            own_doc(other_j(k)).start()

    def permute(rows):
        if gx == 2:
            return rows
        return jnp.concatenate(
            [rows[:, (zz * 2 + xx) * chip : (zz * 2 + xx + 1) * chip] for xx in range(2) for zz in range(nz)],
            axis=1,
        )

    def restore(rows):
        if gx == 2:
            return rows
        return jnp.concatenate(
            [rows[:, (xx * nz + zz) * chip : (xx * nz + zz + 1) * chip] for zz in range(nz) for xx in range(2)],
            axis=1,
        )

    acts = (normed, grads)
    tile = min(64, R)
    split = D * 3 // 8
    over_x, over_t = slice(0, split), slice(split, D)
    back_split = D // 4
    back_x, back_t = slice(0, back_split), slice(back_split, D)

    def act_rows(jj, tt):
        return rows_at((jj * nt + tt) * R, R)

    across_j = c * gx + 1 - x if gx == 2 else c
    partner_j = (1 - c) * gx + x if gx == 2 else 1 - c
    far_j = (1 - c) * gx + 1 - x if gx == 2 else 1 - c
    near = (j, partner_j, across_j, far_j)

    def fill_normed():
        def body(n, carry):
            rows = rows_at(n * tile, tile)
            normal, _ = normalize(tokens[rows, :].astype(F32))
            normed[rows_at((j * nt + t) * R + n * tile, tile), :] = permute(
                (normal * gain[...] + shift[...]).astype(BF16)
            )
            return carry

        lax.fori_loop(0, R // tile, body, 0)

    def fill_grads():
        def body(n, carry):
            grads[rows_at((j * nt + t) * R + n * tile, tile), :] = permute(cotangent[rows_at(n * tile, tile), :])
            return carry

        lax.fori_loop(0, R // tile, body, 0)

    def act_turn(a, tt, src):
        b = acts[a].at[act_rows(j, src)]
        return copy(b, b, turn_send.at[a, tt], turn_recv.at[a, src], turned(tt))

    def act_side(a, jj):
        b = acts[a].at[act_rows(jj, t)]
        return copy(b, b, side_send.at[a], side_recv.at[a], across)

    def act_corner_x(a, jj, tt):
        b = acts[a].at[act_rows(jj, tt), over_x]
        return copy(b, b, corner_x_send.at[a, tt], corner_x_recv.at[a, tt], across)

    def act_corner_t(a, tt, src):
        b = acts[a].at[act_rows(across_j, src), over_t]
        return copy(b, b, corner_t_send.at[a, tt], corner_t_recv.at[a, src], turned(tt))

    def act_pass(a, jj, tt):
        b = acts[a].at[act_rows(jj, tt)]
        return copy(b, b, pass_send.at[a, jj, tt], pass_recv.at[a, jj, tt], partner)

    def act_start_side(a):
        if gx == 2:
            act_side(a, j).start()

    def act_start_turn(a):
        for k in range(1, nt):
            act_turn(a, other_t(k), t).start()
        act_pass(a, j, t).start()

    def act_start(a):
        act_start_side(a)
        act_start_turn(a)

    def act_from_turn(a):
        for k in range(1, nt):
            src = other_t(k)
            act_turn(a, t, src).wait_recv()
            if gx == 2:
                act_corner_x(a, j, src).start()
            act_pass(a, j, src).start()

    def act_from_side(a):
        if gx == 2:
            act_side(a, across_j).wait_recv()
            for k in range(1, nt):
                act_corner_t(a, other_t(k), t).start()
            act_pass(a, across_j, t).start()

    def act_finish(a):
        if gx == 2:
            for k in range(1, nt):
                src = other_t(k)
                act_corner_x(a, across_j, src).wait_recv()
                act_corner_t(a, t, src).wait_recv()
                act_pass(a, across_j, src).start()

    def act_wait_of(a, jj):
        for k in range(nt):
            act_pass(a, jj, k).wait_recv()

    def act_wait(a):
        for xx in range(gx):
            act_wait_of(a, (1 - c) * gx + xx)

    def act_sent(a):
        if gx == 2:
            act_side(a, j).wait_send()
        for k in range(1, nt):
            act_turn(a, other_t(k), t).wait_send()
            if gx == 2:
                act_corner_x(a, j, other_t(k)).wait_send()
                act_corner_t(a, other_t(k), t).wait_send()
        for xx in range(gx):
            for k in range(nt):
                act_pass(a, c * gx + xx, k).wait_send()

    def w_block(i, zz):
        return weights(i).at[z_rows(zz)]

    def send_up(i, src):
        b = w_block(i, src)
        return copy(b, b, up_send.at[i, src], z_recv.at[i, src], along(z + 1))

    def send_down(i, src):
        b = w_block(i, src)
        return copy(b, b, down_send.at[i, src], z_recv.at[i, src], along(z - 1))

    def send_across(i, src, xx):
        b = weights(i).at[rows_at((xx * nz + src) * chip, chip)]
        return copy(b, b, x_send.at[i, src], x_recv.at[i, src], across)

    def send_own(i):
        local_copy(i).wait()
        for k in range(1, members):
            take_part(i, other_j(k)).wait_recv()
        pl.when(z < nz - 1)(lambda: send_up(i, z).start())
        pl.when(z > 0)(lambda: send_down(i, z).start())
        if gx == 1:
            send_across(i, z, x).start()

    def forward_up(i, d):
        @pl.when(z >= d)
        def _():
            send_up(i, z - d).wait_recv()
            pl.when(z < nz - 1)(lambda: send_up(i, z - d).start())
            if gx == 1:
                send_across(i, z - d, x).start()

    def forward_down(i, d):
        @pl.when(z + d <= nz - 1)
        def _():
            send_down(i, z + d).wait_recv()
            pl.when(z > 0)(lambda: send_down(i, z + d).start())
            if gx == 1:
                send_across(i, z + d, x).start()

    def gathered(i):
        if gx == 1:
            for src in range(nz):
                send_across(i, src, 1 - x).wait_recv()

    def own_of(i):
        return of(own_a, own_u, own_d, i)

    def g_across(i, to_z):
        b = pl.ds(to_z * chip, chip)
        return copy(
            of(xs_a, xs_u, xs_d, i).at[b],
            of(xr_a, xr_u, xr_d, i).at[b],
            gx_send.at[i, to_z],
            gx_recv.at[i, to_z],
            across,
        )

    def g_up(i, to_z):
        b = rows_at(to_z * zb, zb)
        return copy(
            of(zs_a, zs_u, zs_d, i).at[b],
            of(zu_a, zu_u, zu_d, i).at[b],
            gu_send.at[i, to_z],
            gu_recv.at[i, to_z],
            along(z + 1),
        )

    def g_down(i, to_z):
        b = rows_at(to_z * zb, zb)
        return copy(
            of(zs_a, zs_u, zs_d, i).at[b],
            of(zd_a, zd_u, zd_d, i).at[b],
            gd_send.at[i, to_z],
            gd_recv.at[i, to_z],
            along(z - 1),
        )

    def g_final(i, jj, src):
        at = (jj % 2 * 2 + jj // 2) * r if gx == 2 else jj * r
        return copy(
            of(fs_a, fs_u, fs_d, i).at[rows_at(at, r)],
            of(fr_a, fr_u, fr_d, i).at[src],
            fin_send.at[i, jj],
            fin_recv.at[i, src],
            member(jj),
        )

    def products(i, columns):
        if i in A:
            return [
                (0, 384, dot(normed[:, columns], grad_z[i], 0, 0)),
                (384, 512, dot(grads[:, columns], attended[i], 0, 0)),
            ]
        if i in U:
            return [(0, pw, dot(normed[:, columns], grad_u[i - na], 0, 0))]
        return [(0, pw, dot(grads[:, columns], active[i - na - nm], 0, 0))]

    cut = min(512, own)

    def weight_grad_cut(i, n):
        at = n * cut if gx == 2 else x * own + n * cut
        for lo, hi, part in products(i, rows_at(at, cut)):
            own_of(i)[n * cut : (n + 1) * cut, lo:hi] = part

    def weight_grad(i):
        if gx == 1:
            xs = of(xs_a, xs_u, xs_d, i)
            for n in range(own // cut):
                for lo, hi, part in products(i, rows_at((1 - x) * own + n * cut, cut)):
                    xs[n * cut : (n + 1) * cut, lo:hi] = part.astype(BF16)
            for to_z in range(nz):
                g_across(i, to_z).start()
        for n in range(own // cut):
            weight_grad_cut(i, n)

    def sum_x(i):
        if gx == 1:
            xr = of(xr_a, xr_u, xr_d, i)
            for to_z in range(nz):
                g_across(i, to_z).wait_recv()
                b = slice(to_z * chip, (to_z + 1) * chip)
                own_of(i)[b, :] += xr[b, :].astype(F32)

    def chain_step(i, to_z, last, came, buffer, send):
        b = rows_at(to_z * zb, zb)
        zs = of(zs_a, zs_u, zs_d, i)

        @pl.when(last)
        def _():
            zs[b, :] = own_of(i)[b, :].astype(BF16)

        @pl.when(jnp.logical_not(last))
        def _():
            came.wait_recv()
            zs[b, :] = (own_of(i)[b, :] + buffer[b, :].astype(F32)).astype(BF16)

        send.start()

    def chain_up(i, n):
        @pl.when(z <= n)
        def _():
            to_z = nz - 1 - n + z
            chain_step(i, to_z, z == 0, g_up(i, to_z), of(zu_a, zu_u, zu_d, i), g_up(i, to_z))

    def chain_down(i, n):
        @pl.when(nz - 1 - z <= n)
        def _():
            to_z = n - (nz - 1 - z)
            chain_step(i, to_z, z == nz - 1, g_down(i, to_z), of(zd_a, zd_u, zd_d, i), g_down(i, to_z))

    def own_index():
        return x * 2 + c if gx == 2 else c

    def chain_end(i):
        b = rows_at(z * zb, zb)

        @pl.when(z > 0)
        def _():
            g_up(i, z).wait_recv()
            own_of(i)[b, :] += of(zu_a, zu_u, zu_d, i)[b, :].astype(F32)

        @pl.when(z < nz - 1)
        def _():
            g_down(i, z).wait_recv()
            own_of(i)[b, :] += of(zd_a, zd_u, zd_d, i)[b, :].astype(F32)

        of(fs_a, fs_u, fs_d, i)[...] = own_of(i)[b, :].astype(BF16)
        for k in range(1, members):
            g_final(i, other_j(k), j).start()

    def finish(i):
        for k in range(1, members):
            g_final(i, j, other_j(k)).wait_recv()
        keep = own_of(i)[rows_at(z * zb + own_index() * r, r), :]
        came = of(fr_a, fr_u, fr_d, i)
        for jj in range(members):
            part = jnp.where(j == jj, keep, came[jj].astype(F32))
            if i in A:
                heads = [
                    part[:, p * 128 + h * HEAD : p * 128 + (h + 1) * HEAD] for h in range(hp) for p in range(3)
                ]
                at = (jj * na + i) * wide
                qkv_grad[:, 3 * at : 3 * (at + wide)] = jnp.concatenate(heads, axis=1)
                dense_grad[:, at : at + wide] = part[:, 384 : 384 + wide]
            else:
                out, k = (up_grad, i - na) if i in U else (down_grad, i - na - nm)
                out[:, jj * units + k * pw : jj * units + (k + 1) * pw] = part

    def pick(parts):
        total = parts[0]
        for jj in range(1, members):
            total = jnp.where(j == jj, parts[jj], total)
        return total

    def prepare():
        for k in range(na):
            for part in range(3):
                ba[k, :, part * 128 : (part + 1) * 128] = pick(
                    [head_part(b_qkv[...].reshape(1, -1), jj, k, part) for jj in range(members)]
                )
        steps = np.arange(ROT // 2, dtype=np.float32) * 2.0 / ROT
        inverse = (np.float32(ROTARY_BASE) ** -steps).astype(np.float32)
        lane = lax.broadcasted_iota(jnp.int32, (128, 128), 1) % HEAD
        scale = jnp.zeros((128, 128), F32)
        for n in range(ROT):
            scale = jnp.where(lane == n, inverse[n % (ROT // 2)], scale)

        def table(n, carry):
            rows = rows_at(n * 128, 128)
            place = (n * 128 + lax.broadcasted_iota(jnp.int32, (128, 128), 0)).astype(F32)
            cos, sin = jnp.cos(place * scale), jnp.sin(place * scale)
            cos_table[rows, :] = cos
            sin_table[rows, :] = jnp.where(lane < ROT // 2, -sin, sin)
            return carry

        lax.fori_loop(0, length // 128, table, 0)

    def prepare_docs():
        for k in range(1, members):
            doc_of(other_j(k)).wait_recv()
        for s in range(members):
            for n in range(length // 128):
                cut = slice(n * 128, (n + 1) * 128)
                rows = jnp.broadcast_to(docs[s, 0:1, cut], (128, 128))
                doc_column[s, cut, :] = jnp.transpose(rows).astype(BF16)

    RT = min(512, total_rows)
    tiles = total_rows // RT
    lanes = lax.broadcasted_iota(jnp.int32, (1, 128), 1)
    first = lanes < HEAD
    low = lanes % HEAD < ROT // 2
    turning = lanes % HEAD < ROT

    def rotated(rows, places, sign):
        near = jnp.where(low, pltpu.roll(rows, 128 - ROT // 2, 1), pltpu.roll(rows, ROT // 2, 1))
        return rows * cos_table[places, :] + jnp.where(turning, sign * near * sin_table[places, :], 0.0)

    def project(k, n):
        rows = rows_at(n * RT, RT)
        places = rows_at(lax.rem(n * RT, length), RT)
        packed = dot(normed[rows, :], wa[k, :, 0:384], 1, 0) + ba[k]
        query[rows, :] = (rotated(packed[:, 0:128], places, 1.0) * (HEAD**-0.5)).astype(BF16)
        key[rows, :] = rotated(packed[:, 128:256], places, 1.0).astype(BF16)
        value[rows, :] = packed[:, 256:384].astype(BF16)

    def project_back(k, n):
        rows = rows_at(n * RT, RT)
        grad_out[rows, :] = dot(grads[rows, :], wa[k, :, 384:512], 1, 0).astype(BF16)

    def each_tile(step, k):
        def body(n, carry):
            step(k, n)
            return carry

        lax.fori_loop(0, tiles, body, 0)

    block = min(128, length // 4)
    window = length // 4 + block

    def stacked(rows):
        if hp == 1:
            return rows
        zero = jnp.zeros_like(rows)
        return jnp.concatenate([jnp.where(first, rows, zero), jnp.where(first, zero, rows)], axis=0)

    def unstacked(rows):
        if hp == 1:
            return rows
        return jnp.where(first, rows[:window], rows[window:])

    def attend(k, s):
        key_sum[...] = jnp.zeros_like(key_sum)
        value_sum[...] = jnp.zeros_like(value_sum)

        def body(n, carry):
            q_at = pl.multiple_of(n * block, block)
            k_at = pl.multiple_of(jnp.maximum(q_at - length // 4, 0), block)
            q_rows = rows_at(s * length + q_at, block)
            k_rows = pl.ds(pl.multiple_of(s * length + k_at, block), window)
            q = query[q_rows, :]
            g = grad_out[q_rows, :]
            keys, values = stacked(key[k_rows, :]), stacked(value[k_rows, :])
            scores = dot(q, keys, 1, 1)
            grad_p = dot(g, values, 1, 1)
            at = k_at + lax.broadcasted_iota(jnp.int32, (block, window), 1)
            here = q_at + lax.broadcasted_iota(jnp.int32, (block, window), 0)
            own_doc_of = doc_column[s, pl.ds(q_at, block), 0:1].astype(F32)
            same = own_doc_of == docs[s, 0:1, pl.ds(k_at, window)]
            allowed = same & (at <= here)
            probs, grad_s = [], []
            for h in range(hp):
                cut = slice(h * window, (h + 1) * window)
                sc = jnp.where(allowed, scores[:, cut], -1e30)
                expos = jnp.exp(sc - jnp.max(sc, axis=-1, keepdims=True))
                p = expos / jnp.sum(expos, axis=-1, keepdims=True)
                gp = grad_p[:, cut]
                inner = jnp.sum(p * gp, axis=-1, keepdims=True)
                probs.append(p.astype(BF16))
                grad_s.append((p * (gp - inner)).astype(BF16))
            p = jnp.concatenate(probs, axis=1) if hp > 1 else probs[0]
            gs = jnp.concatenate(grad_s, axis=1) if hp > 1 else grad_s[0]
            attended[k, q_rows, :] = dot(p, values, 1, 0).astype(BF16)
            places = pl.ds(q_at, block)
            back = rotated(dot(gs, keys, 1, 0) * (HEAD**-0.5), places, -1.0)
            grad_z[k, q_rows, 0:128] = back.astype(BF16)
            here_rows = pl.ds(k_at, window)
            key_sum[here_rows, :] += unstacked(dot(gs, q, 0, 0))
            value_sum[here_rows, :] += unstacked(dot(p, g, 0, 0))
            return carry

        lax.fori_loop(0, length // block, body, 0)
        rows = rows_at(s * length, length)
        grad_z[k, rows, 128:256] = rotated(key_sum[...], slice(None), -1.0).astype(BF16)
        grad_z[k, rows, 256:384] = value_sum[...].astype(BF16)

    def hidden(k, n):
        rows = rows_at(n * RT, RT)
        u = dot(normed[rows, :], wu[k], 1, 0) + b_up[:, rows_at(j * units + k * pw, pw)]
        phi = 0.5 * (1.0 + lax.erf(u * np.float32(0.5**0.5)))
        active[k, rows, :] = (u * phi).astype(BF16)
        slope[k, rows, :] = phi + u * (jnp.exp(-0.5 * u * u) * np.float32((2 * np.pi) ** -0.5))

    def hidden_back(k, n):
        rows = rows_at(n * RT, RT)
        grad_u[k, rows, :] = (dot(grads[rows, :], wd[k], 1, 0) * slope[k, rows, :]).astype(BF16)

    HT = min(512, length)

    def branch(a, jj):
        def body(n, carry):
            rows = rows_at(jj * length + n * HT, HT)
            total = None
            for k in range(na):
                if a == 0:
                    part = dot(attended[k, rows, :], wa[k, :, 384:512], 1, 1)
                else:
                    part = dot(grad_z[k, rows, :], wa[k, :, 0:384], 1, 1)
                total = part if total is None else total + part
            for k in range(nm):
                if a == 0:
                    part = dot(active[k, rows, :], wd[k], 1, 1)
                else:
                    part = dot(grad_u[k, rows, :], wu[k], 1, 1)
                total = total + part
            partials[a][rows, :] = total.astype(BF16)
            return carry

        lax.fori_loop(0, length // HT, body, 0)

    def half_copy(a, jj):
        at = jj - (1 - c) * gx
        return copy(
            partials[a].at[rows_at(jj * length, length)],
            core_in.at[a % nbuf, rows_at(at * length, length)],
            half_send.at[a, at],
            half_recv.at[a, at],
            partner,
        )

    def branch_give(a, jj):
        branch(a, jj)
        half_copy(a, jj).start()

    def branches(a):
        for n, jj in enumerate((far_j, partner_j)[2 - gx :]):
            branch(a, jj)
            if n == 0 and nbuf == 1 and a == second:
                pl.semaphore_wait(credit.at[0], 1)
            half_copy(a, jj).start()
        for jj in (across_j, j)[2 - gx :]:
            branch(a, jj)

    def block_rows(jj, tt):
        return rows_at((jj * nt + tt) * R, R)

    def in_rows(jj, tt):
        return rows_at(((jj - c * gx) * nt + tt) * R, R)

    def both_cores(a, jj, tt, columns=slice(None)):
        return (
            partials[a][block_rows(jj, tt), columns].astype(F32)
            + core_in[a % nbuf, in_rows(jj, tt), columns].astype(F32)
        )

    def corner_t_copy(a, tt, src):
        b = partials[a].at[block_rows(across_j, tt), back_t]
        return copy(b, corner_t.at[a % nbuf, src], corner_t_send.at[2 + a, tt], corner_t_recv.at[2 + a, src], turned(tt))

    def corner_x_copy(a, jj, tt):
        b = partials[a].at[block_rows(jj, tt), back_x]
        return copy(b, corner_x.at[a % nbuf, tt], corner_x_send.at[2 + a, tt], corner_x_recv.at[2 + a, tt], across)

    def side_copy(a, jj):
        b = partials[a].at[block_rows(jj, t)]
        return copy(b, side_x.at[a % nbuf], side_send.at[2 + a], side_recv.at[2 + a], across)

    def turn_copy(a, tt, src):
        b = partials[a].at[block_rows(j, tt)]
        return copy(b, side_t.at[a % nbuf, src], turn_send.at[2 + a, tt], turn_recv.at[2 + a, src], turned(tt))

    def reduce_corner(a):
        if gx == 2:
            half_copy(a, far_j).wait_recv()
            for k in range(1, nt):
                tt = other_t(k)
                partials[a][block_rows(across_j, tt), :] = both_cores(a, across_j, tt).astype(BF16)
                corner_t_copy(a, tt, t).start()
                corner_x_copy(a, across_j, tt).start()

    def reduce_side(a):
        if gx == 2:
            total = both_cores(a, across_j, t, back_t)
            for k in range(1, nt):
                corner_t_copy(a, t, other_t(k)).wait_recv()
                total = total + corner_t[a % nbuf, other_t(k)].astype(F32)
            partials[a][block_rows(across_j, t), back_t] = total.astype(BF16)
            partials[a][block_rows(across_j, t), back_x] = both_cores(a, across_j, t, back_x).astype(BF16)
            side_copy(a, across_j).start()

    def reduce_turn(a):
        if nbuf == 1 and a == second and nt > 1:
            pl.semaphore_wait(credit.at[1], nt - 1)
        half_copy(a, partner_j).wait_recv()
        for k in range(1, nt):
            tt = other_t(k)
            if gx == 2:
                corner_x_copy(a, j, tt).wait_recv()
                total = both_cores(a, j, tt, back_x) + corner_x[a % nbuf, tt].astype(F32)
                partials[a][block_rows(j, tt), back_x] = total.astype(BF16)
                partials[a][block_rows(j, tt), back_t] = both_cores(a, j, tt, back_t).astype(BF16)
            else:
                partials[a][block_rows(j, tt), :] = both_cores(a, j, tt).astype(BF16)
            turn_copy(a, tt, t).start()

    def reduce_wait(a):
        if gx == 2:
            side_copy(a, across_j).wait_recv()
        for k in range(1, nt):
            turn_copy(a, t, other_t(k)).wait_recv()

    def reduced(a, n):
        mine = rows_at((j * nt + t) * R + n * tile, tile)
        came = rows_at(((j - c * gx) * nt + t) * R + n * tile, tile)
        rows = rows_at(n * tile, tile)
        total = partials[a][mine, :].astype(F32) + core_in[a % nbuf, came, :].astype(F32)
        if gx == 2:
            total = total + side_x[a % nbuf, rows, :].astype(F32)
        for k in range(1, nt):
            total = total + side_t[a % nbuf, other_t(k), rows, :].astype(F32)
        return restore(total)

    def reduce_sent(a):
        for xx in range(gx):
            half_copy(a, (1 - c) * gx + xx).wait_send()
        if gx == 2:
            side_copy(a, across_j).wait_send()
        for k in range(1, nt):
            tt = other_t(k)
            turn_copy(a, tt, t).wait_send()
            if gx == 2:
                corner_t_copy(a, tt, t).wait_send()
                corner_x_copy(a, across_j, tt).wait_send()

    def free_buffers():
        if nbuf == 1:
            pl.semaphore_signal(credit.at[0], inc=1, device_id=partner, device_id_type=MESH)
            for k in range(1, nt):
                pl.semaphore_signal(credit.at[1], inc=1, device_id=turned(other_t(k)), device_id_type=MESH)

    def write_output():
        def body(n, carry):
            rows = rows_at(n * tile, tile)
            total = tokens[rows, :].astype(F32) + reduced(0, n) + b_dense[...] + b_down[...]
            output[rows, :] = total.astype(BF16)
            return carry

        lax.fori_loop(0, R // tile, body, 0)

    def sum_biases():
        vec[...] = jnp.zeros_like(vec)
        for k in range(nm):
            vec[3:4, k * pw : (k + 1) * pw] = jnp.sum(grad_u[k].astype(F32), axis=0, keepdims=True)
        for k in range(na):
            at = units + k * 384
            vec[3:4, at : at + 384] = jnp.sum(grad_z[k].astype(F32), axis=0, keepdims=True)

    def write_input_grad():
        def body(n, carry):
            rows = rows_at(n * tile, tile)
            normal, inverse = normalize(tokens[rows, :].astype(F32))
            up = cotangent[rows, :].astype(F32)
            grad = reduced(1, n)
            vec[0:1, :] += jnp.sum(grad * normal, axis=0, keepdims=True)
            vec[1:2, :] += jnp.sum(grad, axis=0, keepdims=True)
            vec[2:3, :] += jnp.sum(up, axis=0, keepdims=True)
            scaled = grad * gain[...]
            input_grad[rows, :] = up + inverse * (
                scaled
                - jnp.mean(scaled, axis=-1, keepdims=True)
                - normal * jnp.mean(scaled * normal, axis=-1, keepdims=True)
            )
            return carry

        lax.fori_loop(0, R // tile, body, 0)

    peers = nz if gx == 2 else 2 * nz
    mates = members * nt
    peer = z if gx == 2 else z * 2 + x
    mate = j * nt + t

    def peer_copy(to, src):
        device_to = device(to, x, c, t) if gx == 2 else device(to // 2, to % 2, c, t)
        return copy(vec_z.at[peer], vec_z.at[src], peer_send.at[to], peer_recv.at[src], device_to)

    def mate_copy(to, src):
        jj, tt = to // nt, to % nt
        device_to = device(z, jj % 2, jj // 2, tt) if gx == 2 else device(z, x, jj, tt)
        return copy(vec_m.at[mate], vec_m.at[src], mate_send.at[to], mate_recv.at[src], device_to)

    def sums_start():
        vec_z[peer] = vec[...]
        for k in range(1, peers):
            peer_copy(lax.rem(peer + k, peers), peer).start()

    def sums_group():
        for k in range(1, peers):
            peer_copy(peer, lax.rem(peer + k, peers)).wait_recv()
        total = vec_z[0]
        for k in range(1, peers):
            total = total + vec_z[k]
        vec_m[mate] = total
        for k in range(1, mates):
            mate_copy(lax.rem(mate + k, mates), mate).start()

    def sums_end():
        for k in range(1, mates):
            mate_copy(mate, lax.rem(mate + k, mates)).wait_recv()
        total = vec_m[0]
        for k in range(1, mates):
            total = total + vec_m[k]
        gain_grad[...] = total[0:1]
        shift_grad[...] = total[1:2]
        dense_bias[...] = total[2:3]
        for jj in range(members):
            row = vec_m[jj * nt + t][3:4]
            up_bias[:, jj * units : (jj + 1) * units] = row[:, :units]
            for k in range(na):
                part = row[:, units + k * 384 : units + (k + 1) * 384]
                heads = [part[:, p * 128 + h * HEAD : p * 128 + (h + 1) * HEAD] for h in range(hp) for p in range(3)]
                at = (jj * na + k) * wide
                qkv_bias[:, 3 * at : 3 * (at + wide)] = jnp.concatenate(heads, axis=1)

    def sums_sent():
        for k in range(1, peers):
            peer_copy(lax.rem(peer + k, peers), peer).wait_send()
        for k in range(1, mates):
            mate_copy(lax.rem(mate + k, mates), mate).wait_send()

    def forwards(some, lo, hi):
        for d in range(lo, hi):
            for i in some:
                forward_up(i, d)
                forward_down(i, d)

    def chains(some, lo, hi):
        for n in range(lo, hi):
            for i in some:
                chain_up(i, n)
                chain_down(i, n)

    second = 0 if gx == 2 else 1

    def any_order():
        stage()
        fill_normed()
        enter()
        for i in U + A + Dn:
            share(i)
        give_docs()
        act_start(0)
        fill_grads()
        act_start(1)
        for i in U + A:
            send_own(i)
        prepare()
        prepare_docs()
        forwards(U + A, 1, 2)
        act_from_turn(0)
        act_from_side(0)
        for i in Dn:
            send_own(i)
        forwards(U, 2, nz)
        act_finish(0)
        act_wait(0)
        for i in U:
            gathered(i)
            each_tile(hidden, i - na)
        act_from_turn(1)
        act_from_side(1)
        forwards(A, 2, nz)
        forwards(Dn, 1, nz)
        act_finish(1)
        act_wait(1)
        for i in Dn:
            weight_grad(i)
            sum_x(i)
        chains(Dn, 0, nz - 1)
        for i in A:
            gathered(i)
            each_tile(project, i)
            each_tile(project_back, i)
            for s in range(members):
                attend(i, s)
            weight_grad(i)
            sum_x(i)
        chains(A, 0, nz - 1)
        for i in Dn:
            gathered(i)
            each_tile(hidden_back, i - na - nm)
        for i in U:
            weight_grad(i)
            sum_x(i)
        act_sent(0)
        act_sent(1)
        sum_biases()
        for a in (1, 0) if gx == 2 else (0, 1):
            branches(a)
            reduce_corner(a)
            if a != second:
                chains(U, 0, nz - 1)
            reduce_side(a)
            reduce_turn(a)
            if a != second:
                for i in Dn + A:
                    chain_end(i)
            reduce_wait(a)
            if a == 0:
                write_output()
            else:
                write_input_grad()
                sums_start()
            if a != second:
                free_buffers()
        for i in U:
            chain_end(i)
        sums_group()
        for i in Dn + A + U:
            finish(i)
        sums_end()

    def tuned_order():
        (a,), (u,), (d,) = A, U, Dn
        stage()
        fill_grads()
        fill_normed()
        enter()
        share(a)
        give_docs()
        share(u)
        act_start_turn(0)
        act_start_side(0)
        act_start_side(1)
        send_own(a)
        act_start_turn(1)
        share(d)
        prepare()
        send_own(u)
        forward_up(a, 1)
        forward_down(a, 1)
        act_from_turn(0)
        act_from_side(0)
        forward_up(u, 1)
        forward_down(u, 1)
        act_wait_of(0, partner_j)
        forward_up(a, 2)
        act_from_turn(1)
        forward_up(u, 2)
        forward_down(a, 2)
        act_from_side(1)
        forward_down(u, 2)
        prepare_docs()
        send_own(d)
        act_wait_of(1, partner_j)
        forward_up(a, 3)
        forward_down(a, 3)
        project(0, partner_j)
        project_back(0, partner_j)
        attend(0, partner_j)
        act_finish(0)
        project(0, across_j)
        project_back(0, j)
        project(0, j)
        forward_down(u, 3)
        forward_up(u, 3)
        hidden(0, across_j)
        hidden(0, j)
        act_wait_of(0, far_j)
        hidden(0, partner_j)
        act_finish(1)
        hidden(0, far_j)
        project(0, far_j)
        project_back(0, across_j)
        act_wait_of(1, far_j)
        weight_grad_cut(d, 1)
        forward_down(d, 1)
        chain_up(d, 0)
        forward_up(d, 1)
        weight_grad_cut(d, 0)
        chain_down(d, 0)
        attend(0, j)
        attend(0, across_j)
        forward_up(d, 2)
        forward_down(d, 2)
        project_back(0, far_j)
        chain_up(d, 1)
        chain_down(d, 1)
        attend(0, far_j)
        weight_grad_cut(a, 0)
        forward_up(d, 3)
        forward_down(d, 3)
        hidden_back(0, far_j)
        branch_give(1, far_j)
        chain_up(d, 2)
        chain_down(d, 2)
        hidden_back(0, across_j)
        branch(1, across_j)
        reduce_corner(1)
        weight_grad_cut(a, 1)
        chain_down(a, 0)
        chain_up(a, 0)
        act_sent(0)
        act_sent(1)
        branch_give(0, far_j)
        branch(0, across_j)
        hidden_back(0, j)
        hidden_back(0, partner_j)
        reduce_corner(0)
        weight_grad_cut(u, 0)
        chain_down(u, 0)
        weight_grad_cut(u, 1)
        chain_up(u, 0)
        chain_end(d)
        chain_up(a, 1)
        branch_give(1, partner_j)
        reduce_side(1)
        branch(0, j)
        branch(1, j)
        chain_up(u, 1)
        chain_down(a, 1)
        reduce_turn(1)
        branch_give(0, partner_j)
        chain_down(u, 1)
        sum_biases()
        chain_up(a, 2)
        reduce_turn(0)
        chain_down(a, 2)
        reduce_side(0)
        reduce_wait(1)
        write_input_grad()
        sums_start()
        chain_down(u, 2)
        chain_up(u, 2)
        chain_end(a)
        sums_group()
        finish(d)
        finish(a)
        chain_end(u)
        reduce_wait(0)
        write_output()
        sums_end()
        finish(u)

    if (gx, na, nm, nz, tiles, RT) == (2, 1, 1, 4, 4, length):
        tuned_order()
    else:
        any_order()

    for i in range(count):
        for k in range(1, members):
            g_final(i, other_j(k), j).wait_send()
            give_part(i, other_j(k)).wait_send()
        for src in range(nz):
            pl.when((z < nz - 1) & (src <= z))(lambda: send_up(i, src).wait_send())
            pl.when((z > 0) & (src >= z))(lambda: send_down(i, src).wait_send())
            pl.when(src > z)(lambda: g_up(i, src).wait_send())
            pl.when(src < z)(lambda: g_down(i, src).wait_send())
            if gx == 1:
                send_across(i, src, x).wait_send()
                g_across(i, src).wait_send()
    for k in range(1, members):
        own_doc(other_j(k)).wait_send()
    reduce_sent(0)
    reduce_sent(1)
    sums_sent()


def hand_out(arrays):
    wide = [n for n, array in enumerate(arrays) if array.shape[0] > 1]
    thin = [n for n, array in enumerate(arrays) if array.shape[0] == 1]

    def body(*refs):
        count = len(arrays)
        given, taken, buffers, sems = refs[:count], refs[count : 2 * count], refs[2 * count : -1], refs[-1]
        reads = [pltpu.make_async_copy(given[n], buffers[i], sems.at[0, i]) for i, n in enumerate(wide)]
        writes = [pltpu.make_async_copy(buffers[i], taken[n], sems.at[1, i]) for i, n in enumerate(wide)]
        for read in reads:
            read.start()
        for n in thin:
            taken[n][...] = given[n][0]
        for read, write in zip(reads, writes):
            read.wait()
            write.start()
        for write in writes:
            write.wait()

    def specs():
        return [pl.BlockSpec(memory_space=pltpu.VMEM if n in thin else pl.ANY) for n in range(len(arrays))]

    return list(
        pl.pallas_call(
            body,
            out_shape=[
                jax.ShapeDtypeStruct(array.shape[1:] if n in thin else array.shape, array.dtype)
                for n, array in enumerate(arrays)
            ],
            in_specs=specs(),
            out_specs=specs(),
            scratch_shapes=[pltpu.VMEM(arrays[n].shape, arrays[n].dtype) for n in wide]
            + [pltpu.SemaphoreType.DMA((2, len(wide)))],
            name="hand_out",
        )(*arrays)
    )


def on_device(
    nt,
    n_dp,
    tokens,
    cotangent,
    segments,
    ln_gain,
    ln_bias,
    w_qkv,
    b_qkv,
    w_dense,
    b_dense,
    w_up,
    b_up,
    w_down,
    b_down,
):
    R, D = tokens.shape
    length = segments.shape[1]
    r = w_qkv.shape[0]
    nz = n_dp // 4
    heads = w_qkv.shape[1] // (3 * HEAD)
    gx = 2 if heads % 4 == 0 and 4 * length * D <= 1 << 21 else 1
    members = 2 * gx
    heads = heads // members
    hp = 2 if heads % 2 == 0 else 1
    na = heads // hp
    units = w_up.shape[1] // members
    pw = 512 if units % 512 == 0 else units
    nm = units // pw
    nbuf = gx
    peers, mates = (nz if gx == 2 else 2 * nz), members * nt
    sizes = dict(nt=nt, nz=nz, gx=gx, na=na, nm=nm, hp=hp, length=length, R=R, r=r, pw=pw, nbuf=nbuf)

    widths = ((na, 512), (nm, pw), (nm, pw))
    count = na + 2 * nm
    rows = members * length
    own = D if gx == 2 else D // 2
    chip = 2 * r
    split = D // 4
    V = pltpu.VMEM
    DMA = pltpu.SemaphoreType.DMA

    def some(shape):
        return V(shape if gx == 2 else (1, 1, 8, 128)[-len(shape) :], BF16)

    scratch = (
        [V((members, na, r, 512), BF16), V((na, 1, 384), F32)]
        + [V((length, 128), F32)] * 2
        + [V((members, 8, length), F32), V((members, length, 128), BF16)]
        + [V((n, D, w), BF16) for n, w in widths]
        + [V((rows, D), BF16), V((rows, D), BF16)]
        + [V((rows, 128), BF16)] * 4
        + [V((na, rows, 128), BF16), V((na, rows, 384), BF16)]
        + [V((length, 128), F32)] * 2
        + [V((nm, rows, pw), BF16), V((nm, rows, pw), F32), V((nm, rows, pw), BF16)]
        + [V((rows, D) if gx == 2 else (8, 128), BF16)]
        + [V((nbuf, gx * length, D), BF16), some((nbuf, nt, R, split)), some((nbuf, nt, R, D - split))]
        + [some((nbuf, R, D)), V((nbuf, nt, R, D), BF16)]
        + [V((n, own, w), F32) for n, w in widths]
        + [V((n, own, w) if gx == 1 else (n, 8, 128), BF16) for _ in range(2) for n, w in widths]
        + [V((n, own, w), BF16) for _ in range(3) for n, w in widths]
        + [V((n, gx * chip, w), BF16) for n, w in widths]
        + [V((n, members, r, w), BF16) for n, w in widths]
        + [V((8, D), F32), V((peers, 8, D), F32), V((mates, 8, D), F32)]
        + [DMA((count,)), DMA((count + 1, members)), DMA((count + 1, members))]
        + [DMA((count, nz))] * 5
        + [DMA((4, nt))] * 2
        + [DMA((4,))] * 2
        + [DMA((4, nt))] * 4
        + [DMA((2, members, nt))] * 2
        + [DMA((count, nz))] * 6
        + [DMA((count, members))] * 2
        + [DMA((2, gx))] * 2
        + [DMA((peers,))] * 2
        + [DMA((mates,))] * 2
        + [pltpu.SemaphoreType.REGULAR((2,))]
    )
    space = pl.BlockSpec(memory_space=pltpu.VMEM)

    def row(vector):
        return vector.reshape(1, -1)

    args = (
        tokens,
        cotangent,
        segments,
        row(ln_gain),
        row(ln_bias),
        w_qkv,
        b_qkv,
        w_dense.T,
        row(b_dense),
        w_up,
        row(b_up),
        w_down.T,
        row(b_down),
    )
    shapes = (
        jax.ShapeDtypeStruct((R, D), BF16),
        jax.ShapeDtypeStruct((R, D), F32),
        jax.ShapeDtypeStruct((1, D), F32),
        jax.ShapeDtypeStruct((1, D), F32),
        jax.ShapeDtypeStruct(w_qkv.shape, F32),
        jax.ShapeDtypeStruct((1, w_qkv.shape[1]), F32),
        jax.ShapeDtypeStruct(w_dense.shape[::-1], F32),
        jax.ShapeDtypeStruct((1, D), F32),
        jax.ShapeDtypeStruct(w_up.shape, F32),
        jax.ShapeDtypeStruct((1, w_up.shape[1]), F32),
        jax.ShapeDtypeStruct(w_down.shape[::-1], F32),
    )
    out = pl.pallas_call(
        functools.partial(kernel, sizes),
        out_shape=shapes,
        in_specs=[space] * len(args),
        out_specs=[space] * len(shapes),
        scratch_shapes=scratch,
        compiler_params=pltpu.CompilerParams(
            collective_id=0, has_side_effects=True, vmem_limit_bytes=67043328
        ),
        name="layer",
    )(*args)
    out = hand_out((*out, out[7]))
    out[6], out[10] = out[6].T, out[10].T
    return tuple(out)


def solution(mesh):
    return jax.shard_map(
        functools.partial(on_device, mesh.shape["tensor"], mesh.shape["dp"]),
        mesh=mesh,
        in_specs=(
            P(("dp", "tensor"), None),
            P(("dp", "tensor"), None),
            P("dp", None),
            P(),
            P(),
            P("dp", "tensor"),
            P("tensor"),
            P("tensor", "dp"),
            P(),
            P("dp", "tensor"),
            P("tensor"),
            P("tensor", "dp"),
            P(),
        ),
        out_specs=(
            P(("dp", "tensor"), None),
            P(("dp", "tensor"), None),
            P(),
            P(),
            P("dp", "tensor"),
            P("tensor"),
            P("tensor", "dp"),
            P(),
            P("dp", "tensor"),
            P("tensor"),
            P("tensor", "dp"),
            P(),
        ),
        check_vma=False,
    )
```

```python
import functools

import jax
import jax.numpy as jnp
import numpy as np
from jax import lax
from jax.experimental import pallas as pl
from jax.experimental.pallas import tpu as pltpu
from jax.sharding import PartitionSpec as P

HEAD = 64
ROT = 16
NORM_EPS = 1e-05
ROTARY_BASE = 10000.0
MESH = pl.DeviceIdType.MESH
F32 = jnp.float32
BF16 = jnp.bfloat16


def dot(left, right, over_left, over_right):
    return lax.dot_general(
        left, right, (((over_left,), (over_right,)), ((), ())), preferred_element_type=F32
    )


def normalize(rows):
    centred = rows - jnp.mean(rows, axis=-1, keepdims=True)
    inverse = lax.rsqrt(jnp.mean(centred * centred, axis=-1, keepdims=True) + NORM_EPS)
    return centred * inverse, inverse


def padded(array):
    rest = -array.shape[1] % 128
    return jnp.concatenate([array, jnp.zeros((array.shape[0], rest), array.dtype)], axis=1) if rest else array


def kernel(
    sizes,
    tokens_hbm,
    cotangent_hbm,
    segments,
    gain,
    shift,
    w_qkv_hbm,
    b_qkv,
    w_dense_hbm,
    b_dense,
    w_up,
    b_up,
    w_down,
    b_down,
    output_hbm,
    input_grad_hbm,
    gain_grad,
    shift_grad,
    qkv_grad_hbm,
    qkv_bias,
    dense_grad_hbm,
    dense_bias,
    up_grad_hbm,
    up_bias,
    down_grad_hbm,
    tokens,
    cotangent,
    w_qkv,
    w_dense,
    output,
    input_grad,
    qkv_grad,
    dense_grad,
    up_grad,
    down_grad,
    wa_in,
    ba,
    cos_table,
    sin_table,
    docs,
    doc_column,
    wa,
    wu,
    wd,
    normed,
    grads,
    query,
    key,
    value,
    grad_out,
    attended,
    grad_z,
    key_sum,
    value_sum,
    active,
    slope,
    grad_u,
    late,
    core_in,
    corner_x,
    corner_t,
    side_x,
    side_t,
    own_a,
    own_u,
    own_d,
    xs_a,
    xs_u,
    xs_d,
    xr_a,
    xr_u,
    xr_d,
    zs_a,
    zs_u,
    zs_d,
    zu_a,
    zu_u,
    zu_d,
    zd_a,
    zd_u,
    zd_d,
    fs_a,
    fs_u,
    fs_d,
    fr_a,
    fr_u,
    fr_d,
    vec,
    vec_z,
    vec_m,
    local_sem,
    io_sem,
    share_send,
    share_recv,
    up_send,
    down_send,
    z_recv,
    x_send,
    x_recv,
    turn_send,
    turn_recv,
    side_send,
    side_recv,
    corner_x_send,
    corner_x_recv,
    corner_t_send,
    corner_t_recv,
    pass_send,
    pass_recv,
    gx_send,
    gx_recv,
    gu_send,
    gu_recv,
    gd_send,
    gd_recv,
    fin_send,
    fin_recv,
    half_send,
    half_recv,
    peer_send,
    peer_recv,
    mate_send,
    mate_recv,
    credit,
):
    nt, nz, gx, na, nm, hp, length, R, r, pw, nbuf = (
        sizes[k] for k in ("nt", "nz", "gx", "na", "nm", "hp", "length", "R", "r", "pw", "nbuf")
    )
    D = tokens.shape[1]
    chip = 2 * r
    zb = gx * chip
    own = D if gx == 2 else D // 2
    members = 2 * gx
    wide = hp * HEAD
    units = nm * pw
    total_rows = members * length
    partials = (grads, late if gx == 2 else normed)
    dp, t = lax.axis_index("dp"), lax.axis_index("tensor")
    z, x, c = dp // 4, (dp // 2) % 2, dp % 2
    j = c * gx + x if gx == 2 else c

    def device(zz, xx, cc, tt):
        return (zz * 4 + xx * 2 + cc, tt)

    partner = device(z, x, 1 - c, t)
    across = device(z, 1 - x, c, t)

    def member(jj):
        return device(z, jj % 2, jj // 2, t) if gx == 2 else device(z, x, jj, t)

    def along(zz):
        return device(zz, x, c, t)

    def turned(tt):
        return device(z, x, c, tt)

    def other_j(k):
        return lax.rem(j + k, members)

    def other_z(k):
        return lax.rem(z + k, nz)

    def other_t(k):
        return lax.rem(t + k, nt)

    def rows_at(start, size):
        return pl.ds(pl.multiple_of(start, size), size)

    def copy(src, dst, send, recv, to):
        return pltpu.make_async_remote_copy(
            src_ref=src, dst_ref=dst, send_sem=send, recv_sem=recv, device_id=to, device_id_type=MESH
        )

    A = list(range(na))
    U = list(range(na, na + nm))
    Dn = list(range(na + nm, na + 2 * nm))
    count = na + 2 * nm

    def of(a, u, d, i):
        if i in A:
            return a.at[i]
        return u.at[i - na] if i in U else d.at[i - na - nm]

    def weights(i):
        return of(wa, wu, wd, i)

    def z_rows(zz):
        return rows_at(zz * zb if gx == 2 else (x * nz + zz) * chip, zb)

    own_rows = rows_at(z * zb + (x * 2 + c) * r if gx == 2 else (x * nz + z) * chip + c * r, r)

    barrier = pltpu.get_barrier_semaphore()
    greeted = [member(other_j(k)) for k in range(1, members)] + ([] if gx == 2 else [across])
    greeted += [
        device(z, jj % 2 if gx == 2 else x, jj // 2 if gx == 2 else jj, other_t(k))
        for k in range(1, nt)
        for jj in [other_j(n) for n in range(members)]
    ]

    def greet(other):
        pl.semaphore_signal(barrier, inc=1, device_id=other, device_id_type=MESH)

    for other in greeted:
        greet(other)
    pl.when(z > 0)(lambda: greet(along(z - 1)))
    pl.when(z < nz - 1)(lambda: greet(along(z + 1)))

    reads = [
        pltpu.make_async_copy(src, dst, io_sem.at[n])
        for n, (src, dst) in enumerate(
            ((w_qkv_hbm, w_qkv), (w_dense_hbm, w_dense), (tokens_hbm, tokens), (cotangent_hbm, cotangent))
        )
    ]
    for read in reads:
        read.start()

    def enter():
        pl.semaphore_wait(barrier, len(greeted) + jnp.minimum(z, 1) + jnp.minimum(nz - 1 - z, 1))

    results = (
        (output, output_hbm),
        (input_grad, input_grad_hbm),
        (qkv_grad, qkv_grad_hbm),
        (dense_grad, dense_grad_hbm),
        (up_grad, up_grad_hbm),
        (down_grad, down_grad_hbm),
    )

    def result(n):
        return pltpu.make_async_copy(*results[n], io_sem.at[4 + n])

    def part_of(i, jj):
        if i in A:
            return wa_in.at[jj, i]
        ref, k = (w_up, i - na) if i in U else (w_down, i - na - nm)
        return ref.at[:, rows_at(jj * units + k * pw, pw)]

    def local_copy(i):
        return pltpu.make_async_copy(part_of(i, j), weights(i).at[own_rows], local_sem.at[i])

    def give_part(i, jj):
        dst = weights(i).at[own_rows]
        return copy(part_of(i, jj), dst, share_send.at[i, jj], share_recv.at[i, j], member(jj))

    def member_rows(jj):
        return rows_at(z * zb + (jj % 2 * 2 + jj // 2) * r if gx == 2 else (x * nz + z) * chip + jj * r, r)

    def take_part(i, jj):
        dst = weights(i).at[member_rows(jj)]
        return copy(part_of(i, j), dst, share_send.at[i, jj], share_recv.at[i, jj], member(jj))

    def share(i):
        local_copy(i).start()
        for k in range(1, members):
            give_part(i, other_j(k)).start()

    def head_part(array, jj, k, part):
        at = [((jj * na + k) * hp + h) * 3 * HEAD + part * HEAD for h in range(hp)]
        return padded(jnp.concatenate([array[:, a : a + HEAD] for a in at], axis=1))

    def own_doc(jj):
        return copy(docs.at[j], docs.at[j], share_send.at[count, jj], share_recv.at[count, j], member(jj))

    def doc_of(jj):
        return copy(docs.at[jj], docs.at[jj], share_send.at[count, jj], share_recv.at[count, jj], member(jj))

    def stage():
        reads[0].wait()
        reads[1].wait()
        for jj in range(members):
            for k in range(na):
                for part in range(3):
                    wa_in[jj, k, :, part * 128 : (part + 1) * 128] = head_part(w_qkv[...], jj, k, part)
                at = (jj * na + k) * wide
                wa_in[jj, k, :, 384:512] = padded(w_dense[:, at : at + wide])
        docs[j] = jnp.broadcast_to(segments[...].astype(F32), docs.shape[1:])

    def give_docs():
        for k in range(1, members):
            own_doc(other_j(k)).start()

    def permute(rows):
        if gx == 2:
            return rows
        return jnp.concatenate(
            [rows[:, (zz * 2 + xx) * chip : (zz * 2 + xx + 1) * chip] for xx in range(2) for zz in range(nz)],
            axis=1,
        )

    def restore(rows):
        if gx == 2:
            return rows
        return jnp.concatenate(
            [rows[:, (xx * nz + zz) * chip : (xx * nz + zz + 1) * chip] for zz in range(nz) for xx in range(2)],
            axis=1,
        )

    acts = (normed, grads)
    tile = min(64, R)
    split = D * 3 // 8
    over_x, over_t = slice(0, split), slice(split, D)
    back_split = D // 4
    back_x, back_t = slice(0, back_split), slice(back_split, D)

    def act_rows(jj, tt):
        return rows_at((jj * nt + tt) * R, R)

    across_j = c * gx + 1 - x if gx == 2 else c
    partner_j = (1 - c) * gx + x if gx == 2 else 1 - c
    far_j = (1 - c) * gx + 1 - x if gx == 2 else 1 - c
    near = (j, partner_j, across_j, far_j)

    def fill_normed():
        reads[2].wait()

        def body(n, carry):
            rows = rows_at(n * tile, tile)
            normal, _ = normalize(tokens[rows, :].astype(F32))
            normed[rows_at((j * nt + t) * R + n * tile, tile), :] = permute(
                (normal * gain[...] + shift[...]).astype(BF16)
            )
            return carry

        lax.fori_loop(0, R // tile, body, 0)

    def fill_grads():
        reads[3].wait()

        def body(n, carry):
            grads[rows_at((j * nt + t) * R + n * tile, tile), :] = permute(cotangent[rows_at(n * tile, tile), :])
            return carry

        lax.fori_loop(0, R // tile, body, 0)

    def act_turn(a, tt, src):
        b = acts[a].at[act_rows(j, src)]
        return copy(b, b, turn_send.at[a, tt], turn_recv.at[a, src], turned(tt))

    def act_side(a, jj):
        b = acts[a].at[act_rows(jj, t)]
        return copy(b, b, side_send.at[a], side_recv.at[a], across)

    def act_corner_x(a, jj, tt):
        b = acts[a].at[act_rows(jj, tt), over_x]
        return copy(b, b, corner_x_send.at[a, tt], corner_x_recv.at[a, tt], across)

    def act_corner_t(a, tt, src):
        b = acts[a].at[act_rows(across_j, src), over_t]
        return copy(b, b, corner_t_send.at[a, tt], corner_t_recv.at[a, src], turned(tt))

    def act_pass(a, jj, tt):
        b = acts[a].at[act_rows(jj, tt)]
        return copy(b, b, pass_send.at[a, jj, tt], pass_recv.at[a, jj, tt], partner)

    def act_start_side(a):
        if gx == 2:
            act_side(a, j).start()

    def act_start_turn(a):
        for k in range(1, nt):
            act_turn(a, other_t(k), t).start()
        act_pass(a, j, t).start()

    def act_start(a):
        act_start_side(a)
        act_start_turn(a)

    def act_from_turn(a):
        for k in range(1, nt):
            src = other_t(k)
            act_turn(a, t, src).wait_recv()
            if gx == 2:
                act_corner_x(a, j, src).start()
            act_pass(a, j, src).start()

    def act_from_side(a):
        if gx == 2:
            act_side(a, across_j).wait_recv()
            for k in range(1, nt):
                act_corner_t(a, other_t(k), t).start()
            act_pass(a, across_j, t).start()

    def act_finish(a):
        if gx == 2:
            for k in range(1, nt):
                src = other_t(k)
                act_corner_x(a, across_j, src).wait_recv()
                act_corner_t(a, t, src).wait_recv()
                act_pass(a, across_j, src).start()

    def act_wait_of(a, jj):
        for k in range(nt):
            act_pass(a, jj, k).wait_recv()

    def act_wait(a):
        for xx in range(gx):
            act_wait_of(a, (1 - c) * gx + xx)

    def act_sent(a):
        if gx == 2:
            act_side(a, j).wait_send()
        for k in range(1, nt):
            act_turn(a, other_t(k), t).wait_send()
            if gx == 2:
                act_corner_x(a, j, other_t(k)).wait_send()
                act_corner_t(a, other_t(k), t).wait_send()
        for xx in range(gx):
            for k in range(nt):
                act_pass(a, c * gx + xx, k).wait_send()

    def w_block(i, zz):
        return weights(i).at[z_rows(zz)]

    def send_up(i, src):
        b = w_block(i, src)
        return copy(b, b, up_send.at[i, src], z_recv.at[i, src], along(z + 1))

    def send_down(i, src):
        b = w_block(i, src)
        return copy(b, b, down_send.at[i, src], z_recv.at[i, src], along(z - 1))

    def send_across(i, src, xx):
        b = weights(i).at[rows_at((xx * nz + src) * chip, chip)]
        return copy(b, b, x_send.at[i, src], x_recv.at[i, src], across)

    def send_first(i):
        def along_z(sems, to):
            return copy(part_of(i, j), weights(i).at[own_rows], sems.at[i, z], z_recv.at[i, z], to)

        pl.when(z < nz - 1)(lambda: along_z(up_send, along(z + 1)).start())
        pl.when(z > 0)(lambda: along_z(down_send, along(z - 1)).start())

    def send_own(i):
        local_copy(i).wait()
        for k in range(1, members):
            jj = other_j(k)
            take_part(i, jj).wait_recv()
            rows = weights(i).at[member_rows(jj)]

            def along_z(sems, to):
                return copy(rows, rows, sems.at[i, z], z_recv.at[i, z], to)

            pl.when(z < nz - 1)(lambda: along_z(up_send, along(z + 1)).start())
            pl.when(z > 0)(lambda: along_z(down_send, along(z - 1)).start())
        if gx == 1:
            send_across(i, z, x).start()

    def forward_up(i, d):
        @pl.when(z >= d)
        def _():
            send_up(i, z - d).wait_recv()
            pl.when(z < nz - 1)(lambda: send_up(i, z - d).start())
            if gx == 1:
                send_across(i, z - d, x).start()

    def forward_down(i, d):
        @pl.when(z + d <= nz - 1)
        def _():
            send_down(i, z + d).wait_recv()
            pl.when(z > 0)(lambda: send_down(i, z + d).start())
            if gx == 1:
                send_across(i, z + d, x).start()

    def gathered(i):
        if gx == 1:
            for src in range(nz):
                send_across(i, src, 1 - x).wait_recv()

    def own_of(i):
        return of(own_a, own_u, own_d, i)

    def g_across(i, to_z):
        b = pl.ds(to_z * chip, chip)
        return copy(
            of(xs_a, xs_u, xs_d, i).at[b],
            of(xr_a, xr_u, xr_d, i).at[b],
            gx_send.at[i, to_z],
            gx_recv.at[i, to_z],
            across,
        )

    def g_up(i, to_z):
        b = rows_at(to_z * zb, zb)
        return copy(
            of(zs_a, zs_u, zs_d, i).at[b],
            of(zu_a, zu_u, zu_d, i).at[b],
            gu_send.at[i, to_z],
            gu_recv.at[i, to_z],
            along(z + 1),
        )

    def g_down(i, to_z):
        b = rows_at(to_z * zb, zb)
        return copy(
            of(zs_a, zs_u, zs_d, i).at[b],
            of(zd_a, zd_u, zd_d, i).at[b],
            gd_send.at[i, to_z],
            gd_recv.at[i, to_z],
            along(z - 1),
        )

    def g_final(i, jj, src):
        at = (jj % 2 * 2 + jj // 2) * r if gx == 2 else jj * r
        return copy(
            of(fs_a, fs_u, fs_d, i).at[rows_at(at, r)],
            of(fr_a, fr_u, fr_d, i).at[src],
            fin_send.at[i, jj],
            fin_recv.at[i, src],
            member(jj),
        )

    def products(i, columns):
        if i in A:
            return [
                (0, 384, dot(normed[:, columns], grad_z[i], 0, 0)),
                (384, 512, dot(grads[:, columns], attended[i], 0, 0)),
            ]
        if i in U:
            return [(0, pw, dot(normed[:, columns], grad_u[i - na], 0, 0))]
        return [(0, pw, dot(grads[:, columns], active[i - na - nm], 0, 0))]

    cut = min(512, own)

    def weight_grad_cut(i, n):
        at = n * cut if gx == 2 else x * own + n * cut
        for lo, hi, part in products(i, rows_at(at, cut)):
            own_of(i)[n * cut : (n + 1) * cut, lo:hi] = part

    def weight_grad(i):
        if gx == 1:
            xs = of(xs_a, xs_u, xs_d, i)
            for n in range(own // cut):
                for lo, hi, part in products(i, rows_at((1 - x) * own + n * cut, cut)):
                    xs[n * cut : (n + 1) * cut, lo:hi] = part.astype(BF16)
            for to_z in range(nz):
                g_across(i, to_z).start()
        for n in range(own // cut):
            weight_grad_cut(i, n)

    def sum_x(i):
        if gx == 1:
            xr = of(xr_a, xr_u, xr_d, i)
            for to_z in range(nz):
                g_across(i, to_z).wait_recv()
                b = slice(to_z * chip, (to_z + 1) * chip)
                own_of(i)[b, :] += xr[b, :].astype(F32)

    def chain_step(i, to_z, last, came, buffer, send):
        b = rows_at(to_z * zb, zb)
        zs = of(zs_a, zs_u, zs_d, i)

        @pl.when(last)
        def _():
            zs[b, :] = own_of(i)[b, :].astype(BF16)

        @pl.when(jnp.logical_not(last))
        def _():
            came.wait_recv()
            zs[b, :] = (own_of(i)[b, :] + buffer[b, :].astype(F32)).astype(BF16)

        send.start()

    def chain_up(i, n):
        @pl.when(z <= n)
        def _():
            to_z = nz - 1 - n + z
            chain_step(i, to_z, z == 0, g_up(i, to_z), of(zu_a, zu_u, zu_d, i), g_up(i, to_z))

    def chain_down(i, n):
        @pl.when(nz - 1 - z <= n)
        def _():
            to_z = n - (nz - 1 - z)
            chain_step(i, to_z, z == nz - 1, g_down(i, to_z), of(zd_a, zd_u, zd_d, i), g_down(i, to_z))

    def own_index():
        return x * 2 + c if gx == 2 else c

    def chain_end(i):
        b = rows_at(z * zb, zb)

        @pl.when(z > 0)
        def _():
            g_up(i, z).wait_recv()
            own_of(i)[b, :] += of(zu_a, zu_u, zu_d, i)[b, :].astype(F32)

        @pl.when(z < nz - 1)
        def _():
            g_down(i, z).wait_recv()
            own_of(i)[b, :] += of(zd_a, zd_u, zd_d, i)[b, :].astype(F32)

        of(fs_a, fs_u, fs_d, i)[...] = own_of(i)[b, :].astype(BF16)
        for k in range(1, members):
            g_final(i, other_j(k), j).start()

    def finish(i):
        for k in range(1, members):
            g_final(i, j, other_j(k)).wait_recv()
        keep = own_of(i)[rows_at(z * zb + own_index() * r, r), :]
        came = of(fr_a, fr_u, fr_d, i)
        for jj in range(members):
            part = jnp.where(j == jj, keep, came[jj].astype(F32))
            if i in A:
                heads = [
                    part[:, p * 128 + h * HEAD : p * 128 + (h + 1) * HEAD] for h in range(hp) for p in range(3)
                ]
                at = (jj * na + i) * wide
                qkv_grad[:, 3 * at : 3 * (at + wide)] = jnp.concatenate(heads, axis=1)
                dense_grad[:, at : at + wide] = part[:, 384 : 384 + wide]
            else:
                out, k = (up_grad, i - na) if i in U else (down_grad, i - na - nm)
                out[:, jj * units + k * pw : jj * units + (k + 1) * pw] = part
        if i == A[-1]:
            result(2).start()
            result(3).start()
        if i in (U[-1], Dn[-1]):
            result(4 if i in U else 5).start()

    def pick(parts):
        total = parts[0]
        for jj in range(1, members):
            total = jnp.where(j == jj, parts[jj], total)
        return total

    def prepare():
        for k in range(na):
            for part in range(3):
                ba[k, :, part * 128 : (part + 1) * 128] = pick(
                    [head_part(b_qkv[...].reshape(1, -1), jj, k, part) for jj in range(members)]
                )
        steps = np.arange(ROT // 2, dtype=np.float32) * 2.0 / ROT
        inverse = (np.float32(ROTARY_BASE) ** -steps).astype(np.float32)
        lane = lax.broadcasted_iota(jnp.int32, (128, 128), 1) % HEAD
        scale = jnp.zeros((128, 128), F32)
        for n in range(ROT):
            scale = jnp.where(lane == n, inverse[n % (ROT // 2)], scale)

        def table(n, carry):
            rows = rows_at(n * 128, 128)
            place = (n * 128 + lax.broadcasted_iota(jnp.int32, (128, 128), 0)).astype(F32)
            cos, sin = jnp.cos(place * scale), jnp.sin(place * scale)
            cos_table[rows, :] = cos
            sin_table[rows, :] = jnp.where(lane < ROT // 2, -sin, sin)
            return carry

        lax.fori_loop(0, length // 128, table, 0)

    def prepare_docs():
        for k in range(1, members):
            doc_of(other_j(k)).wait_recv()
        for s in range(members):
            for n in range(length // 128):
                cut = slice(n * 128, (n + 1) * 128)
                rows = jnp.broadcast_to(docs[s, 0:1, cut], (128, 128))
                doc_column[s, cut, :] = jnp.transpose(rows).astype(BF16)

    RT = min(512, total_rows)
    tiles = total_rows // RT
    lanes = lax.broadcasted_iota(jnp.int32, (1, 128), 1)
    first = lanes < HEAD
    low = lanes % HEAD < ROT // 2
    turning = lanes % HEAD < ROT

    def rotated(rows, places, sign):
        near = jnp.where(low, pltpu.roll(rows, 128 - ROT // 2, 1), pltpu.roll(rows, ROT // 2, 1))
        return rows * cos_table[places, :] + jnp.where(turning, sign * near * sin_table[places, :], 0.0)

    def project(k, n):
        rows = rows_at(n * RT, RT)
        places = rows_at(lax.rem(n * RT, length), RT)
        packed = dot(normed[rows, :], wa[k, :, 0:384], 1, 0) + ba[k]
        query[rows, :] = (rotated(packed[:, 0:128], places, 1.0) * (HEAD**-0.5)).astype(BF16)
        key[rows, :] = rotated(packed[:, 128:256], places, 1.0).astype(BF16)
        value[rows, :] = packed[:, 256:384].astype(BF16)

    def project_back(k, n):
        rows = rows_at(n * RT, RT)
        grad_out[rows, :] = dot(grads[rows, :], wa[k, :, 384:512], 1, 0).astype(BF16)

    def each_tile(step, k):
        def body(n, carry):
            step(k, n)
            return carry

        lax.fori_loop(0, tiles, body, 0)

    block = min(128, length // 4)
    window = length // 4 + block

    def stacked(rows):
        if hp == 1:
            return rows
        zero = jnp.zeros_like(rows)
        return jnp.concatenate([jnp.where(first, rows, zero), jnp.where(first, zero, rows)], axis=0)

    def unstacked(rows):
        if hp == 1:
            return rows
        return jnp.where(first, rows[:window], rows[window:])

    def attend(k, s):
        key_sum[...] = jnp.zeros_like(key_sum)
        value_sum[...] = jnp.zeros_like(value_sum)

        def body(n, carry):
            q_at = pl.multiple_of(n * block, block)
            k_at = pl.multiple_of(jnp.maximum(q_at - length // 4, 0), block)
            q_rows = rows_at(s * length + q_at, block)
            k_rows = pl.ds(pl.multiple_of(s * length + k_at, block), window)
            q = query[q_rows, :]
            g = grad_out[q_rows, :]
            keys, values = stacked(key[k_rows, :]), stacked(value[k_rows, :])
            scores = dot(q, keys, 1, 1)
            grad_p = dot(g, values, 1, 1)
            at = k_at + lax.broadcasted_iota(jnp.int32, (block, window), 1)
            here = q_at + lax.broadcasted_iota(jnp.int32, (block, window), 0)
            own_doc_of = doc_column[s, pl.ds(q_at, block), 0:1].astype(F32)
            same = own_doc_of == docs[s, 0:1, pl.ds(k_at, window)]
            allowed = same & (at <= here)
            probs, grad_s = [], []
            for h in range(hp):
                cut = slice(h * window, (h + 1) * window)
                sc = jnp.where(allowed, scores[:, cut], -1e30)
                expos = jnp.exp(sc - jnp.max(sc, axis=-1, keepdims=True))
                p = expos / jnp.sum(expos, axis=-1, keepdims=True)
                gp = grad_p[:, cut]
                inner = jnp.sum(p * gp, axis=-1, keepdims=True)
                probs.append(p.astype(BF16))
                grad_s.append((p * (gp - inner)).astype(BF16))
            p = jnp.concatenate(probs, axis=1) if hp > 1 else probs[0]
            gs = jnp.concatenate(grad_s, axis=1) if hp > 1 else grad_s[0]
            attended[k, q_rows, :] = dot(p, values, 1, 0).astype(BF16)
            places = pl.ds(q_at, block)
            back = rotated(dot(gs, keys, 1, 0) * (HEAD**-0.5), places, -1.0)
            grad_z[k, q_rows, 0:128] = back.astype(BF16)
            here_rows = pl.ds(k_at, window)
            key_sum[here_rows, :] += unstacked(dot(gs, q, 0, 0))
            value_sum[here_rows, :] += unstacked(dot(p, g, 0, 0))
            return carry

        lax.fori_loop(0, length // block, body, 0)
        rows = rows_at(s * length, length)
        grad_z[k, rows, 128:256] = rotated(key_sum[...], slice(None), -1.0).astype(BF16)
        grad_z[k, rows, 256:384] = value_sum[...].astype(BF16)

    def hidden(k, n):
        rows = rows_at(n * RT, RT)
        u = dot(normed[rows, :], wu[k], 1, 0) + b_up[:, rows_at(j * units + k * pw, pw)]
        phi = 0.5 * (1.0 + lax.erf(u * np.float32(0.5**0.5)))
        active[k, rows, :] = (u * phi).astype(BF16)
        slope[k, rows, :] = phi + u * (jnp.exp(-0.5 * u * u) * np.float32((2 * np.pi) ** -0.5))

    def hidden_back(k, n):
        rows = rows_at(n * RT, RT)
        grad_u[k, rows, :] = (dot(grads[rows, :], wd[k], 1, 0) * slope[k, rows, :]).astype(BF16)

    HT = min(512, length)

    def branch(a, jj):
        def body(n, carry):
            rows = rows_at(jj * length + n * HT, HT)
            total = None
            for k in range(na):
                if a == 0:
                    part = dot(attended[k, rows, :], wa[k, :, 384:512], 1, 1)
                else:
                    part = dot(grad_z[k, rows, :], wa[k, :, 0:384], 1, 1)
                total = part if total is None else total + part
            for k in range(nm):
                if a == 0:
                    part = dot(active[k, rows, :], wd[k], 1, 1)
                else:
                    part = dot(grad_u[k, rows, :], wu[k], 1, 1)
                total = total + part
            partials[a][rows, :] = total.astype(BF16)
            return carry

        lax.fori_loop(0, length // HT, body, 0)

    def half_copy(a, jj):
        at = jj - (1 - c) * gx
        return copy(
            partials[a].at[rows_at(jj * length, length)],
            core_in.at[a % nbuf, rows_at(at * length, length)],
            half_send.at[a, at],
            half_recv.at[a, at],
            partner,
        )

    def branch_give(a, jj):
        branch(a, jj)
        half_copy(a, jj).start()

    def branches(a):
        for n, jj in enumerate((far_j, partner_j)[2 - gx :]):
            branch(a, jj)
            if n == 0 and nbuf == 1 and a == second:
                pl.semaphore_wait(credit.at[0], 1)
            half_copy(a, jj).start()
        for jj in (across_j, j)[2 - gx :]:
            branch(a, jj)

    def block_rows(jj, tt):
        return rows_at((jj * nt + tt) * R, R)

    def in_rows(jj, tt):
        return rows_at(((jj - c * gx) * nt + tt) * R, R)

    def both_cores(a, jj, tt, columns=slice(None)):
        return (
            partials[a][block_rows(jj, tt), columns].astype(F32)
            + core_in[a % nbuf, in_rows(jj, tt), columns].astype(F32)
        )

    def corner_t_copy(a, tt, src):
        b = partials[a].at[block_rows(across_j, tt), back_t]
        return copy(b, corner_t.at[a % nbuf, src], corner_t_send.at[2 + a, tt], corner_t_recv.at[2 + a, src], turned(tt))

    def corner_x_copy(a, jj, tt):
        b = partials[a].at[block_rows(jj, tt), back_x]
        return copy(b, corner_x.at[a % nbuf, tt], corner_x_send.at[2 + a, tt], corner_x_recv.at[2 + a, tt], across)

    def side_copy(a, jj):
        b = partials[a].at[block_rows(jj, t)]
        return copy(b, side_x.at[a % nbuf], side_send.at[2 + a], side_recv.at[2 + a], across)

    def turn_copy(a, tt, src):
        b = partials[a].at[block_rows(j, tt)]
        return copy(b, side_t.at[a % nbuf, src], turn_send.at[2 + a, tt], turn_recv.at[2 + a, src], turned(tt))

    def reduce_corner(a):
        if gx == 2:
            half_copy(a, far_j).wait_recv()
            for k in range(1, nt):
                tt = other_t(k)
                partials[a][block_rows(across_j, tt), :] = both_cores(a, across_j, tt).astype(BF16)
                corner_t_copy(a, tt, t).start()
                corner_x_copy(a, across_j, tt).start()

    def reduce_side(a):
        if gx == 2:
            total = both_cores(a, across_j, t, back_t)
            for k in range(1, nt):
                corner_t_copy(a, t, other_t(k)).wait_recv()
                total = total + corner_t[a % nbuf, other_t(k)].astype(F32)
            partials[a][block_rows(across_j, t), back_t] = total.astype(BF16)
            partials[a][block_rows(across_j, t), back_x] = both_cores(a, across_j, t, back_x).astype(BF16)
            side_copy(a, across_j).start()

    def reduce_turn(a):
        if nbuf == 1 and a == second and nt > 1:
            pl.semaphore_wait(credit.at[1], nt - 1)
        half_copy(a, partner_j).wait_recv()
        for k in range(1, nt):
            tt = other_t(k)
            if gx == 2:
                corner_x_copy(a, j, tt).wait_recv()
                total = both_cores(a, j, tt, back_x) + corner_x[a % nbuf, tt].astype(F32)
                partials[a][block_rows(j, tt), back_x] = total.astype(BF16)
                partials[a][block_rows(j, tt), back_t] = both_cores(a, j, tt, back_t).astype(BF16)
            else:
                partials[a][block_rows(j, tt), :] = both_cores(a, j, tt).astype(BF16)
            turn_copy(a, tt, t).start()

    def reduce_wait(a):
        if gx == 2:
            side_copy(a, across_j).wait_recv()
        for k in range(1, nt):
            turn_copy(a, t, other_t(k)).wait_recv()

    def reduced(a, n):
        mine = rows_at((j * nt + t) * R + n * tile, tile)
        came = rows_at(((j - c * gx) * nt + t) * R + n * tile, tile)
        rows = rows_at(n * tile, tile)
        total = partials[a][mine, :].astype(F32) + core_in[a % nbuf, came, :].astype(F32)
        if gx == 2:
            total = total + side_x[a % nbuf, rows, :].astype(F32)
        for k in range(1, nt):
            total = total + side_t[a % nbuf, other_t(k), rows, :].astype(F32)
        return restore(total)

    def reduce_sent(a):
        for xx in range(gx):
            half_copy(a, (1 - c) * gx + xx).wait_send()
        if gx == 2:
            side_copy(a, across_j).wait_send()
        for k in range(1, nt):
            tt = other_t(k)
            turn_copy(a, tt, t).wait_send()
            if gx == 2:
                corner_t_copy(a, tt, t).wait_send()
                corner_x_copy(a, across_j, tt).wait_send()

    def free_buffers():
        if nbuf == 1:
            pl.semaphore_signal(credit.at[0], inc=1, device_id=partner, device_id_type=MESH)
            for k in range(1, nt):
                pl.semaphore_signal(credit.at[1], inc=1, device_id=turned(other_t(k)), device_id_type=MESH)

    def write_output():
        def body(n, carry):
            rows = rows_at(n * tile, tile)
            total = tokens[rows, :].astype(F32) + reduced(0, n) + b_dense[...] + b_down[...]
            output[rows, :] = total.astype(BF16)
            return carry

        lax.fori_loop(0, R // tile, body, 0)
        result(0).start()

    def put(row, at, values):
        end = at + values.shape[1]
        for h in range(2):
            lo, hi = max(at, h * D // 2), min(end, (h + 1) * D // 2)
            if lo < hi:
                cols = slice(lo - h * D // 2, hi - h * D // 2)
                vec[2 * row + h : 2 * row + h + 1, cols] += values[:, lo - at : hi - at]

    def taken(array, row):
        return jnp.concatenate([array[2 * row : 2 * row + 1], array[2 * row + 1 : 2 * row + 2]], axis=1)

    def sum_biases():
        vec[...] = jnp.zeros_like(vec)
        for k in range(nm):
            put(3, k * pw, jnp.sum(grad_u[k].astype(F32), axis=0, keepdims=True))
        for k in range(na):
            put(3, units + k * 384, jnp.sum(grad_z[k].astype(F32), axis=0, keepdims=True))

    def write_input_grad():
        def body(n, carry):
            rows = rows_at(n * tile, tile)
            normal, inverse = normalize(tokens[rows, :].astype(F32))
            up = cotangent[rows, :].astype(F32)
            grad = reduced(1, n)
            put(0, 0, jnp.sum(grad * normal, axis=0, keepdims=True))
            put(1, 0, jnp.sum(grad, axis=0, keepdims=True))
            put(2, 0, jnp.sum(up, axis=0, keepdims=True))
            scaled = grad * gain[...]
            input_grad[rows, :] = up + inverse * (
                scaled
                - jnp.mean(scaled, axis=-1, keepdims=True)
                - normal * jnp.mean(scaled * normal, axis=-1, keepdims=True)
            )
            return carry

        lax.fori_loop(0, R // tile, body, 0)
        result(1).start()

    peers = nz if gx == 2 else 2 * nz
    mates = members * nt
    peer = z if gx == 2 else z * 2 + x
    mate = j * nt + t

    def peer_copy(to, src):
        device_to = device(to, x, c, t) if gx == 2 else device(to // 2, to % 2, c, t)
        return copy(vec_z.at[peer], vec_z.at[src], peer_send.at[to], peer_recv.at[src], device_to)

    def mate_copy(to, src):
        jj, tt = to // nt, to % nt
        device_to = device(z, jj % 2, jj // 2, tt) if gx == 2 else device(z, x, jj, tt)
        return copy(vec_m.at[mate], vec_m.at[src], mate_send.at[to], mate_recv.at[src], device_to)

    def sums_start():
        vec_z[peer] = vec[...]
        for k in range(1, peers):
            peer_copy(lax.rem(peer + k, peers), peer).start()

    def sums_group():
        for k in range(1, peers):
            peer_copy(peer, lax.rem(peer + k, peers)).wait_recv()
        total = vec_z[0]
        for k in range(1, peers):
            total = total + vec_z[k]
        vec_m[mate] = total
        for k in range(1, mates):
            mate_copy(lax.rem(mate + k, mates), mate).start()

    def sums_end():
        for k in range(1, mates):
            mate_copy(mate, lax.rem(mate + k, mates)).wait_recv()
        total = vec_m[0]
        for k in range(1, mates):
            total = total + vec_m[k]
        gain_grad[...] = taken(total, 0)
        shift_grad[...] = taken(total, 1)
        dense_bias[...] = taken(total, 2)
        for jj in range(members):
            row = taken(vec_m[jj * nt + t], 3)
            up_bias[:, jj * units : (jj + 1) * units] = row[:, :units]
            for k in range(na):
                part = row[:, units + k * 384 : units + (k + 1) * 384]
                heads = [part[:, p * 128 + h * HEAD : p * 128 + (h + 1) * HEAD] for h in range(hp) for p in range(3)]
                at = (jj * na + k) * wide
                qkv_bias[:, 3 * at : 3 * (at + wide)] = jnp.concatenate(heads, axis=1)

    def sums_sent():
        for k in range(1, peers):
            peer_copy(lax.rem(peer + k, peers), peer).wait_send()
        for k in range(1, mates):
            mate_copy(lax.rem(mate + k, mates), mate).wait_send()

    def forwards(some, lo, hi):
        for d in range(lo, hi):
            for i in some:
                forward_up(i, d)
                forward_down(i, d)

    def chains(some, lo, hi):
        for n in range(lo, hi):
            for i in some:
                chain_up(i, n)
                chain_down(i, n)

    second = 0 if gx == 2 else 1

    def any_order():
        stage()
        fill_normed()
        enter()
        for i in U + A + Dn:
            send_first(i)
            share(i)
        give_docs()
        act_start(0)
        fill_grads()
        act_start(1)
        for i in U + A:
            send_own(i)
        prepare()
        prepare_docs()
        forwards(U + A, 1, 2)
        act_from_turn(0)
        act_from_side(0)
        for i in Dn:
            send_own(i)
        forwards(U, 2, nz)
        act_finish(0)
        act_wait(0)
        for i in U:
            gathered(i)
            each_tile(hidden, i - na)
        act_from_turn(1)
        act_from_side(1)
        forwards(A, 2, nz)
        forwards(Dn, 1, nz)
        act_finish(1)
        act_wait(1)
        for i in Dn:
            weight_grad(i)
            sum_x(i)
        chains(Dn, 0, nz - 1)
        for i in A:
            gathered(i)
            each_tile(project, i)
            each_tile(project_back, i)
            for s in range(members):
                attend(i, s)
            weight_grad(i)
            sum_x(i)
        chains(A, 0, nz - 1)
        for i in Dn:
            gathered(i)
            each_tile(hidden_back, i - na - nm)
        for i in U:
            weight_grad(i)
            sum_x(i)
        act_sent(0)
        act_sent(1)
        sum_biases()
        for a in (1, 0) if gx == 2 else (0, 1):
            branches(a)
            reduce_corner(a)
            if a != second:
                chains(U, 0, nz - 1)
            reduce_side(a)
            reduce_turn(a)
            if a != second:
                for i in Dn + A:
                    chain_end(i)
            reduce_wait(a)
            if a == 0:
                write_output()
            else:
                write_input_grad()
                sums_start()
            if a != second:
                free_buffers()
        for i in U:
            chain_end(i)
        sums_group()
        for i in Dn + A + U:
            finish(i)
        sums_end()

    def tuned_order():
        (a,), (u,), (d,) = A, U, Dn
        stage()
        enter()
        share(a)
        give_docs()
        send_first(d)
        fill_normed()
        send_first(u)
        share(u)
        prepare()
        send_first(a)
        fill_grads()
        act_start_turn(0)
        send_own(a)
        act_start_side(0)
        act_start_side(1)
        act_start_turn(1)
        send_own(u)
        forward_up(a, 1)
        share(d)
        forward_down(a, 1)
        forward_down(u, 1)
        forward_down(a, 2)
        forward_up(u, 1)
        prepare_docs()
        forward_up(a, 2)
        act_from_turn(0)
        act_from_side(0)
        act_wait_of(0, partner_j)
        forward_down(u, 2)
        forward_up(u, 2)
        forward_up(a, 3)
        forward_down(a, 3)
        act_from_side(1)
        act_from_turn(1)
        project(0, partner_j)
        send_own(d)
        project_back(0, j)
        project(0, j)
        attend(0, j)
        act_wait_of(1, partner_j)
        act_finish(0)
        forward_down(u, 3)
        forward_up(u, 3)
        hidden(0, across_j)
        hidden(0, j)
        act_wait_of(0, far_j)
        hidden(0, partner_j)
        hidden(0, far_j)
        act_finish(1)
        forward_up(d, 1)
        forward_down(d, 1)
        project(0, across_j)
        project(0, far_j)
        act_wait_of(1, far_j)
        weight_grad_cut(d, 0)
        chain_down(d, 0)
        weight_grad_cut(d, 1)
        chain_up(d, 0)
        project_back(0, far_j)
        attend(0, far_j)
        project_back(0, across_j)
        forward_up(d, 2)
        forward_down(d, 2)
        attend(0, across_j)
        chain_down(d, 1)
        project_back(0, partner_j)
        chain_up(d, 1)
        attend(0, partner_j)
        forward_down(d, 3)
        forward_up(d, 3)
        hidden_back(0, far_j)
        branch_give(1, far_j)
        hidden_back(0, across_j)
        chain_down(d, 2)
        chain_up(d, 2)
        branch(1, across_j)
        reduce_corner(1)
        weight_grad_cut(a, 0)
        weight_grad_cut(a, 1)
        chain_down(a, 0)
        chain_up(a, 0)
        act_sent(0)
        act_sent(1)
        branch_give(0, far_j)
        hidden_back(0, j)
        hidden_back(0, partner_j)
        branch(0, across_j)
        weight_grad_cut(u, 0)
        reduce_corner(0)
        chain_down(u, 0)
        weight_grad_cut(u, 1)
        chain_up(u, 0)
        sum_biases()
        chain_end(d)
        chain_up(a, 1)
        reduce_side(1)
        branch(1, j)
        branch_give(1, partner_j)
        chain_down(a, 1)
        branch(0, j)
        reduce_turn(1)
        branch_give(0, partner_j)
        chain_up(u, 1)
        chain_down(u, 1)
        finish(d)
        reduce_side(0)
        reduce_turn(0)
        chain_up(a, 2)
        chain_down(a, 2)
        reduce_wait(1)
        write_input_grad()
        sums_start()
        chain_down(u, 2)
        chain_up(u, 2)
        chain_end(a)
        sums_group()
        chain_end(u)
        sums_end()
        reduce_wait(0)
        write_output()
        finish(a)
        finish(u)

    if (gx, na, nm, nz, tiles, RT) == (2, 1, 1, 4, 4, length):
        tuned_order()
    else:
        any_order()

    for i in range(count):
        for k in range(1, members):
            g_final(i, other_j(k), j).wait_send()
            give_part(i, other_j(k)).wait_send()
        for src in range(nz):
            pl.when((z < nz - 1) & (src <= z))(lambda: send_up(i, src).wait_send())
            pl.when((z > 0) & (src >= z))(lambda: send_down(i, src).wait_send())
            pl.when(src > z)(lambda: g_up(i, src).wait_send())
            pl.when(src < z)(lambda: g_down(i, src).wait_send())
            if gx == 1:
                send_across(i, src, x).wait_send()
                g_across(i, src).wait_send()
    for k in range(1, members):
        own_doc(other_j(k)).wait_send()
    reduce_sent(0)
    reduce_sent(1)
    sums_sent()
    for n in range(len(results)):
        result(n).wait()


def hand_out(arrays):
    wide = [n for n, array in enumerate(arrays) if array.shape[0] > 1]
    thin = [n for n, array in enumerate(arrays) if array.shape[0] == 1]

    def body(*refs):
        count = len(arrays)
        given, taken, buffers, sems = refs[:count], refs[count : 2 * count], refs[2 * count : -1], refs[-1]
        reads = [pltpu.make_async_copy(given[n], buffers[i], sems.at[0, i]) for i, n in enumerate(wide)]
        writes = [pltpu.make_async_copy(buffers[i], taken[n], sems.at[1, i]) for i, n in enumerate(wide)]
        for read in reads:
            read.start()
        for n in thin:
            taken[n][...] = given[n][0]
        for read, write in zip(reads, writes):
            read.wait()
            write.start()
        for write in writes:
            write.wait()

    def specs():
        return [pl.BlockSpec(memory_space=pltpu.VMEM if n in thin else pl.ANY) for n in range(len(arrays))]

    return list(
        pl.pallas_call(
            body,
            out_shape=[
                jax.ShapeDtypeStruct(array.shape[1:] if n in thin else array.shape, array.dtype)
                for n, array in enumerate(arrays)
            ],
            in_specs=specs(),
            out_specs=specs(),
            scratch_shapes=[pltpu.VMEM(arrays[n].shape, arrays[n].dtype) for n in wide]
            + [pltpu.SemaphoreType.DMA((2, len(wide)))],
            name="hand_out",
        )(*arrays)
    )


def on_device(
    nt,
    n_dp,
    tokens,
    cotangent,
    segments,
    ln_gain,
    ln_bias,
    w_qkv,
    b_qkv,
    w_dense,
    b_dense,
    w_up,
    b_up,
    w_down,
    b_down,
):
    R, D = tokens.shape
    length = segments.shape[1]
    r = w_qkv.shape[0]
    nz = n_dp // 4
    heads = w_qkv.shape[1] // (3 * HEAD)
    gx = 2 if heads % 4 == 0 and 4 * length * D <= 1 << 21 else 1
    members = 2 * gx
    heads = heads // members
    hp = 2 if heads % 2 == 0 else 1
    na = heads // hp
    units = w_up.shape[1] // members
    pw = 512 if units % 512 == 0 else units
    nm = units // pw
    nbuf = gx
    peers, mates = (nz if gx == 2 else 2 * nz), members * nt
    sizes = dict(nt=nt, nz=nz, gx=gx, na=na, nm=nm, hp=hp, length=length, R=R, r=r, pw=pw, nbuf=nbuf)

    widths = ((na, 512), (nm, pw), (nm, pw))
    count = na + 2 * nm
    rows = members * length
    own = D if gx == 2 else D // 2
    chip = 2 * r
    split = D // 4
    V = pltpu.VMEM
    DMA = pltpu.SemaphoreType.DMA

    def some(shape):
        return V(shape if gx == 2 else (1, 1, 8, 128)[-len(shape) :], BF16)

    scratch = (
        [V((members, na, r, 512), BF16), V((na, 1, 384), F32)]
        + [V((length, 128), F32)] * 2
        + [V((members, 8, length), F32), V((members, length, 128), BF16)]
        + [V((n, D, w), BF16) for n, w in widths]
        + [V((rows, D), BF16), V((rows, D), BF16)]
        + [V((rows, 128), BF16)] * 4
        + [V((na, rows, 128), BF16), V((na, rows, 384), BF16)]
        + [V((length, 128), F32)] * 2
        + [V((nm, rows, pw), BF16), V((nm, rows, pw), F32), V((nm, rows, pw), BF16)]
        + [V((rows, D) if gx == 2 else (8, 128), BF16)]
        + [V((nbuf, gx * length, D), BF16), some((nbuf, nt, R, split)), some((nbuf, nt, R, D - split))]
        + [some((nbuf, R, D)), V((nbuf, nt, R, D), BF16)]
        + [V((n, own, w), F32) for n, w in widths]
        + [V((n, own, w) if gx == 1 else (n, 8, 128), BF16) for _ in range(2) for n, w in widths]
        + [V((n, own, w), BF16) for _ in range(3) for n, w in widths]
        + [V((n, gx * chip, w), BF16) for n, w in widths]
        + [V((n, members, r, w), BF16) for n, w in widths]
        + [V((8, D // 2), F32), V((peers, 8, D // 2), F32), V((mates, 8, D // 2), F32)]
        + [DMA((count,)), DMA((10,)), DMA((count + 1, members)), DMA((count + 1, members))]
        + [DMA((count, nz))] * 5
        + [DMA((4, nt))] * 2
        + [DMA((4,))] * 2
        + [DMA((4, nt))] * 4
        + [DMA((2, members, nt))] * 2
        + [DMA((count, nz))] * 6
        + [DMA((count, members))] * 2
        + [DMA((2, gx))] * 2
        + [DMA((peers,))] * 2
        + [DMA((mates,))] * 2
        + [pltpu.SemaphoreType.REGULAR((2,))]
    )
    space, far = pl.BlockSpec(memory_space=pltpu.VMEM), pl.BlockSpec(memory_space=pl.ANY)

    def row(vector):
        return vector.reshape(1, -1)

    args = (
        tokens,
        cotangent,
        segments,
        row(ln_gain),
        row(ln_bias),
        w_qkv,
        b_qkv,
        w_dense.T,
        row(b_dense),
        w_up,
        row(b_up),
        w_down.T,
        row(b_down),
    )
    shapes = (
        jax.ShapeDtypeStruct((R, D), BF16),
        jax.ShapeDtypeStruct((R, D), F32),
        jax.ShapeDtypeStruct((1, D), F32),
        jax.ShapeDtypeStruct((1, D), F32),
        jax.ShapeDtypeStruct(w_qkv.shape, F32),
        jax.ShapeDtypeStruct((1, w_qkv.shape[1]), F32),
        jax.ShapeDtypeStruct(w_dense.shape[::-1], F32),
        jax.ShapeDtypeStruct((1, D), F32),
        jax.ShapeDtypeStruct(w_up.shape, F32),
        jax.ShapeDtypeStruct((1, w_up.shape[1]), F32),
        jax.ShapeDtypeStruct(w_down.shape[::-1], F32),
    )
    out = pl.pallas_call(
        functools.partial(kernel, sizes),
        out_shape=shapes,
        in_specs=[far if n in (0, 1, 5, 7, 9, 11) else space for n in range(len(args))],
        out_specs=[space if n in (2, 3, 5, 7, 9) else far for n in range(len(shapes))],
        scratch_shapes=[V(args[n].shape, BF16) for n in (0, 1, 5, 7)]
        + [V(shapes[n].shape, shapes[n].dtype) for n in (0, 1, 4, 6, 8, 10)]
        + scratch,
        compiler_params=pltpu.CompilerParams(
            collective_id=0, has_side_effects=True, vmem_limit_bytes=67043328
        ),
        name="layer",
    )(*args)
    out = hand_out((*out, out[7]))
    out[6], out[10] = out[6].T, out[10].T
    return tuple(out)


def solution(mesh):
    return jax.shard_map(
        functools.partial(on_device, mesh.shape["tensor"], mesh.shape["dp"]),
        mesh=mesh,
        in_specs=(
            P(("dp", "tensor"), None),
            P(("dp", "tensor"), None),
            P("dp", None),
            P(),
            P(),
            P("dp", "tensor"),
            P("tensor"),
            P("tensor", "dp"),
            P(),
            P("dp", "tensor"),
            P("tensor"),
            P("tensor", "dp"),
            P(),
        ),
        out_specs=(
            P(("dp", "tensor"), None),
            P(("dp", "tensor"), None),
            P(),
            P(),
            P("dp", "tensor"),
            P("tensor"),
            P("tensor", "dp"),
            P(),
            P("dp", "tensor"),
            P("tensor"),
            P("tensor", "dp"),
            P(),
        ),
        check_vma=False,
    )
```

```python
import functools

import jax
import jax.numpy as jnp
import numpy as np
from jax import lax
from jax.experimental import pallas as pl
from jax.experimental.pallas import tpu as pltpu
from jax.sharding import PartitionSpec as P

HEAD = 64
ROT = 16
NORM_EPS = 1e-05
ROTARY_BASE = 10000.0
MESH = pl.DeviceIdType.MESH
F32 = jnp.float32
BF16 = jnp.bfloat16


def dot(left, right, over_left, over_right):
    return lax.dot_general(
        left, right, (((over_left,), (over_right,)), ((), ())), preferred_element_type=F32
    )


def normalize(rows):
    centred = rows - jnp.mean(rows, axis=-1, keepdims=True)
    inverse = lax.rsqrt(jnp.mean(centred * centred, axis=-1, keepdims=True) + NORM_EPS)
    return centred * inverse, inverse


def padded(array):
    rest = -array.shape[1] % 128
    return jnp.concatenate([array, jnp.zeros((array.shape[0], rest), array.dtype)], axis=1) if rest else array


def kernel(
    sizes,
    tokens_hbm,
    cotangent_hbm,
    segments,
    gain,
    shift,
    w_qkv_hbm,
    b_qkv,
    w_dense_hbm,
    b_dense,
    w_up,
    b_up,
    w_down,
    b_down,
    output_hbm,
    input_grad_hbm,
    gain_grad,
    shift_grad,
    qkv_grad_hbm,
    qkv_bias,
    dense_grad_hbm,
    dense_bias,
    up_grad_hbm,
    up_bias,
    down_grad_hbm,
    tokens,
    cotangent,
    w_qkv,
    w_dense,
    output,
    input_grad,
    qkv_grad,
    dense_grad,
    up_grad,
    down_grad,
    wa_in,
    ba,
    cos_table,
    sin_table,
    docs,
    doc_column,
    wa,
    wu,
    wd,
    normed,
    grads,
    query,
    key,
    value,
    grad_out,
    attended,
    grad_z,
    key_sum,
    value_sum,
    active,
    slope,
    grad_u,
    late,
    core_in,
    corner_x,
    corner_t,
    side_x,
    side_t,
    own_a,
    own_u,
    own_d,
    xs_a,
    xs_u,
    xs_d,
    xr_a,
    xr_u,
    xr_d,
    zs_a,
    zs_u,
    zs_d,
    zu_a,
    zu_u,
    zu_d,
    zd_a,
    zd_u,
    zd_d,
    fs_a,
    fs_u,
    fs_d,
    fr_a,
    fr_u,
    fr_d,
    vec,
    vec_z,
    vec_m,
    local_sem,
    io_sem,
    share_send,
    share_recv,
    up_send,
    down_send,
    z_recv,
    x_send,
    x_recv,
    turn_send,
    turn_recv,
    side_send,
    side_recv,
    corner_x_send,
    corner_x_recv,
    corner_t_send,
    corner_t_recv,
    pass_send,
    pass_recv,
    gx_send,
    gx_recv,
    g_send,
    g_recv,
    fin_send,
    fin_recv,
    half_send,
    half_recv,
    peer_send,
    peer_recv,
    mate_send,
    mate_recv,
    credit,
):
    nt, nz, gx, na, nm, hp, length, R, r, pw, nbuf = (
        sizes[k] for k in ("nt", "nz", "gx", "na", "nm", "hp", "length", "R", "r", "pw", "nbuf")
    )
    D = tokens.shape[1]
    chip = 2 * r
    zb = gx * chip
    own = D if gx == 2 else D // 2
    members = 2 * gx
    wide = hp * HEAD
    units = nm * pw
    total_rows = members * length
    partials = (grads, late if gx == 2 else normed)
    dp, t = lax.axis_index("dp"), lax.axis_index("tensor")
    z, x, c = dp // 4, (dp // 2) % 2, dp % 2
    j = c * gx + x if gx == 2 else c

    def device(zz, xx, cc, tt):
        return (zz * 4 + xx * 2 + cc, tt)

    partner = device(z, x, 1 - c, t)
    across = device(z, 1 - x, c, t)

    def member(jj):
        return device(z, jj % 2, jj // 2, t) if gx == 2 else device(z, x, jj, t)

    def along(zz):
        return device(zz, x, c, t)

    def turned(tt):
        return device(z, x, c, tt)

    def other_j(k):
        return lax.rem(j + k, members)

    def other_z(k):
        return lax.rem(z + k, nz)

    def other_t(k):
        return lax.rem(t + k, nt)

    def step_of(src, tt):
        return lax.rem(tt - src + nt, nt) - 1

    def rows_at(start, size):
        return pl.ds(pl.multiple_of(start, size), size)

    def copy(src, dst, send, recv, to):
        return pltpu.make_async_remote_copy(
            src_ref=src, dst_ref=dst, send_sem=send, recv_sem=recv, device_id=to, device_id_type=MESH
        )

    A = list(range(na))
    U = list(range(na, na + nm))
    Dn = list(range(na + nm, na + 2 * nm))
    count = na + 2 * nm

    def of(a, u, d, i):
        if i in A:
            return a.at[i]
        return u.at[i - na] if i in U else d.at[i - na - nm]

    def weights(i):
        return of(wa, wu, wd, i)

    def z_rows(zz):
        return rows_at(zz * zb if gx == 2 else (x * nz + zz) * chip, zb)

    own_rows = rows_at(z * zb + (x * 2 + c) * r if gx == 2 else (x * nz + z) * chip + c * r, r)

    barrier = pltpu.get_barrier_semaphore()
    greeted = [member(other_j(k)) for k in range(1, members)] + ([] if gx == 2 else [across])
    greeted += [
        device(z, jj % 2 if gx == 2 else x, jj // 2 if gx == 2 else jj, other_t(k))
        for k in range(1, nt)
        for jj in [other_j(n) for n in range(members)]
    ]

    def greet(other):
        pl.semaphore_signal(barrier, inc=1, device_id=other, device_id_type=MESH)

    for other in greeted:
        greet(other)
    pl.when(z > 0)(lambda: greet(along(z - 1)))
    pl.when(z < nz - 1)(lambda: greet(along(z + 1)))

    reads = [
        pltpu.make_async_copy(src, dst, io_sem.at[n])
        for n, (src, dst) in enumerate(
            ((w_qkv_hbm, w_qkv), (w_dense_hbm, w_dense), (tokens_hbm, tokens), (cotangent_hbm, cotangent))
        )
    ]
    for read in reads:
        read.start()

    def enter():
        pl.semaphore_wait(barrier, len(greeted) + jnp.minimum(z, 1) + jnp.minimum(nz - 1 - z, 1))

    results = (
        (output, output_hbm),
        (input_grad, input_grad_hbm),
        (qkv_grad, qkv_grad_hbm),
        (dense_grad, dense_grad_hbm),
        (up_grad, up_grad_hbm),
        (down_grad, down_grad_hbm),
    )

    def result(n):
        return pltpu.make_async_copy(*results[n], io_sem.at[4 + n])

    def part_of(i, jj):
        if i in A:
            return wa_in.at[jj, i]
        ref, k = (w_up, i - na) if i in U else (w_down, i - na - nm)
        return ref.at[:, rows_at(jj * units + k * pw, pw)]

    def local_copy(i):
        return pltpu.make_async_copy(part_of(i, j), weights(i).at[own_rows], local_sem.at[i])

    def give_part(i, jj):
        dst = weights(i).at[own_rows]
        return copy(part_of(i, jj), dst, share_send.at[i], share_recv.at[i], member(jj))

    def all_parts(i):
        rows = weights(i).at[pl.ds(0, (members - 1) * r)]
        return copy(rows, rows, share_send.at[i], share_recv.at[i], partner)

    def member_rows(jj):
        return rows_at(z * zb + (jj % 2 * 2 + jj // 2) * r if gx == 2 else (x * nz + z) * chip + jj * r, r)

    def share(i):
        local_copy(i).start()
        for k in range(1, members):
            give_part(i, other_j(k)).start()

    def head_part(array, jj, k, part):
        at = [((jj * na + k) * hp + h) * 3 * HEAD + part * HEAD for h in range(hp)]
        return padded(jnp.concatenate([array[:, a : a + HEAD] for a in at], axis=1))

    def own_doc(jj):
        return copy(docs.at[j], docs.at[j], share_send.at[count], share_recv.at[count], member(jj))

    def all_docs():
        rows = docs.at[pl.ds(0, members - 1)]
        return copy(rows, rows, share_send.at[count], share_recv.at[count], partner)

    def stage():
        reads[0].wait()
        reads[1].wait()
        for jj in range(members):
            for k in range(na):
                for part in range(3):
                    wa_in[jj, k, :, part * 128 : (part + 1) * 128] = head_part(w_qkv[...], jj, k, part)
                at = (jj * na + k) * wide
                wa_in[jj, k, :, 384:512] = padded(w_dense[:, at : at + wide])
        docs[j] = jnp.broadcast_to(segments[...].astype(F32), docs.shape[1:])

    def give_docs():
        for k in range(1, members):
            own_doc(other_j(k)).start()

    def permute(rows):
        if gx == 2:
            return rows
        return jnp.concatenate(
            [rows[:, (zz * 2 + xx) * chip : (zz * 2 + xx + 1) * chip] for xx in range(2) for zz in range(nz)],
            axis=1,
        )

    def restore(rows):
        if gx == 2:
            return rows
        return jnp.concatenate(
            [rows[:, (xx * nz + zz) * chip : (xx * nz + zz + 1) * chip] for zz in range(nz) for xx in range(2)],
            axis=1,
        )

    acts = (normed, grads)
    tile = min(64, R)
    split = D * 3 // 8
    over_x, over_t = slice(0, split), slice(split, D)
    back_split = D // 4
    back_x, back_t = slice(0, back_split), slice(back_split, D)

    def act_rows(jj, tt):
        return rows_at((jj * nt + tt) * R, R)

    across_j = c * gx + 1 - x if gx == 2 else c
    partner_j = (1 - c) * gx + x if gx == 2 else 1 - c
    far_j = (1 - c) * gx + 1 - x if gx == 2 else 1 - c
    near = (j, partner_j, across_j, far_j)

    def fill_normed():
        reads[2].wait()

        def body(n, carry):
            rows = rows_at(n * tile, tile)
            normal, _ = normalize(tokens[rows, :].astype(F32))
            normed[rows_at((j * nt + t) * R + n * tile, tile), :] = permute(
                (normal * gain[...] + shift[...]).astype(BF16)
            )
            return carry

        lax.fori_loop(0, R // tile, body, 0)

    def fill_grads():
        reads[3].wait()

        def body(n, carry):
            grads[rows_at((j * nt + t) * R + n * tile, tile), :] = permute(cotangent[rows_at(n * tile, tile), :])
            return carry

        lax.fori_loop(0, R // tile, body, 0)

    def act_turn(a, tt, src):
        b = acts[a].at[act_rows(j, src)]
        return copy(b, b, turn_send.at[a, step_of(src, tt)], turn_recv.at[a, step_of(src, tt)], turned(tt))

    def act_side(a, jj):
        b = acts[a].at[act_rows(jj, t)]
        return copy(b, b, side_send.at[a], side_recv.at[a], across)

    def act_corner_x(a, jj, tt):
        b = acts[a].at[act_rows(jj, tt), over_x]
        return copy(b, b, corner_x_send.at[a, step_of(t, tt)], corner_x_recv.at[a, step_of(t, tt)], across)

    def act_corner_t(a, tt, src):
        b = acts[a].at[act_rows(across_j, src), over_t]
        return copy(b, b, corner_t_send.at[a, step_of(src, tt)], corner_t_recv.at[a, step_of(src, tt)], turned(tt))

    def act_pass(a, jj, tt):
        b = acts[a].at[act_rows(jj, tt)]
        return copy(b, b, pass_send.at[a, jj % gx, tt], pass_recv.at[a, jj % gx, tt], partner)

    def act_start_side(a):
        if gx == 2:
            act_side(a, j).start()

    def act_start_turn(a):
        for k in range(1, nt):
            act_turn(a, other_t(k), t).start()
        act_pass(a, j, t).start()

    def act_start(a):
        act_start_side(a)
        act_start_turn(a)

    def act_from_turn(a):
        for k in range(1, nt):
            src = other_t(k)
            act_turn(a, t, src).wait_recv()
            if gx == 2:
                act_corner_x(a, j, src).start()
            act_pass(a, j, src).start()

    def act_from_side(a):
        if gx == 2:
            act_side(a, across_j).wait_recv()
            for k in range(1, nt):
                act_corner_t(a, other_t(k), t).start()
            act_pass(a, across_j, t).start()

    def act_finish(a):
        if gx == 2:
            for k in range(1, nt):
                src = other_t(k)
                act_corner_x(a, across_j, src).wait_recv()
                act_corner_t(a, t, src).wait_recv()
                act_pass(a, across_j, src).start()

    def act_wait_of(a, jj):
        for k in range(nt):
            act_pass(a, jj, k).wait_recv()

    def act_wait(a):
        for xx in range(gx):
            act_wait_of(a, (1 - c) * gx + xx)

    def act_sent(a):
        if gx == 2:
            act_side(a, j).wait_send()
        for k in range(1, nt):
            act_turn(a, other_t(k), t).wait_send()
            if gx == 2:
                act_corner_x(a, j, other_t(k)).wait_send()
                act_corner_t(a, other_t(k), t).wait_send()
        for xx in range(gx):
            for k in range(nt):
                act_pass(a, c * gx + xx, k).wait_send()

    def w_block(i, zz):
        return weights(i).at[z_rows(zz)]

    def send_up(i, src):
        b = w_block(i, src)
        return copy(b, b, up_send.at[i], z_recv.at[i, src], along(z + 1))

    def send_down(i, src):
        b = w_block(i, src)
        return copy(b, b, down_send.at[i], z_recv.at[i, src], along(z - 1))

    def send_across(i, src, xx):
        b = weights(i).at[rows_at((xx * nz + src) * chip, chip)]
        return copy(b, b, x_send.at[i, src], x_recv.at[i, src], across)

    def send_first(i):
        def along_z(sems, to):
            return copy(part_of(i, j), weights(i).at[own_rows], sems.at[i], z_recv.at[i, z], to)

        pl.when(z < nz - 1)(lambda: along_z(up_send, along(z + 1)).start())
        pl.when(z > 0)(lambda: along_z(down_send, along(z - 1)).start())

    def send_own(i):
        local_copy(i).wait()
        all_parts(i).wait_recv()
        for k in range(1, members):
            jj = other_j(k)
            rows = weights(i).at[member_rows(jj)]

            def along_z(sems, to):
                return copy(rows, rows, sems.at[i], z_recv.at[i, z], to)

            pl.when(z < nz - 1)(lambda: along_z(up_send, along(z + 1)).start())
            pl.when(z > 0)(lambda: along_z(down_send, along(z - 1)).start())
        if gx == 1:
            send_across(i, z, x).start()

    def forward_up(i, d):
        @pl.when(z >= d)
        def _():
            send_up(i, z - d).wait_recv()
            pl.when(z < nz - 1)(lambda: send_up(i, z - d).start())
            if gx == 1:
                send_across(i, z - d, x).start()

    def forward_down(i, d):
        @pl.when(z + d <= nz - 1)
        def _():
            send_down(i, z + d).wait_recv()
            pl.when(z > 0)(lambda: send_down(i, z + d).start())
            if gx == 1:
                send_across(i, z + d, x).start()

    def gathered(i):
        if gx == 1:
            for src in range(nz):
                send_across(i, src, 1 - x).wait_recv()

    def own_of(i):
        return of(own_a, own_u, own_d, i)

    def g_across(i, to_z):
        b = pl.ds(to_z * chip, chip)
        return copy(
            of(xs_a, xs_u, xs_d, i).at[b],
            of(xr_a, xr_u, xr_d, i).at[b],
            gx_send.at[i, to_z],
            gx_recv.at[i, to_z],
            across,
        )

    def g_up(i, to_z):
        b = rows_at(to_z * zb, zb)
        return copy(
            of(zs_a, zs_u, zs_d, i).at[b],
            of(zu_a, zu_u, zu_d, i).at[b],
            g_send.at[i],
            g_recv.at[i, to_z + 1],
            along(z + 1),
        )

    def g_down(i, to_z):
        b = rows_at(to_z * zb, zb)
        return copy(
            of(zs_a, zs_u, zs_d, i).at[b],
            of(zd_a, zd_u, zd_d, i).at[b],
            g_send.at[i],
            g_recv.at[i, to_z],
            along(z - 1),
        )

    def g_final(i, jj, src):
        at = (jj % 2 * 2 + jj // 2) * r if gx == 2 else jj * r
        return copy(
            of(fs_a, fs_u, fs_d, i).at[rows_at(at, r)],
            of(fr_a, fr_u, fr_d, i).at[src],
            fin_send.at[i],
            fin_recv.at[i],
            member(jj),
        )

    def all_given(i):
        rows = of(fs_a, fs_u, fs_d, i).at[pl.ds(0, (members - 1) * r)]
        return copy(rows, rows, fin_send.at[i], fin_recv.at[i], partner)

    def all_taken(i):
        rows = of(fr_a, fr_u, fr_d, i).at[pl.ds(0, members - 1)]
        return copy(rows, rows, fin_send.at[i], fin_recv.at[i], partner)

    def products(i, columns):
        if i in A:
            return [
                (0, 384, dot(normed[:, columns], grad_z[i], 0, 0)),
                (384, 512, dot(grads[:, columns], attended[i], 0, 0)),
            ]
        if i in U:
            return [(0, pw, dot(normed[:, columns], grad_u[i - na], 0, 0))]
        return [(0, pw, dot(grads[:, columns], active[i - na - nm], 0, 0))]

    cut = min(512, own)

    def weight_grad_cut(i, n):
        at = n * cut if gx == 2 else x * own + n * cut
        for lo, hi, part in products(i, rows_at(at, cut)):
            own_of(i)[n * cut : (n + 1) * cut, lo:hi] = part

    def weight_grad(i):
        if gx == 1:
            xs = of(xs_a, xs_u, xs_d, i)
            for n in range(own // cut):
                for lo, hi, part in products(i, rows_at((1 - x) * own + n * cut, cut)):
                    xs[n * cut : (n + 1) * cut, lo:hi] = part.astype(BF16)
            for to_z in range(nz):
                g_across(i, to_z).start()
        for n in range(own // cut):
            weight_grad_cut(i, n)

    def sum_x(i):
        if gx == 1:
            xr = of(xr_a, xr_u, xr_d, i)
            for to_z in range(nz):
                g_across(i, to_z).wait_recv()
                b = slice(to_z * chip, (to_z + 1) * chip)
                own_of(i)[b, :] += xr[b, :].astype(F32)

    def chain_step(i, to_z, last, came, buffer, send):
        b = rows_at(to_z * zb, zb)
        zs = of(zs_a, zs_u, zs_d, i)

        @pl.when(last)
        def _():
            zs[b, :] = own_of(i)[b, :].astype(BF16)

        @pl.when(jnp.logical_not(last))
        def _():
            came.wait_recv()
            zs[b, :] = (own_of(i)[b, :] + buffer[b, :].astype(F32)).astype(BF16)

        send.start()

    def chain_up(i, n):
        @pl.when(z <= n)
        def _():
            to_z = nz - 1 - n + z
            chain_step(i, to_z, z == 0, g_up(i, to_z), of(zu_a, zu_u, zu_d, i), g_up(i, to_z))

    def chain_down(i, n):
        @pl.when(nz - 1 - z <= n)
        def _():
            to_z = n - (nz - 1 - z)
            chain_step(i, to_z, z == nz - 1, g_down(i, to_z), of(zd_a, zd_u, zd_d, i), g_down(i, to_z))

    def own_index():
        return x * 2 + c if gx == 2 else c

    def chain_end(i):
        b = rows_at(z * zb, zb)

        @pl.when(z > 0)
        def _():
            g_up(i, z).wait_recv()
            own_of(i)[b, :] += of(zu_a, zu_u, zu_d, i)[b, :].astype(F32)

        @pl.when(z < nz - 1)
        def _():
            g_down(i, z).wait_recv()
            own_of(i)[b, :] += of(zd_a, zd_u, zd_d, i)[b, :].astype(F32)

        of(fs_a, fs_u, fs_d, i)[...] = own_of(i)[b, :].astype(BF16)
        for k in range(1, members):
            g_final(i, other_j(k), j).start()

    def finish(i):
        all_taken(i).wait_recv()
        keep = own_of(i)[rows_at(z * zb + own_index() * r, r), :]
        came = of(fr_a, fr_u, fr_d, i)
        for jj in range(members):
            part = jnp.where(j == jj, keep, came[jj].astype(F32))
            if i in A:
                heads = [
                    part[:, p * 128 + h * HEAD : p * 128 + (h + 1) * HEAD] for h in range(hp) for p in range(3)
                ]
                at = (jj * na + i) * wide
                qkv_grad[:, 3 * at : 3 * (at + wide)] = jnp.concatenate(heads, axis=1)
                dense_grad[:, at : at + wide] = part[:, 384 : 384 + wide]
            else:
                out, k = (up_grad, i - na) if i in U else (down_grad, i - na - nm)
                out[:, jj * units + k * pw : jj * units + (k + 1) * pw] = part
        if i == A[-1]:
            result(2).start()
            result(3).start()
        if i in (U[-1], Dn[-1]):
            result(4 if i in U else 5).start()

    def pick(parts):
        total = parts[0]
        for jj in range(1, members):
            total = jnp.where(j == jj, parts[jj], total)
        return total

    def prepare():
        for k in range(na):
            for part in range(3):
                ba[k, :, part * 128 : (part + 1) * 128] = pick(
                    [head_part(b_qkv[...].reshape(1, -1), jj, k, part) for jj in range(members)]
                )
        steps = np.arange(ROT // 2, dtype=np.float32) * 2.0 / ROT
        inverse = (np.float32(ROTARY_BASE) ** -steps).astype(np.float32)
        lane = lax.broadcasted_iota(jnp.int32, (128, 128), 1) % HEAD
        scale = jnp.zeros((128, 128), F32)
        for n in range(ROT):
            scale = jnp.where(lane == n, inverse[n % (ROT // 2)], scale)

        def table(n, carry):
            rows = rows_at(n * 128, 128)
            place = (n * 128 + lax.broadcasted_iota(jnp.int32, (128, 128), 0)).astype(F32)
            cos, sin = jnp.cos(place * scale), jnp.sin(place * scale)
            cos_table[rows, :] = cos
            sin_table[rows, :] = jnp.where(lane < ROT // 2, -sin, sin)
            return carry

        lax.fori_loop(0, length // 128, table, 0)

    def prepare_docs():
        all_docs().wait_recv()
        for s in range(members):
            for n in range(length // 128):
                cut = slice(n * 128, (n + 1) * 128)
                rows = jnp.broadcast_to(docs[s, 0:1, cut], (128, 128))
                doc_column[s, cut, :] = jnp.transpose(rows).astype(BF16)

    RT = min(512, total_rows)
    tiles = total_rows // RT
    lanes = lax.broadcasted_iota(jnp.int32, (1, 128), 1)
    first = lanes < HEAD
    low = lanes % HEAD < ROT // 2
    turning = lanes % HEAD < ROT

    def rotated(rows, places, sign):
        near = jnp.where(low, pltpu.roll(rows, 128 - ROT // 2, 1), pltpu.roll(rows, ROT // 2, 1))
        return rows * cos_table[places, :] + jnp.where(turning, sign * near * sin_table[places, :], 0.0)

    def project(k, n):
        rows = rows_at(n * RT, RT)
        places = rows_at(lax.rem(n * RT, length), RT)
        packed = dot(normed[rows, :], wa[k, :, 0:384], 1, 0) + ba[k]
        query[rows, :] = (rotated(packed[:, 0:128], places, 1.0) * (HEAD**-0.5)).astype(BF16)
        key[rows, :] = rotated(packed[:, 128:256], places, 1.0).astype(BF16)
        value[rows, :] = packed[:, 256:384].astype(BF16)

    def project_back(k, n):
        rows = rows_at(n * RT, RT)
        grad_out[rows, :] = dot(grads[rows, :], wa[k, :, 384:512], 1, 0).astype(BF16)

    def each_tile(step, k):
        def body(n, carry):
            step(k, n)
            return carry

        lax.fori_loop(0, tiles, body, 0)

    block = min(128, length // 4)
    window = length // 4 + block

    def stacked(rows):
        if hp == 1:
            return rows
        zero = jnp.zeros_like(rows)
        return jnp.concatenate([jnp.where(first, rows, zero), jnp.where(first, zero, rows)], axis=0)

    def unstacked(rows):
        if hp == 1:
            return rows
        return jnp.where(first, rows[:window], rows[window:])

    def attend(k, s):
        key_sum[...] = jnp.zeros_like(key_sum)
        value_sum[...] = jnp.zeros_like(value_sum)

        def body(n, carry):
            q_at = pl.multiple_of(n * block, block)
            k_at = pl.multiple_of(jnp.maximum(q_at - length // 4, 0), block)
            q_rows = rows_at(s * length + q_at, block)
            k_rows = pl.ds(pl.multiple_of(s * length + k_at, block), window)
            q = query[q_rows, :]
            g = grad_out[q_rows, :]
            keys, values = stacked(key[k_rows, :]), stacked(value[k_rows, :])
            scores = dot(q, keys, 1, 1)
            grad_p = dot(g, values, 1, 1)
            at = k_at + lax.broadcasted_iota(jnp.int32, (block, window), 1)
            here = q_at + lax.broadcasted_iota(jnp.int32, (block, window), 0)
            own_doc_of = doc_column[s, pl.ds(q_at, block), 0:1].astype(F32)
            same = own_doc_of == docs[s, 0:1, pl.ds(k_at, window)]
            allowed = same & (at <= here)
            probs, grad_s = [], []
            for h in range(hp):
                cut = slice(h * window, (h + 1) * window)
                sc = jnp.where(allowed, scores[:, cut], -1e30)
                expos = jnp.exp(sc - jnp.max(sc, axis=-1, keepdims=True))
                p = expos / jnp.sum(expos, axis=-1, keepdims=True)
                gp = grad_p[:, cut]
                inner = jnp.sum(p * gp, axis=-1, keepdims=True)
                probs.append(p.astype(BF16))
                grad_s.append((p * (gp - inner)).astype(BF16))
            p = jnp.concatenate(probs, axis=1) if hp > 1 else probs[0]
            gs = jnp.concatenate(grad_s, axis=1) if hp > 1 else grad_s[0]
            attended[k, q_rows, :] = dot(p, values, 1, 0).astype(BF16)
            places = pl.ds(q_at, block)
            back = rotated(dot(gs, keys, 1, 0) * (HEAD**-0.5), places, -1.0)
            grad_z[k, q_rows, 0:128] = back.astype(BF16)
            here_rows = pl.ds(k_at, window)
            key_sum[here_rows, :] += unstacked(dot(gs, q, 0, 0))
            value_sum[here_rows, :] += unstacked(dot(p, g, 0, 0))
            return carry

        lax.fori_loop(0, length // block, body, 0)
        rows = rows_at(s * length, length)
        grad_z[k, rows, 128:256] = rotated(key_sum[...], slice(None), -1.0).astype(BF16)
        grad_z[k, rows, 256:384] = value_sum[...].astype(BF16)

    def hidden(k, n):
        rows = rows_at(n * RT, RT)
        u = dot(normed[rows, :], wu[k], 1, 0) + b_up[:, rows_at(j * units + k * pw, pw)]
        phi = 0.5 * (1.0 + lax.erf(u * np.float32(0.5**0.5)))
        active[k, rows, :] = (u * phi).astype(BF16)
        slope[k, rows, :] = phi + u * (jnp.exp(-0.5 * u * u) * np.float32((2 * np.pi) ** -0.5))

    def hidden_back(k, n):
        rows = rows_at(n * RT, RT)
        grad_u[k, rows, :] = (dot(grads[rows, :], wd[k], 1, 0) * slope[k, rows, :]).astype(BF16)

    HT = min(512, length)

    def branch(a, jj):
        def body(n, carry):
            rows = rows_at(jj * length + n * HT, HT)
            total = None
            for k in range(na):
                if a == 0:
                    part = dot(attended[k, rows, :], wa[k, :, 384:512], 1, 1)
                else:
                    part = dot(grad_z[k, rows, :], wa[k, :, 0:384], 1, 1)
                total = part if total is None else total + part
            for k in range(nm):
                if a == 0:
                    part = dot(active[k, rows, :], wd[k], 1, 1)
                else:
                    part = dot(grad_u[k, rows, :], wu[k], 1, 1)
                total = total + part
            partials[a][rows, :] = total.astype(BF16)
            return carry

        lax.fori_loop(0, length // HT, body, 0)

    def half_copy(a, jj):
        at = jj - (1 - c) * gx
        return copy(
            partials[a].at[rows_at(jj * length, length)],
            core_in.at[a % nbuf, rows_at(at * length, length)],
            half_send.at[a, at],
            half_recv.at[a, at],
            partner,
        )

    def branch_give(a, jj):
        branch(a, jj)
        half_copy(a, jj).start()

    def branches(a):
        for n, jj in enumerate((far_j, partner_j)[2 - gx :]):
            branch(a, jj)
            if n == 0 and nbuf == 1 and a == second:
                pl.semaphore_wait(credit.at[0], 1)
            half_copy(a, jj).start()
        for jj in (across_j, j)[2 - gx :]:
            branch(a, jj)

    def block_rows(jj, tt):
        return rows_at((jj * nt + tt) * R, R)

    def in_rows(jj, tt):
        return rows_at(((jj - c * gx) * nt + tt) * R, R)

    def both_cores(a, jj, tt, columns=slice(None)):
        return (
            partials[a][block_rows(jj, tt), columns].astype(F32)
            + core_in[a % nbuf, in_rows(jj, tt), columns].astype(F32)
        )

    def corner_t_copy(a, tt, src):
        b = partials[a].at[block_rows(across_j, tt), back_t]
        n = step_of(src, tt)
        return copy(b, corner_t.at[a % nbuf, src], corner_t_send.at[2 + a, n], corner_t_recv.at[2 + a, n], turned(tt))

    def corner_x_copy(a, jj, tt):
        b = partials[a].at[block_rows(jj, tt), back_x]
        n = step_of(t, tt)
        return copy(b, corner_x.at[a % nbuf, tt], corner_x_send.at[2 + a, n], corner_x_recv.at[2 + a, n], across)

    def side_copy(a, jj):
        b = partials[a].at[block_rows(jj, t)]
        return copy(b, side_x.at[a % nbuf], side_send.at[2 + a], side_recv.at[2 + a], across)

    def turn_copy(a, tt, src):
        b = partials[a].at[block_rows(j, tt)]
        n = step_of(src, tt)
        return copy(b, side_t.at[a % nbuf, src], turn_send.at[2 + a, n], turn_recv.at[2 + a, n], turned(tt))

    def reduce_corner(a):
        if gx == 2:
            half_copy(a, far_j).wait_recv()
            for k in range(1, nt):
                tt = other_t(k)
                partials[a][block_rows(across_j, tt), :] = both_cores(a, across_j, tt).astype(BF16)
                corner_t_copy(a, tt, t).start()
                corner_x_copy(a, across_j, tt).start()

    def reduce_side(a):
        if gx == 2:
            total = both_cores(a, across_j, t, back_t)
            for k in range(1, nt):
                corner_t_copy(a, t, other_t(k)).wait_recv()
                total = total + corner_t[a % nbuf, other_t(k)].astype(F32)
            partials[a][block_rows(across_j, t), back_t] = total.astype(BF16)
            partials[a][block_rows(across_j, t), back_x] = both_cores(a, across_j, t, back_x).astype(BF16)
            side_copy(a, across_j).start()

    def reduce_turn(a):
        if nbuf == 1 and a == second and nt > 1:
            pl.semaphore_wait(credit.at[1], nt - 1)
        half_copy(a, partner_j).wait_recv()
        for k in range(1, nt):
            tt = other_t(k)
            if gx == 2:
                corner_x_copy(a, j, tt).wait_recv()
                total = both_cores(a, j, tt, back_x) + corner_x[a % nbuf, tt].astype(F32)
                partials[a][block_rows(j, tt), back_x] = total.astype(BF16)
                partials[a][block_rows(j, tt), back_t] = both_cores(a, j, tt, back_t).astype(BF16)
            else:
                partials[a][block_rows(j, tt), :] = both_cores(a, j, tt).astype(BF16)
            turn_copy(a, tt, t).start()

    def reduce_wait(a):
        if gx == 2:
            side_copy(a, across_j).wait_recv()
        for k in range(1, nt):
            turn_copy(a, t, other_t(k)).wait_recv()

    def reduced(a, n):
        mine = rows_at((j * nt + t) * R + n * tile, tile)
        came = rows_at(((j - c * gx) * nt + t) * R + n * tile, tile)
        rows = rows_at(n * tile, tile)
        total = partials[a][mine, :].astype(F32) + core_in[a % nbuf, came, :].astype(F32)
        if gx == 2:
            total = total + side_x[a % nbuf, rows, :].astype(F32)
        for k in range(1, nt):
            total = total + side_t[a % nbuf, other_t(k), rows, :].astype(F32)
        return restore(total)

    def reduce_sent(a):
        for xx in range(gx):
            half_copy(a, (1 - c) * gx + xx).wait_send()
        if gx == 2:
            side_copy(a, across_j).wait_send()
        for k in range(1, nt):
            tt = other_t(k)
            turn_copy(a, tt, t).wait_send()
            if gx == 2:
                corner_t_copy(a, tt, t).wait_send()
                corner_x_copy(a, across_j, tt).wait_send()

    def free_buffers():
        if nbuf == 1:
            pl.semaphore_signal(credit.at[0], inc=1, device_id=partner, device_id_type=MESH)
            for k in range(1, nt):
                pl.semaphore_signal(credit.at[1], inc=1, device_id=turned(other_t(k)), device_id_type=MESH)

    def write_output():
        def body(n, carry):
            rows = rows_at(n * tile, tile)
            total = tokens[rows, :].astype(F32) + reduced(0, n) + b_dense[...] + b_down[...]
            output[rows, :] = total.astype(BF16)
            return carry

        lax.fori_loop(0, R // tile, body, 0)
        result(0).start()

    def put(row, at, values):
        end = at + values.shape[1]
        for h in range(2):
            lo, hi = max(at, h * D // 2), min(end, (h + 1) * D // 2)
            if lo < hi:
                cols = slice(lo - h * D // 2, hi - h * D // 2)
                vec[2 * row + h : 2 * row + h + 1, cols] += values[:, lo - at : hi - at]

    def taken(array, row):
        return jnp.concatenate([array[2 * row : 2 * row + 1], array[2 * row + 1 : 2 * row + 2]], axis=1)

    def sum_biases():
        vec[...] = jnp.zeros_like(vec)
        for k in range(nm):
            put(3, k * pw, jnp.sum(grad_u[k].astype(F32), axis=0, keepdims=True))
        for k in range(na):
            put(3, units + k * 384, jnp.sum(grad_z[k].astype(F32), axis=0, keepdims=True))

    def write_input_grad():
        def body(n, carry):
            rows = rows_at(n * tile, tile)
            normal, inverse = normalize(tokens[rows, :].astype(F32))
            up = cotangent[rows, :].astype(F32)
            grad = reduced(1, n)
            put(0, 0, jnp.sum(grad * normal, axis=0, keepdims=True))
            put(1, 0, jnp.sum(grad, axis=0, keepdims=True))
            put(2, 0, jnp.sum(up, axis=0, keepdims=True))
            scaled = grad * gain[...]
            input_grad[rows, :] = up + inverse * (
                scaled
                - jnp.mean(scaled, axis=-1, keepdims=True)
                - normal * jnp.mean(scaled * normal, axis=-1, keepdims=True)
            )
            return carry

        lax.fori_loop(0, R // tile, body, 0)
        result(1).start()

    peers = nz if gx == 2 else 2 * nz
    mates = members * nt
    peer = z if gx == 2 else z * 2 + x
    mate = j * nt + t

    def peer_copy(to, src):
        device_to = device(to, x, c, t) if gx == 2 else device(to // 2, to % 2, c, t)
        return copy(vec_z.at[peer], vec_z.at[src], peer_send.at[0], peer_recv.at[0], device_to)

    def mate_copy(to, src):
        jj, tt = to // nt, to % nt
        device_to = device(z, jj % 2, jj // 2, tt) if gx == 2 else device(z, x, jj, tt)
        return copy(vec_m.at[mate], vec_m.at[src], mate_send.at[0], mate_recv.at[0], device_to)

    def all_peers():
        rows = vec_z.at[pl.ds(0, peers - 1)]
        return copy(rows, rows, peer_send.at[0], peer_recv.at[0], partner)

    def all_mates():
        rows = vec_m.at[pl.ds(0, mates - 1)]
        return copy(rows, rows, mate_send.at[0], mate_recv.at[0], partner)

    def sums_start():
        vec_z[peer] = vec[...]
        for k in range(1, peers):
            peer_copy(lax.rem(peer + k, peers), peer).start()

    def sums_group():
        all_peers().wait_recv()
        total = vec_z[0]
        for k in range(1, peers):
            total = total + vec_z[k]
        vec_m[mate] = total
        for k in range(1, mates):
            mate_copy(lax.rem(mate + k, mates), mate).start()

    def sums_end():
        all_mates().wait_recv()
        total = vec_m[0]
        for k in range(1, mates):
            total = total + vec_m[k]
        gain_grad[...] = taken(total, 0)
        shift_grad[...] = taken(total, 1)
        dense_bias[...] = taken(total, 2)
        for jj in range(members):
            row = taken(vec_m[jj * nt + t], 3)
            up_bias[:, jj * units : (jj + 1) * units] = row[:, :units]
            for k in range(na):
                part = row[:, units + k * 384 : units + (k + 1) * 384]
                heads = [part[:, p * 128 + h * HEAD : p * 128 + (h + 1) * HEAD] for h in range(hp) for p in range(3)]
                at = (jj * na + k) * wide
                qkv_bias[:, 3 * at : 3 * (at + wide)] = jnp.concatenate(heads, axis=1)

    def sums_sent():
        all_peers().wait_send()
        all_mates().wait_send()

    def forwards(some, lo, hi):
        for d in range(lo, hi):
            for i in some:
                forward_up(i, d)
                forward_down(i, d)

    def chains(some, lo, hi):
        for n in range(lo, hi):
            for i in some:
                chain_up(i, n)
                chain_down(i, n)

    second = 0 if gx == 2 else 1

    def any_order():
        stage()
        fill_normed()
        enter()
        for i in U + A + Dn:
            send_first(i)
            share(i)
        give_docs()
        act_start(0)
        fill_grads()
        act_start(1)
        for i in U + A:
            send_own(i)
        prepare()
        prepare_docs()
        forwards(U + A, 1, 2)
        act_from_turn(0)
        act_from_side(0)
        for i in Dn:
            send_own(i)
        forwards(U, 2, nz)
        act_finish(0)
        act_wait(0)
        for i in U:
            gathered(i)
            each_tile(hidden, i - na)
        act_from_turn(1)
        act_from_side(1)
        forwards(A, 2, nz)
        forwards(Dn, 1, nz)
        act_finish(1)
        act_wait(1)
        for i in Dn:
            weight_grad(i)
            sum_x(i)
        chains(Dn, 0, nz - 1)
        for i in A:
            gathered(i)
            each_tile(project, i)
            each_tile(project_back, i)
            for s in range(members):
                attend(i, s)
            weight_grad(i)
            sum_x(i)
        chains(A, 0, nz - 1)
        for i in Dn:
            gathered(i)
            each_tile(hidden_back, i - na - nm)
        for i in U:
            weight_grad(i)
            sum_x(i)
        act_sent(0)
        act_sent(1)
        sum_biases()
        for a in (1, 0) if gx == 2 else (0, 1):
            branches(a)
            reduce_corner(a)
            if a != second:
                chains(U, 0, nz - 1)
            reduce_side(a)
            reduce_turn(a)
            if a != second:
                for i in Dn + A:
                    chain_end(i)
            reduce_wait(a)
            if a == 0:
                write_output()
            else:
                write_input_grad()
                sums_start()
            if a != second:
                free_buffers()
        for i in U:
            chain_end(i)
        sums_group()
        for i in Dn + A + U:
            finish(i)
        sums_end()

    def tuned_order():
        (a,), (u,), (d,) = A, U, Dn
        stage()
        enter()
        share(a)
        give_docs()
        send_first(d)
        fill_normed()
        send_first(u)
        share(u)
        prepare()
        send_first(a)
        fill_grads()
        act_start_turn(0)
        send_own(a)
        act_start_side(0)
        act_start_side(1)
        act_start_turn(1)
        send_own(u)
        forward_up(a, 1)
        share(d)
        forward_down(a, 1)
        forward_down(u, 1)
        forward_down(a, 2)
        forward_up(u, 1)
        prepare_docs()
        forward_up(a, 2)
        act_from_turn(0)
        act_from_side(0)
        act_wait_of(0, partner_j)
        forward_down(u, 2)
        forward_up(u, 2)
        forward_up(a, 3)
        forward_down(a, 3)
        act_from_side(1)
        act_from_turn(1)
        project(0, partner_j)
        send_own(d)
        project_back(0, j)
        project(0, j)
        attend(0, j)
        act_wait_of(1, partner_j)
        act_finish(0)
        forward_down(u, 3)
        forward_up(u, 3)
        hidden(0, across_j)
        hidden(0, j)
        act_wait_of(0, far_j)
        hidden(0, partner_j)
        hidden(0, far_j)
        act_finish(1)
        forward_up(d, 1)
        forward_down(d, 1)
        project(0, across_j)
        project(0, far_j)
        act_wait_of(1, far_j)
        weight_grad_cut(d, 0)
        chain_down(d, 0)
        weight_grad_cut(d, 1)
        chain_up(d, 0)
        project_back(0, far_j)
        attend(0, far_j)
        project_back(0, across_j)
        forward_up(d, 2)
        forward_down(d, 2)
        attend(0, across_j)
        chain_down(d, 1)
        project_back(0, partner_j)
        chain_up(d, 1)
        attend(0, partner_j)
        forward_down(d, 3)
        forward_up(d, 3)
        hidden_back(0, far_j)
        branch_give(1, far_j)
        hidden_back(0, across_j)
        chain_down(d, 2)
        chain_up(d, 2)
        branch(1, across_j)
        reduce_corner(1)
        weight_grad_cut(a, 0)
        weight_grad_cut(a, 1)
        chain_down(a, 0)
        chain_up(a, 0)
        act_sent(0)
        act_sent(1)
        branch_give(0, far_j)
        hidden_back(0, j)
        hidden_back(0, partner_j)
        branch(0, across_j)
        weight_grad_cut(u, 0)
        reduce_corner(0)
        chain_down(u, 0)
        weight_grad_cut(u, 1)
        chain_up(u, 0)
        sum_biases()
        chain_end(d)
        chain_up(a, 1)
        reduce_side(1)
        branch(1, j)
        branch_give(1, partner_j)
        chain_down(a, 1)
        branch(0, j)
        reduce_turn(1)
        branch_give(0, partner_j)
        chain_up(u, 1)
        chain_down(u, 1)
        finish(d)
        reduce_side(0)
        reduce_turn(0)
        chain_up(a, 2)
        chain_down(a, 2)
        reduce_wait(1)
        write_input_grad()
        sums_start()
        chain_down(u, 2)
        chain_up(u, 2)
        chain_end(a)
        sums_group()
        chain_end(u)
        sums_end()
        reduce_wait(0)
        write_output()
        finish(a)
        finish(u)

    if (gx, na, nm, nz, tiles, RT) == (2, 1, 1, 4, 4, length):
        tuned_order()
    else:
        any_order()

    for i in range(count):
        all_given(i).wait_send()
        all_parts(i).wait_send()
        for n in range(1, nz):
            blocks = weights(i).at[pl.ds(0, n * zb)]
            pl.when(z == n - 1)(
                lambda: copy(blocks, blocks, up_send.at[i], z_recv.at[i, 0], along(z + 1)).wait_send()
            )
            pl.when(z == nz - n)(
                lambda: copy(blocks, blocks, down_send.at[i], z_recv.at[i, 0], along(z - 1)).wait_send()
            )
        sums = of(zs_a, zs_u, zs_d, i).at[pl.ds(0, (nz - 1) * zb)]
        copy(sums, sums, g_send.at[i], g_recv.at[i, 0], partner).wait_send()
        if gx == 1:
            for src in range(nz):
                send_across(i, src, x).wait_send()
                g_across(i, src).wait_send()
    all_docs().wait_send()
    reduce_sent(0)
    reduce_sent(1)
    sums_sent()
    for n in range(len(results)):
        result(n).wait()


def hand_out(arrays):
    wide = [n for n, array in enumerate(arrays) if array.shape[0] > 1]
    thin = [n for n, array in enumerate(arrays) if array.shape[0] == 1]

    def body(*refs):
        count = len(arrays)
        given, taken, buffers, sems = refs[:count], refs[count : 2 * count], refs[2 * count : -1], refs[-1]
        reads = [pltpu.make_async_copy(given[n], buffers[i], sems.at[0, i]) for i, n in enumerate(wide)]
        writes = [pltpu.make_async_copy(buffers[i], taken[n], sems.at[1, i]) for i, n in enumerate(wide)]
        for read in reads:
            read.start()
        for n in thin:
            taken[n][...] = given[n][0]
        for read, write in zip(reads, writes):
            read.wait()
            write.start()
        for write in writes:
            write.wait()

    def specs():
        return [pl.BlockSpec(memory_space=pltpu.VMEM if n in thin else pl.ANY) for n in range(len(arrays))]

    return list(
        pl.pallas_call(
            body,
            out_shape=[
                jax.ShapeDtypeStruct(array.shape[1:] if n in thin else array.shape, array.dtype)
                for n, array in enumerate(arrays)
            ],
            in_specs=specs(),
            out_specs=specs(),
            scratch_shapes=[pltpu.VMEM(arrays[n].shape, arrays[n].dtype) for n in wide]
            + [pltpu.SemaphoreType.DMA((2, len(wide)))],
            name="hand_out",
        )(*arrays)
    )


def on_device(
    nt,
    n_dp,
    tokens,
    cotangent,
    segments,
    ln_gain,
    ln_bias,
    w_qkv,
    b_qkv,
    w_dense,
    b_dense,
    w_up,
    b_up,
    w_down,
    b_down,
):
    R, D = tokens.shape
    length = segments.shape[1]
    r = w_qkv.shape[0]
    nz = n_dp // 4
    heads = w_qkv.shape[1] // (3 * HEAD)
    gx = 2 if heads % 4 == 0 and 4 * length * D <= 1 << 21 else 1
    members = 2 * gx
    heads = heads // members
    hp = 2 if heads % 2 == 0 else 1
    na = heads // hp
    units = w_up.shape[1] // members
    pw = 512 if units % 512 == 0 else units
    nm = units // pw
    nbuf = gx
    peers, mates, steps = (nz if gx == 2 else 2 * nz), members * nt, max(nt - 1, 1)
    sizes = dict(nt=nt, nz=nz, gx=gx, na=na, nm=nm, hp=hp, length=length, R=R, r=r, pw=pw, nbuf=nbuf)

    widths = ((na, 512), (nm, pw), (nm, pw))
    count = na + 2 * nm
    rows = members * length
    own = D if gx == 2 else D // 2
    chip = 2 * r
    split = D // 4
    V = pltpu.VMEM
    DMA = pltpu.SemaphoreType.DMA

    def some(shape):
        return V(shape if gx == 2 else (1, 1, 8, 128)[-len(shape) :], BF16)

    scratch = (
        [V((members, na, r, 512), BF16), V((na, 1, 384), F32)]
        + [V((length, 128), F32)] * 2
        + [V((members, 8, length), F32), V((members, length, 128), BF16)]
        + [V((n, D, w), BF16) for n, w in widths]
        + [V((rows, D), BF16), V((rows, D), BF16)]
        + [V((rows, 128), BF16)] * 4
        + [V((na, rows, 128), BF16), V((na, rows, 384), BF16)]
        + [V((length, 128), F32)] * 2
        + [V((nm, rows, pw), BF16), V((nm, rows, pw), F32), V((nm, rows, pw), BF16)]
        + [V((rows, D) if gx == 2 else (8, 128), BF16)]
        + [V((nbuf, gx * length, D), BF16), some((nbuf, nt, R, split)), some((nbuf, nt, R, D - split))]
        + [some((nbuf, R, D)), V((nbuf, nt, R, D), BF16)]
        + [V((n, own, w), F32) for n, w in widths]
        + [V((n, own, w) if gx == 1 else (n, 8, 128), BF16) for _ in range(2) for n, w in widths]
        + [V((n, own, w), BF16) for _ in range(3) for n, w in widths]
        + [V((n, gx * chip, w), BF16) for n, w in widths]
        + [V((n, members, r, w), BF16) for n, w in widths]
        + [V((8, D // 2), F32), V((peers, 8, D // 2), F32), V((mates, 8, D // 2), F32)]
        + [DMA((count,)), DMA((10,)), DMA((count + 1,)), DMA((count + 1,))]
        + [DMA((count,)), DMA((count,)), DMA((count, nz))]
        + [DMA((count, nz) if gx == 1 else (1, 1))] * 2
        + [DMA((4, steps))] * 2
        + [DMA((4,))] * 2
        + [DMA((4, steps))] * 4
        + [DMA((2, gx, nt))] * 2
        + [DMA((count, nz) if gx == 1 else (1, 1))] * 2
        + [DMA((count,)), DMA((count, nz + 1))]
        + [DMA((count,))] * 2
        + [DMA((2, gx))] * 2
        + [DMA((1,))] * 4
        + [pltpu.SemaphoreType.REGULAR((2,))]
    )
    space, far = pl.BlockSpec(memory_space=pltpu.VMEM), pl.BlockSpec(memory_space=pl.ANY)

    def row(vector):
        return vector.reshape(1, -1)

    args = (
        tokens,
        cotangent,
        segments,
        row(ln_gain),
        row(ln_bias),
        w_qkv,
        b_qkv,
        w_dense.T,
        row(b_dense),
        w_up,
        row(b_up),
        w_down.T,
        row(b_down),
    )
    shapes = (
        jax.ShapeDtypeStruct((R, D), BF16),
        jax.ShapeDtypeStruct((R, D), F32),
        jax.ShapeDtypeStruct((1, D), F32),
        jax.ShapeDtypeStruct((1, D), F32),
        jax.ShapeDtypeStruct(w_qkv.shape, F32),
        jax.ShapeDtypeStruct((1, w_qkv.shape[1]), F32),
        jax.ShapeDtypeStruct(w_dense.shape[::-1], F32),
        jax.ShapeDtypeStruct((1, D), F32),
        jax.ShapeDtypeStruct(w_up.shape, F32),
        jax.ShapeDtypeStruct((1, w_up.shape[1]), F32),
        jax.ShapeDtypeStruct(w_down.shape[::-1], F32),
    )
    out = pl.pallas_call(
        functools.partial(kernel, sizes),
        out_shape=shapes,
        in_specs=[far if n in (0, 1, 5, 7, 9, 11) else space for n in range(len(args))],
        out_specs=[space if n in (2, 3, 5, 7, 9) else far for n in range(len(shapes))],
        scratch_shapes=[V(args[n].shape, BF16) for n in (0, 1, 5, 7)]
        + [V(shapes[n].shape, shapes[n].dtype) for n in (0, 1, 4, 6, 8, 10)]
        + scratch,
        compiler_params=pltpu.CompilerParams(
            collective_id=0, has_side_effects=True, vmem_limit_bytes=67043328
        ),
        name="layer",
    )(*args)
    out = hand_out((*out, out[7]))
    out[6], out[10] = out[6].T, out[10].T
    return tuple(out)


def solution(mesh):
    return jax.shard_map(
        functools.partial(on_device, mesh.shape["tensor"], mesh.shape["dp"]),
        mesh=mesh,
        in_specs=(
            P(("dp", "tensor"), None),
            P(("dp", "tensor"), None),
            P("dp", None),
            P(),
            P(),
            P("dp", "tensor"),
            P("tensor"),
            P("tensor", "dp"),
            P(),
            P("dp", "tensor"),
            P("tensor"),
            P("tensor", "dp"),
            P(),
        ),
        out_specs=(
            P(("dp", "tensor"), None),
            P(("dp", "tensor"), None),
            P(),
            P(),
            P("dp", "tensor"),
            P("tensor"),
            P("tensor", "dp"),
            P(),
            P("dp", "tensor"),
            P("tensor"),
            P("tensor", "dp"),
            P(),
        ),
        check_vma=False,
    )
```

```python
import functools

import jax
import jax.numpy as jnp
import numpy as np
from jax import lax
from jax.experimental import pallas as pl
from jax.experimental.pallas import tpu as pltpu
from jax.sharding import PartitionSpec as P

HEAD = 64
ROT = 16
NORM_EPS = 1e-05
ROTARY_BASE = 10000.0
MESH = pl.DeviceIdType.MESH
F32 = jnp.float32
BF16 = jnp.bfloat16


def dot(left, right, over_left, over_right):
    return lax.dot_general(
        left, right, (((over_left,), (over_right,)), ((), ())), preferred_element_type=F32
    )


def normalize(rows):
    centred = rows - jnp.mean(rows, axis=-1, keepdims=True)
    inverse = lax.rsqrt(jnp.mean(centred * centred, axis=-1, keepdims=True) + NORM_EPS)
    return centred * inverse, inverse


def padded(array):
    rest = -array.shape[1] % 128
    return jnp.concatenate([array, jnp.zeros((array.shape[0], rest), array.dtype)], axis=1) if rest else array


def kernel(
    sizes,
    tokens_hbm,
    cotangent_hbm,
    segments_hbm,
    gain_hbm,
    shift_hbm,
    w_qkv_hbm,
    b_qkv_hbm,
    w_dense_hbm,
    b_dense_hbm,
    w_up,
    b_up_hbm,
    w_down,
    b_down_hbm,
    output_hbm,
    input_grad_hbm,
    gain_grad_hbm,
    shift_grad_hbm,
    qkv_grad_hbm,
    qkv_bias_hbm,
    dense_grad_hbm,
    dense_bias_hbm,
    up_grad_hbm,
    up_bias_hbm,
    down_grad_hbm,
    tokens,
    cotangent,
    segments,
    gain,
    shift,
    w_qkv,
    b_qkv,
    w_dense,
    b_dense,
    b_up,
    b_down,
    output,
    input_grad,
    gain_grad,
    shift_grad,
    qkv_grad,
    qkv_bias,
    dense_grad,
    dense_bias,
    up_grad,
    up_bias,
    down_grad,
    wa_in,
    ba,
    cos_table,
    sin_table,
    docs,
    doc_column,
    wa,
    wu,
    wd,
    normed,
    grads,
    query,
    key,
    value,
    grad_out,
    attended,
    grad_z,
    key_sum,
    value_sum,
    active,
    slope,
    grad_u,
    late,
    core_in,
    corner_x,
    corner_t,
    side_x,
    side_t,
    own_a,
    own_u,
    own_d,
    xs_a,
    xs_u,
    xs_d,
    xr_a,
    xr_u,
    xr_d,
    zs_a,
    zs_u,
    zs_d,
    zu_a,
    zu_u,
    zu_d,
    zd_a,
    zd_u,
    zd_d,
    fs_a,
    fs_u,
    fs_d,
    fr_a,
    fr_u,
    fr_d,
    vec,
    vec_z,
    vec_m,
    local_sem,
    io_sem,
    share_send,
    share_recv,
    up_send,
    down_send,
    z_recv,
    x_send,
    x_recv,
    turn_send,
    turn_recv,
    side_send,
    side_recv,
    corner_x_send,
    corner_x_recv,
    corner_t_send,
    corner_t_recv,
    pass_send,
    pass_recv,
    gx_send,
    gx_recv,
    g_send,
    g_recv,
    fin_send,
    fin_recv,
    half_send,
    half_recv,
    peer_send,
    peer_recv,
    mate_send,
    mate_recv,
    credit,
):
    nt, nz, gx, na, nm, hp, length, R, r, pw, nbuf = (
        sizes[k] for k in ("nt", "nz", "gx", "na", "nm", "hp", "length", "R", "r", "pw", "nbuf")
    )
    D = tokens.shape[1]
    chip = 2 * r
    zb = gx * chip
    own = D if gx == 2 else D // 2
    members = 2 * gx
    wide = hp * HEAD
    units = nm * pw
    total_rows = members * length
    partials = (grads, late if gx == 2 else normed)
    dp, t = lax.axis_index("dp"), lax.axis_index("tensor")
    z, x, c = dp // 4, (dp // 2) % 2, dp % 2
    j = c * gx + x if gx == 2 else c

    def device(zz, xx, cc, tt):
        return (zz * 4 + xx * 2 + cc, tt)

    partner = device(z, x, 1 - c, t)
    across = device(z, 1 - x, c, t)

    def member(jj):
        return device(z, jj % 2, jj // 2, t) if gx == 2 else device(z, x, jj, t)

    def along(zz):
        return device(zz, x, c, t)

    def turned(tt):
        return device(z, x, c, tt)

    def other_j(k):
        return lax.rem(j + k, members)

    def other_z(k):
        return lax.rem(z + k, nz)

    def other_t(k):
        return lax.rem(t + k, nt)

    def step_of(src, tt):
        return lax.rem(tt - src + nt, nt) - 1

    def rows_at(start, size):
        return pl.ds(pl.multiple_of(start, size), size)

    def copy(src, dst, send, recv, to):
        return pltpu.make_async_remote_copy(
            src_ref=src, dst_ref=dst, send_sem=send, recv_sem=recv, device_id=to, device_id_type=MESH
        )

    A = list(range(na))
    U = list(range(na, na + nm))
    Dn = list(range(na + nm, na + 2 * nm))
    count = na + 2 * nm

    def of(a, u, d, i):
        if i in A:
            return a.at[i]
        return u.at[i - na] if i in U else d.at[i - na - nm]

    def weights(i):
        return of(wa, wu, wd, i)

    def z_rows(zz):
        return rows_at(zz * zb if gx == 2 else (x * nz + zz) * chip, zb)

    own_rows = rows_at(z * zb + (x * 2 + c) * r if gx == 2 else (x * nz + z) * chip + c * r, r)

    barrier = pltpu.get_barrier_semaphore()
    greeted = [member(other_j(k)) for k in range(1, members)] + ([] if gx == 2 else [across])
    greeted += [
        device(z, jj % 2 if gx == 2 else x, jj // 2 if gx == 2 else jj, other_t(k))
        for k in range(1, nt)
        for jj in [other_j(n) for n in range(members)]
    ]

    def greet(other):
        pl.semaphore_signal(barrier, inc=1, device_id=other, device_id_type=MESH)

    for other in greeted:
        greet(other)
    pl.when(z > 0)(lambda: greet(along(z - 1)))
    pl.when(z < nz - 1)(lambda: greet(along(z + 1)))

    reads = [
        pltpu.make_async_copy(src, dst, io_sem.at[n])
        for n, (src, dst) in enumerate(
            (
                (segments_hbm, segments),
                (gain_hbm, gain),
                (shift_hbm, shift),
                (b_qkv_hbm, b_qkv),
                (b_dense_hbm, b_dense),
                (b_up_hbm, b_up),
                (b_down_hbm, b_down),
                (w_qkv_hbm, w_qkv),
                (w_dense_hbm, w_dense),
                (tokens_hbm, tokens),
                (cotangent_hbm, cotangent),
            )
        )
    ]
    for read in reads:
        read.start()

    def enter():
        pl.semaphore_wait(barrier, len(greeted) + jnp.minimum(z, 1) + jnp.minimum(nz - 1 - z, 1))

    results = (
        (output, output_hbm),
        (input_grad, input_grad_hbm),
        (qkv_grad, qkv_grad_hbm),
        (dense_grad, dense_grad_hbm),
        (up_grad, up_grad_hbm),
        (down_grad, down_grad_hbm),
        (gain_grad, gain_grad_hbm),
        (shift_grad, shift_grad_hbm),
        (qkv_bias, qkv_bias_hbm),
        (dense_bias, dense_bias_hbm),
        (up_bias, up_bias_hbm),
    )

    def result(n):
        return pltpu.make_async_copy(*results[n], io_sem.at[11 + n])

    def part_of(i, jj):
        if i in A:
            return wa_in.at[jj, i]
        ref, k = (w_up, i - na) if i in U else (w_down, i - na - nm)
        return ref.at[:, rows_at(jj * units + k * pw, pw)]

    def local_copy(i):
        return pltpu.make_async_copy(part_of(i, j), weights(i).at[own_rows], local_sem.at[i])

    def give_part(i, jj):
        dst = weights(i).at[own_rows]
        return copy(part_of(i, jj), dst, share_send.at[i], share_recv.at[i], member(jj))

    def all_parts(i):
        rows = weights(i).at[pl.ds(0, (members - 1) * r)]
        return copy(rows, rows, share_send.at[i], share_recv.at[i], partner)

    def member_rows(jj):
        return rows_at(z * zb + (jj % 2 * 2 + jj // 2) * r if gx == 2 else (x * nz + z) * chip + jj * r, r)

    def share(i):
        local_copy(i).start()
        for k in range(1, members):
            give_part(i, other_j(k)).start()

    def head_part(array, jj, k, part):
        at = [((jj * na + k) * hp + h) * 3 * HEAD + part * HEAD for h in range(hp)]
        return padded(jnp.concatenate([array[:, a : a + HEAD] for a in at], axis=1))

    def own_doc(jj):
        return copy(docs.at[j], docs.at[j], share_send.at[count], share_recv.at[count], member(jj))

    def all_docs():
        rows = docs.at[pl.ds(0, members - 1)]
        return copy(rows, rows, share_send.at[count], share_recv.at[count], partner)

    def stage():
        for read in reads[:9]:
            read.wait()
        for jj in range(members):
            for k in range(na):
                for part in range(3):
                    wa_in[jj, k, :, part * 128 : (part + 1) * 128] = head_part(w_qkv[...], jj, k, part)
                at = (jj * na + k) * wide
                wa_in[jj, k, :, 384:512] = padded(w_dense[:, at : at + wide])
        docs[j] = jnp.broadcast_to(segments[...].astype(F32), docs.shape[1:])

    def give_docs():
        for k in range(1, members):
            own_doc(other_j(k)).start()

    def permute(rows):
        if gx == 2:
            return rows
        return jnp.concatenate(
            [rows[:, (zz * 2 + xx) * chip : (zz * 2 + xx + 1) * chip] for xx in range(2) for zz in range(nz)],
            axis=1,
        )

    def restore(rows):
        if gx == 2:
            return rows
        return jnp.concatenate(
            [rows[:, (xx * nz + zz) * chip : (xx * nz + zz + 1) * chip] for zz in range(nz) for xx in range(2)],
            axis=1,
        )

    acts = (normed, grads)
    tile = min(64, R)
    split = D * 3 // 8
    over_x, over_t = slice(0, split), slice(split, D)
    back_split = D // 4
    back_x, back_t = slice(0, back_split), slice(back_split, D)

    def act_rows(jj, tt):
        return rows_at((jj * nt + tt) * R, R)

    across_j = c * gx + 1 - x if gx == 2 else c
    partner_j = (1 - c) * gx + x if gx == 2 else 1 - c
    far_j = (1 - c) * gx + 1 - x if gx == 2 else 1 - c
    near = (j, partner_j, across_j, far_j)

    def fill_normed():
        reads[9].wait()

        def body(n, carry):
            rows = rows_at(n * tile, tile)
            normal, _ = normalize(tokens[rows, :].astype(F32))
            normed[rows_at((j * nt + t) * R + n * tile, tile), :] = permute(
                (normal * gain[...] + shift[...]).astype(BF16)
            )
            return carry

        lax.fori_loop(0, R // tile, body, 0)

    def fill_grads():
        reads[10].wait()

        def body(n, carry):
            grads[rows_at((j * nt + t) * R + n * tile, tile), :] = permute(cotangent[rows_at(n * tile, tile), :])
            return carry

        lax.fori_loop(0, R // tile, body, 0)

    def act_turn(a, tt, src):
        b = acts[a].at[act_rows(j, src)]
        return copy(b, b, turn_send.at[a, step_of(src, tt)], turn_recv.at[a, step_of(src, tt)], turned(tt))

    def act_side(a, jj):
        b = acts[a].at[act_rows(jj, t)]
        return copy(b, b, side_send.at[a], side_recv.at[a], across)

    def act_corner_x(a, jj, tt):
        b = acts[a].at[act_rows(jj, tt), over_x]
        return copy(b, b, corner_x_send.at[a, step_of(t, tt)], corner_x_recv.at[a, step_of(t, tt)], across)

    def act_corner_t(a, tt, src):
        b = acts[a].at[act_rows(across_j, src), over_t]
        return copy(b, b, corner_t_send.at[a, step_of(src, tt)], corner_t_recv.at[a, step_of(src, tt)], turned(tt))

    def act_pass(a, jj, tt):
        b = acts[a].at[act_rows(jj, tt)]
        return copy(b, b, pass_send.at[a, jj % gx, tt], pass_recv.at[a, jj % gx, tt], partner)

    def act_start_side(a):
        if gx == 2:
            act_side(a, j).start()

    def act_start_turn(a):
        for k in range(1, nt):
            act_turn(a, other_t(k), t).start()
        act_pass(a, j, t).start()

    def act_start(a):
        act_start_side(a)
        act_start_turn(a)

    def act_from_turn(a):
        for k in range(1, nt):
            src = other_t(k)
            act_turn(a, t, src).wait_recv()
            if gx == 2:
                act_corner_x(a, j, src).start()
            act_pass(a, j, src).start()

    def act_from_side(a):
        if gx == 2:
            act_side(a, across_j).wait_recv()
            for k in range(1, nt):
                act_corner_t(a, other_t(k), t).start()
            act_pass(a, across_j, t).start()

    def act_finish(a):
        if gx == 2:
            for k in range(1, nt):
                src = other_t(k)
                act_corner_x(a, across_j, src).wait_recv()
                act_corner_t(a, t, src).wait_recv()
                act_pass(a, across_j, src).start()

    def act_wait_of(a, jj):
        for k in range(nt):
            act_pass(a, jj, k).wait_recv()

    def act_wait(a):
        for xx in range(gx):
            act_wait_of(a, (1 - c) * gx + xx)

    def act_sent(a):
        if gx == 2:
            act_side(a, j).wait_send()
        for k in range(1, nt):
            act_turn(a, other_t(k), t).wait_send()
            if gx == 2:
                act_corner_x(a, j, other_t(k)).wait_send()
                act_corner_t(a, other_t(k), t).wait_send()
        for xx in range(gx):
            for k in range(nt):
                act_pass(a, c * gx + xx, k).wait_send()

    def w_block(i, zz):
        return weights(i).at[z_rows(zz)]

    def send_up(i, src):
        b = w_block(i, src)
        return copy(b, b, up_send.at[i], z_recv.at[i, src], along(z + 1))

    def send_down(i, src):
        b = w_block(i, src)
        return copy(b, b, down_send.at[i], z_recv.at[i, src], along(z - 1))

    def send_across(i, src, xx):
        b = weights(i).at[rows_at((xx * nz + src) * chip, chip)]
        return copy(b, b, x_send.at[i, src], x_recv.at[i, src], across)

    def send_first(i):
        def along_z(sems, to):
            return copy(part_of(i, j), weights(i).at[own_rows], sems.at[i], z_recv.at[i, z], to)

        pl.when(z < nz - 1)(lambda: along_z(up_send, along(z + 1)).start())
        pl.when(z > 0)(lambda: along_z(down_send, along(z - 1)).start())

    def send_own(i):
        local_copy(i).wait()
        all_parts(i).wait_recv()
        for k in range(1, members):
            jj = other_j(k)
            rows = weights(i).at[member_rows(jj)]

            def along_z(sems, to):
                return copy(rows, rows, sems.at[i], z_recv.at[i, z], to)

            pl.when(z < nz - 1)(lambda: along_z(up_send, along(z + 1)).start())
            pl.when(z > 0)(lambda: along_z(down_send, along(z - 1)).start())
        if gx == 1:
            send_across(i, z, x).start()

    def forward_up(i, d):
        @pl.when(z >= d)
        def _():
            send_up(i, z - d).wait_recv()
            pl.when(z < nz - 1)(lambda: send_up(i, z - d).start())
            if gx == 1:
                send_across(i, z - d, x).start()

    def forward_down(i, d):
        @pl.when(z + d <= nz - 1)
        def _():
            send_down(i, z + d).wait_recv()
            pl.when(z > 0)(lambda: send_down(i, z + d).start())
            if gx == 1:
                send_across(i, z + d, x).start()

    def gathered(i):
        if gx == 1:
            for src in range(nz):
                send_across(i, src, 1 - x).wait_recv()

    def own_of(i):
        return of(own_a, own_u, own_d, i)

    def g_across(i, to_z):
        b = pl.ds(to_z * chip, chip)
        return copy(
            of(xs_a, xs_u, xs_d, i).at[b],
            of(xr_a, xr_u, xr_d, i).at[b],
            gx_send.at[i, to_z],
            gx_recv.at[i, to_z],
            across,
        )

    def g_up(i, to_z):
        b = rows_at(to_z * zb, zb)
        return copy(
            of(zs_a, zs_u, zs_d, i).at[b],
            of(zu_a, zu_u, zu_d, i).at[b],
            g_send.at[i],
            g_recv.at[i, to_z + 1],
            along(z + 1),
        )

    def g_down(i, to_z):
        b = rows_at(to_z * zb, zb)
        return copy(
            of(zs_a, zs_u, zs_d, i).at[b],
            of(zd_a, zd_u, zd_d, i).at[b],
            g_send.at[i],
            g_recv.at[i, to_z],
            along(z - 1),
        )

    def g_final(i, jj, src):
        at = (jj % 2 * 2 + jj // 2) * r if gx == 2 else jj * r
        return copy(
            of(fs_a, fs_u, fs_d, i).at[rows_at(at, r)],
            of(fr_a, fr_u, fr_d, i).at[src],
            fin_send.at[i],
            fin_recv.at[i],
            member(jj),
        )

    def all_given(i):
        rows = of(fs_a, fs_u, fs_d, i).at[pl.ds(0, (members - 1) * r)]
        return copy(rows, rows, fin_send.at[i], fin_recv.at[i], partner)

    def all_taken(i):
        rows = of(fr_a, fr_u, fr_d, i).at[pl.ds(0, members - 1)]
        return copy(rows, rows, fin_send.at[i], fin_recv.at[i], partner)

    def products(i, columns):
        if i in A:
            return [
                (0, 384, dot(normed[:, columns], grad_z[i], 0, 0)),
                (384, 512, dot(grads[:, columns], attended[i], 0, 0)),
            ]
        if i in U:
            return [(0, pw, dot(normed[:, columns], grad_u[i - na], 0, 0))]
        return [(0, pw, dot(grads[:, columns], active[i - na - nm], 0, 0))]

    cut = min(512, own)

    def weight_grad_cut(i, n):
        at = n * cut if gx == 2 else x * own + n * cut
        for lo, hi, part in products(i, rows_at(at, cut)):
            own_of(i)[n * cut : (n + 1) * cut, lo:hi] = part

    def weight_grad(i):
        if gx == 1:
            xs = of(xs_a, xs_u, xs_d, i)
            for n in range(own // cut):
                for lo, hi, part in products(i, rows_at((1 - x) * own + n * cut, cut)):
                    xs[n * cut : (n + 1) * cut, lo:hi] = part.astype(BF16)
            for to_z in range(nz):
                g_across(i, to_z).start()
        for n in range(own // cut):
            weight_grad_cut(i, n)

    def sum_x(i):
        if gx == 1:
            xr = of(xr_a, xr_u, xr_d, i)
            for to_z in range(nz):
                g_across(i, to_z).wait_recv()
                b = slice(to_z * chip, (to_z + 1) * chip)
                own_of(i)[b, :] += xr[b, :].astype(F32)

    def chain_step(i, to_z, last, came, buffer, send):
        b = rows_at(to_z * zb, zb)
        zs = of(zs_a, zs_u, zs_d, i)

        @pl.when(last)
        def _():
            zs[b, :] = own_of(i)[b, :].astype(BF16)

        @pl.when(jnp.logical_not(last))
        def _():
            came.wait_recv()
            zs[b, :] = (own_of(i)[b, :] + buffer[b, :].astype(F32)).astype(BF16)

        send.start()

    def chain_up(i, n):
        @pl.when(z <= n)
        def _():
            to_z = nz - 1 - n + z
            chain_step(i, to_z, z == 0, g_up(i, to_z), of(zu_a, zu_u, zu_d, i), g_up(i, to_z))

    def chain_down(i, n):
        @pl.when(nz - 1 - z <= n)
        def _():
            to_z = n - (nz - 1 - z)
            chain_step(i, to_z, z == nz - 1, g_down(i, to_z), of(zd_a, zd_u, zd_d, i), g_down(i, to_z))

    def own_index():
        return x * 2 + c if gx == 2 else c

    def chain_end(i):
        b = rows_at(z * zb, zb)

        @pl.when(z > 0)
        def _():
            g_up(i, z).wait_recv()
            own_of(i)[b, :] += of(zu_a, zu_u, zu_d, i)[b, :].astype(F32)

        @pl.when(z < nz - 1)
        def _():
            g_down(i, z).wait_recv()
            own_of(i)[b, :] += of(zd_a, zd_u, zd_d, i)[b, :].astype(F32)

        of(fs_a, fs_u, fs_d, i)[...] = own_of(i)[b, :].astype(BF16)
        for k in range(1, members):
            g_final(i, other_j(k), j).start()

    def finish(i):
        all_taken(i).wait_recv()
        keep = own_of(i)[rows_at(z * zb + own_index() * r, r), :]
        came = of(fr_a, fr_u, fr_d, i)
        for jj in range(members):
            part = jnp.where(j == jj, keep, came[jj].astype(F32))
            if i in A:
                heads = [
                    part[:, p * 128 + h * HEAD : p * 128 + (h + 1) * HEAD] for h in range(hp) for p in range(3)
                ]
                at = (jj * na + i) * wide
                qkv_grad[:, 3 * at : 3 * (at + wide)] = jnp.concatenate(heads, axis=1)
                dense_grad[:, at : at + wide] = part[:, 384 : 384 + wide]
            else:
                out, k = (up_grad, i - na) if i in U else (down_grad, i - na - nm)
                out[:, jj * units + k * pw : jj * units + (k + 1) * pw] = part
        if i == A[-1]:
            result(2).start()
            result(3).start()
        if i in (U[-1], Dn[-1]):
            result(4 if i in U else 5).start()

    def pick(parts):
        total = parts[0]
        for jj in range(1, members):
            total = jnp.where(j == jj, parts[jj], total)
        return total

    def prepare():
        for k in range(na):
            for part in range(3):
                ba[k, :, part * 128 : (part + 1) * 128] = pick(
                    [head_part(b_qkv[...].reshape(1, -1), jj, k, part) for jj in range(members)]
                )
        steps = np.arange(ROT // 2, dtype=np.float32) * 2.0 / ROT
        inverse = (np.float32(ROTARY_BASE) ** -steps).astype(np.float32)
        lane = lax.broadcasted_iota(jnp.int32, (128, 128), 1) % HEAD
        scale = jnp.zeros((128, 128), F32)
        for n in range(ROT):
            scale = jnp.where(lane == n, inverse[n % (ROT // 2)], scale)

        def table(n, carry):
            rows = rows_at(n * 128, 128)
            place = (n * 128 + lax.broadcasted_iota(jnp.int32, (128, 128), 0)).astype(F32)
            cos, sin = jnp.cos(place * scale), jnp.sin(place * scale)
            cos_table[rows, :] = cos
            sin_table[rows, :] = jnp.where(lane < ROT // 2, -sin, sin)
            return carry

        lax.fori_loop(0, length // 128, table, 0)

    def prepare_docs():
        all_docs().wait_recv()
        for s in range(members):
            for n in range(length // 128):
                cut = slice(n * 128, (n + 1) * 128)
                rows = jnp.broadcast_to(docs[s, 0:1, cut], (128, 128))
                doc_column[s, cut, :] = jnp.transpose(rows).astype(BF16)

    RT = min(512, total_rows)
    tiles = total_rows // RT
    lanes = lax.broadcasted_iota(jnp.int32, (1, 128), 1)
    first = lanes < HEAD
    low = lanes % HEAD < ROT // 2
    turning = lanes % HEAD < ROT

    def rotated(rows, places, sign):
        near = jnp.where(low, pltpu.roll(rows, 128 - ROT // 2, 1), pltpu.roll(rows, ROT // 2, 1))
        return rows * cos_table[places, :] + jnp.where(turning, sign * near * sin_table[places, :], 0.0)

    def project(k, n):
        rows = rows_at(n * RT, RT)
        places = rows_at(lax.rem(n * RT, length), RT)
        packed = dot(normed[rows, :], wa[k, :, 0:384], 1, 0) + ba[k]
        query[rows, :] = (rotated(packed[:, 0:128], places, 1.0) * (HEAD**-0.5)).astype(BF16)
        key[rows, :] = rotated(packed[:, 128:256], places, 1.0).astype(BF16)
        value[rows, :] = packed[:, 256:384].astype(BF16)

    def project_back(k, n):
        rows = rows_at(n * RT, RT)
        grad_out[rows, :] = dot(grads[rows, :], wa[k, :, 384:512], 1, 0).astype(BF16)

    def each_tile(step, k):
        def body(n, carry):
            step(k, n)
            return carry

        lax.fori_loop(0, tiles, body, 0)

    block = min(128, length // 4)
    window = length // 4 + block

    def stacked(rows):
        if hp == 1:
            return rows
        zero = jnp.zeros_like(rows)
        return jnp.concatenate([jnp.where(first, rows, zero), jnp.where(first, zero, rows)], axis=0)

    def unstacked(rows):
        if hp == 1:
            return rows
        return jnp.where(first, rows[:window], rows[window:])

    def attend(k, s):
        key_sum[...] = jnp.zeros_like(key_sum)
        value_sum[...] = jnp.zeros_like(value_sum)

        def body(n, carry):
            q_at = pl.multiple_of(n * block, block)
            k_at = pl.multiple_of(jnp.maximum(q_at - length // 4, 0), block)
            q_rows = rows_at(s * length + q_at, block)
            k_rows = pl.ds(pl.multiple_of(s * length + k_at, block), window)
            q = query[q_rows, :]
            g = grad_out[q_rows, :]
            keys, values = stacked(key[k_rows, :]), stacked(value[k_rows, :])
            scores = dot(q, keys, 1, 1)
            grad_p = dot(g, values, 1, 1)
            at = k_at + lax.broadcasted_iota(jnp.int32, (block, window), 1)
            here = q_at + lax.broadcasted_iota(jnp.int32, (block, window), 0)
            own_doc_of = doc_column[s, pl.ds(q_at, block), 0:1].astype(F32)
            same = own_doc_of == docs[s, 0:1, pl.ds(k_at, window)]
            allowed = same & (at <= here)
            probs, grad_s = [], []
            for h in range(hp):
                cut = slice(h * window, (h + 1) * window)
                sc = jnp.where(allowed, scores[:, cut], -1e30)
                expos = jnp.exp(sc - jnp.max(sc, axis=-1, keepdims=True))
                p = expos / jnp.sum(expos, axis=-1, keepdims=True)
                gp = grad_p[:, cut]
                inner = jnp.sum(p * gp, axis=-1, keepdims=True)
                probs.append(p.astype(BF16))
                grad_s.append((p * (gp - inner)).astype(BF16))
            p = jnp.concatenate(probs, axis=1) if hp > 1 else probs[0]
            gs = jnp.concatenate(grad_s, axis=1) if hp > 1 else grad_s[0]
            attended[k, q_rows, :] = dot(p, values, 1, 0).astype(BF16)
            places = pl.ds(q_at, block)
            back = rotated(dot(gs, keys, 1, 0) * (HEAD**-0.5), places, -1.0)
            grad_z[k, q_rows, 0:128] = back.astype(BF16)
            here_rows = pl.ds(k_at, window)
            key_sum[here_rows, :] += unstacked(dot(gs, q, 0, 0))
            value_sum[here_rows, :] += unstacked(dot(p, g, 0, 0))
            return carry

        lax.fori_loop(0, length // block, body, 0)
        rows = rows_at(s * length, length)
        grad_z[k, rows, 128:256] = rotated(key_sum[...], slice(None), -1.0).astype(BF16)
        grad_z[k, rows, 256:384] = value_sum[...].astype(BF16)

    def hidden(k, n):
        rows = rows_at(n * RT, RT)
        u = dot(normed[rows, :], wu[k], 1, 0) + b_up[:, rows_at(j * units + k * pw, pw)]
        phi = 0.5 * (1.0 + lax.erf(u * np.float32(0.5**0.5)))
        active[k, rows, :] = (u * phi).astype(BF16)
        slope[k, rows, :] = phi + u * (jnp.exp(-0.5 * u * u) * np.float32((2 * np.pi) ** -0.5))

    def hidden_back(k, n):
        rows = rows_at(n * RT, RT)
        grad_u[k, rows, :] = (dot(grads[rows, :], wd[k], 1, 0) * slope[k, rows, :]).astype(BF16)

    HT = min(512, length)

    def branch(a, jj):
        def body(n, carry):
            rows = rows_at(jj * length + n * HT, HT)
            total = None
            for k in range(na):
                if a == 0:
                    part = dot(attended[k, rows, :], wa[k, :, 384:512], 1, 1)
                else:
                    part = dot(grad_z[k, rows, :], wa[k, :, 0:384], 1, 1)
                total = part if total is None else total + part
            for k in range(nm):
                if a == 0:
                    part = dot(active[k, rows, :], wd[k], 1, 1)
                else:
                    part = dot(grad_u[k, rows, :], wu[k], 1, 1)
                total = total + part
            partials[a][rows, :] = total.astype(BF16)
            return carry

        lax.fori_loop(0, length // HT, body, 0)

    def half_copy(a, jj):
        at = jj - (1 - c) * gx
        return copy(
            partials[a].at[rows_at(jj * length, length)],
            core_in.at[a % nbuf, rows_at(at * length, length)],
            half_send.at[a, at],
            half_recv.at[a, at],
            partner,
        )

    def branch_give(a, jj):
        branch(a, jj)
        half_copy(a, jj).start()

    def branches(a):
        for n, jj in enumerate((far_j, partner_j)[2 - gx :]):
            branch(a, jj)
            if n == 0 and nbuf == 1 and a == second:
                pl.semaphore_wait(credit.at[0], 1)
            half_copy(a, jj).start()
        for jj in (across_j, j)[2 - gx :]:
            branch(a, jj)

    def block_rows(jj, tt):
        return rows_at((jj * nt + tt) * R, R)

    def in_rows(jj, tt):
        return rows_at(((jj - c * gx) * nt + tt) * R, R)

    def both_cores(a, jj, tt, columns=slice(None)):
        return (
            partials[a][block_rows(jj, tt), columns].astype(F32)
            + core_in[a % nbuf, in_rows(jj, tt), columns].astype(F32)
        )

    def corner_t_copy(a, tt, src):
        b = partials[a].at[block_rows(across_j, tt), back_t]
        n = step_of(src, tt)
        return copy(b, corner_t.at[a % nbuf, src], corner_t_send.at[2 + a, n], corner_t_recv.at[2 + a, n], turned(tt))

    def corner_x_copy(a, jj, tt):
        b = partials[a].at[block_rows(jj, tt), back_x]
        n = step_of(t, tt)
        return copy(b, corner_x.at[a % nbuf, tt], corner_x_send.at[2 + a, n], corner_x_recv.at[2 + a, n], across)

    def side_copy(a, jj):
        b = partials[a].at[block_rows(jj, t)]
        return copy(b, side_x.at[a % nbuf], side_send.at[2 + a], side_recv.at[2 + a], across)

    def turn_copy(a, tt, src):
        b = partials[a].at[block_rows(j, tt)]
        n = step_of(src, tt)
        return copy(b, side_t.at[a % nbuf, src], turn_send.at[2 + a, n], turn_recv.at[2 + a, n], turned(tt))

    def reduce_corner(a):
        if gx == 2:
            half_copy(a, far_j).wait_recv()
            for k in range(1, nt):
                tt = other_t(k)
                partials[a][block_rows(across_j, tt), :] = both_cores(a, across_j, tt).astype(BF16)
                corner_t_copy(a, tt, t).start()
                corner_x_copy(a, across_j, tt).start()

    def reduce_side(a):
        if gx == 2:
            total = both_cores(a, across_j, t, back_t)
            for k in range(1, nt):
                corner_t_copy(a, t, other_t(k)).wait_recv()
                total = total + corner_t[a % nbuf, other_t(k)].astype(F32)
            partials[a][block_rows(across_j, t), back_t] = total.astype(BF16)
            partials[a][block_rows(across_j, t), back_x] = both_cores(a, across_j, t, back_x).astype(BF16)
            side_copy(a, across_j).start()

    def reduce_turn(a):
        if nbuf == 1 and a == second and nt > 1:
            pl.semaphore_wait(credit.at[1], nt - 1)
        half_copy(a, partner_j).wait_recv()
        for k in range(1, nt):
            tt = other_t(k)
            if gx == 2:
                corner_x_copy(a, j, tt).wait_recv()
                total = both_cores(a, j, tt, back_x) + corner_x[a % nbuf, tt].astype(F32)
                partials[a][block_rows(j, tt), back_x] = total.astype(BF16)
                partials[a][block_rows(j, tt), back_t] = both_cores(a, j, tt, back_t).astype(BF16)
            else:
                partials[a][block_rows(j, tt), :] = both_cores(a, j, tt).astype(BF16)
            turn_copy(a, tt, t).start()

    def reduce_wait(a):
        if gx == 2:
            side_copy(a, across_j).wait_recv()
        for k in range(1, nt):
            turn_copy(a, t, other_t(k)).wait_recv()

    def reduced(a, n):
        mine = rows_at((j * nt + t) * R + n * tile, tile)
        came = rows_at(((j - c * gx) * nt + t) * R + n * tile, tile)
        rows = rows_at(n * tile, tile)
        total = partials[a][mine, :].astype(F32) + core_in[a % nbuf, came, :].astype(F32)
        if gx == 2:
            total = total + side_x[a % nbuf, rows, :].astype(F32)
        for k in range(1, nt):
            total = total + side_t[a % nbuf, other_t(k), rows, :].astype(F32)
        return restore(total)

    def reduce_sent(a):
        for xx in range(gx):
            half_copy(a, (1 - c) * gx + xx).wait_send()
        if gx == 2:
            side_copy(a, across_j).wait_send()
        for k in range(1, nt):
            tt = other_t(k)
            turn_copy(a, tt, t).wait_send()
            if gx == 2:
                corner_t_copy(a, tt, t).wait_send()
                corner_x_copy(a, across_j, tt).wait_send()

    def free_buffers():
        if nbuf == 1:
            pl.semaphore_signal(credit.at[0], inc=1, device_id=partner, device_id_type=MESH)
            for k in range(1, nt):
                pl.semaphore_signal(credit.at[1], inc=1, device_id=turned(other_t(k)), device_id_type=MESH)

    def write_output():
        def body(n, carry):
            rows = rows_at(n * tile, tile)
            total = tokens[rows, :].astype(F32) + reduced(0, n) + b_dense[...] + b_down[...]
            output[rows, :] = total.astype(BF16)
            return carry

        lax.fori_loop(0, R // tile, body, 0)
        result(0).start()

    def put(row, at, values):
        end = at + values.shape[1]
        for h in range(2):
            lo, hi = max(at, h * D // 2), min(end, (h + 1) * D // 2)
            if lo < hi:
                cols = slice(lo - h * D // 2, hi - h * D // 2)
                vec[2 * row + h : 2 * row + h + 1, cols] += values[:, lo - at : hi - at]

    def taken(array, row):
        return jnp.concatenate([array[2 * row : 2 * row + 1], array[2 * row + 1 : 2 * row + 2]], axis=1)

    def sum_biases():
        vec[...] = jnp.zeros_like(vec)
        for k in range(nm):
            put(3, k * pw, jnp.sum(grad_u[k].astype(F32), axis=0, keepdims=True))
        for k in range(na):
            put(3, units + k * 384, jnp.sum(grad_z[k].astype(F32), axis=0, keepdims=True))

    def write_input_grad():
        def body(n, carry):
            rows = rows_at(n * tile, tile)
            normal, inverse = normalize(tokens[rows, :].astype(F32))
            up = cotangent[rows, :].astype(F32)
            grad = reduced(1, n)
            put(0, 0, jnp.sum(grad * normal, axis=0, keepdims=True))
            put(1, 0, jnp.sum(grad, axis=0, keepdims=True))
            put(2, 0, jnp.sum(up, axis=0, keepdims=True))
            scaled = grad * gain[...]
            input_grad[rows, :] = up + inverse * (
                scaled
                - jnp.mean(scaled, axis=-1, keepdims=True)
                - normal * jnp.mean(scaled * normal, axis=-1, keepdims=True)
            )
            return carry

        lax.fori_loop(0, R // tile, body, 0)
        result(1).start()

    peers = nz if gx == 2 else 2 * nz
    mates = members * nt
    peer = z if gx == 2 else z * 2 + x
    mate = j * nt + t

    def peer_copy(to, src):
        device_to = device(to, x, c, t) if gx == 2 else device(to // 2, to % 2, c, t)
        return copy(vec_z.at[peer], vec_z.at[src], peer_send.at[0], peer_recv.at[0], device_to)

    def mate_copy(to, src):
        jj, tt = to // nt, to % nt
        device_to = device(z, jj % 2, jj // 2, tt) if gx == 2 else device(z, x, jj, tt)
        return copy(vec_m.at[mate], vec_m.at[src], mate_send.at[0], mate_recv.at[0], device_to)

    def all_peers():
        rows = vec_z.at[pl.ds(0, peers - 1)]
        return copy(rows, rows, peer_send.at[0], peer_recv.at[0], partner)

    def all_mates():
        rows = vec_m.at[pl.ds(0, mates - 1)]
        return copy(rows, rows, mate_send.at[0], mate_recv.at[0], partner)

    def sums_start():
        vec_z[peer] = vec[...]
        for k in range(1, peers):
            peer_copy(lax.rem(peer + k, peers), peer).start()

    def sums_group():
        all_peers().wait_recv()
        total = vec_z[0]
        for k in range(1, peers):
            total = total + vec_z[k]
        vec_m[mate] = total
        for k in range(1, mates):
            mate_copy(lax.rem(mate + k, mates), mate).start()

    def sums_end():
        all_mates().wait_recv()
        total = vec_m[0]
        for k in range(1, mates):
            total = total + vec_m[k]
        gain_grad[...] = taken(total, 0)
        shift_grad[...] = taken(total, 1)
        dense_bias[...] = taken(total, 2)
        for jj in range(members):
            row = taken(vec_m[jj * nt + t], 3)
            up_bias[:, jj * units : (jj + 1) * units] = row[:, :units]
            for k in range(na):
                part = row[:, units + k * 384 : units + (k + 1) * 384]
                heads = [part[:, p * 128 + h * HEAD : p * 128 + (h + 1) * HEAD] for h in range(hp) for p in range(3)]
                at = (jj * na + k) * wide
                qkv_bias[:, 3 * at : 3 * (at + wide)] = jnp.concatenate(heads, axis=1)
        for n in range(6, 11):
            result(n).start()

    def sums_sent():
        all_peers().wait_send()
        all_mates().wait_send()

    def forwards(some, lo, hi):
        for d in range(lo, hi):
            for i in some:
                forward_up(i, d)
                forward_down(i, d)

    def chains(some, lo, hi):
        for n in range(lo, hi):
            for i in some:
                chain_up(i, n)
                chain_down(i, n)

    second = 0 if gx == 2 else 1

    def any_order():
        stage()
        fill_normed()
        enter()
        for i in U + A + Dn:
            send_first(i)
            share(i)
        give_docs()
        act_start(0)
        fill_grads()
        act_start(1)
        for i in U + A:
            send_own(i)
        prepare()
        prepare_docs()
        forwards(U + A, 1, 2)
        act_from_turn(0)
        act_from_side(0)
        for i in Dn:
            send_own(i)
        forwards(U, 2, nz)
        act_finish(0)
        act_wait(0)
        for i in U:
            gathered(i)
            each_tile(hidden, i - na)
        act_from_turn(1)
        act_from_side(1)
        forwards(A, 2, nz)
        forwards(Dn, 1, nz)
        act_finish(1)
        act_wait(1)
        for i in Dn:
            weight_grad(i)
            sum_x(i)
        chains(Dn, 0, nz - 1)
        for i in A:
            gathered(i)
            each_tile(project, i)
            each_tile(project_back, i)
            for s in range(members):
                attend(i, s)
            weight_grad(i)
            sum_x(i)
        chains(A, 0, nz - 1)
        for i in Dn:
            gathered(i)
            each_tile(hidden_back, i - na - nm)
        for i in U:
            weight_grad(i)
            sum_x(i)
        act_sent(0)
        act_sent(1)
        sum_biases()
        for a in (1, 0) if gx == 2 else (0, 1):
            branches(a)
            reduce_corner(a)
            if a != second:
                chains(U, 0, nz - 1)
            reduce_side(a)
            reduce_turn(a)
            if a != second:
                for i in Dn + A:
                    chain_end(i)
            reduce_wait(a)
            if a == 0:
                write_output()
            else:
                write_input_grad()
                sums_start()
            if a != second:
                free_buffers()
        for i in U:
            chain_end(i)
        sums_group()
        for i in Dn + A + U:
            finish(i)
        sums_end()

    def tuned_order():
        (a,), (u,), (d,) = A, U, Dn
        stage()
        enter()
        share(a)
        give_docs()
        send_first(d)
        fill_normed()
        send_first(u)
        share(u)
        prepare()
        send_first(a)
        fill_grads()
        act_start_turn(0)
        send_own(a)
        act_start_side(0)
        act_start_side(1)
        act_start_turn(1)
        send_own(u)
        forward_up(a, 1)
        share(d)
        forward_down(a, 1)
        forward_down(u, 1)
        forward_down(a, 2)
        forward_up(u, 1)
        prepare_docs()
        forward_up(a, 2)
        act_from_turn(0)
        act_from_side(0)
        act_wait_of(0, partner_j)
        forward_down(u, 2)
        forward_up(u, 2)
        forward_up(a, 3)
        forward_down(a, 3)
        act_from_side(1)
        act_from_turn(1)
        project(0, partner_j)
        send_own(d)
        project_back(0, j)
        project(0, j)
        attend(0, j)
        act_wait_of(1, partner_j)
        act_finish(0)
        forward_down(u, 3)
        forward_up(u, 3)
        hidden(0, across_j)
        hidden(0, j)
        act_wait_of(0, far_j)
        hidden(0, partner_j)
        hidden(0, far_j)
        act_finish(1)
        forward_up(d, 1)
        forward_down(d, 1)
        project(0, across_j)
        project(0, far_j)
        act_wait_of(1, far_j)
        weight_grad_cut(d, 0)
        chain_down(d, 0)
        weight_grad_cut(d, 1)
        chain_up(d, 0)
        project_back(0, far_j)
        attend(0, far_j)
        project_back(0, across_j)
        forward_up(d, 2)
        forward_down(d, 2)
        attend(0, across_j)
        chain_down(d, 1)
        project_back(0, partner_j)
        chain_up(d, 1)
        attend(0, partner_j)
        forward_down(d, 3)
        forward_up(d, 3)
        hidden_back(0, far_j)
        branch_give(1, far_j)
        hidden_back(0, across_j)
        chain_down(d, 2)
        chain_up(d, 2)
        branch(1, across_j)
        reduce_corner(1)
        weight_grad_cut(a, 0)
        weight_grad_cut(a, 1)
        chain_down(a, 0)
        chain_up(a, 0)
        act_sent(0)
        act_sent(1)
        branch_give(0, far_j)
        hidden_back(0, j)
        hidden_back(0, partner_j)
        branch(0, across_j)
        weight_grad_cut(u, 0)
        reduce_corner(0)
        chain_down(u, 0)
        weight_grad_cut(u, 1)
        chain_up(u, 0)
        sum_biases()
        chain_end(d)
        chain_up(a, 1)
        reduce_side(1)
        branch(1, j)
        branch_give(1, partner_j)
        chain_down(a, 1)
        branch(0, j)
        reduce_turn(1)
        branch_give(0, partner_j)
        chain_up(u, 1)
        chain_down(u, 1)
        finish(d)
        reduce_side(0)
        reduce_turn(0)
        chain_up(a, 2)
        chain_down(a, 2)
        reduce_wait(1)
        write_input_grad()
        sums_start()
        chain_down(u, 2)
        chain_up(u, 2)
        chain_end(a)
        sums_group()
        chain_end(u)
        sums_end()
        reduce_wait(0)
        write_output()
        finish(a)
        finish(u)

    if (gx, na, nm, nz, tiles, RT) == (2, 1, 1, 4, 4, length):
        tuned_order()
    else:
        any_order()

    for i in range(count):
        all_given(i).wait_send()
        all_parts(i).wait_send()
        for n in range(1, nz):
            blocks = weights(i).at[pl.ds(0, n * zb)]
            pl.when(z == n - 1)(
                lambda: copy(blocks, blocks, up_send.at[i], z_recv.at[i, 0], along(z + 1)).wait_send()
            )
            pl.when(z == nz - n)(
                lambda: copy(blocks, blocks, down_send.at[i], z_recv.at[i, 0], along(z - 1)).wait_send()
            )
        sums = of(zs_a, zs_u, zs_d, i).at[pl.ds(0, (nz - 1) * zb)]
        copy(sums, sums, g_send.at[i], g_recv.at[i, 0], partner).wait_send()
        if gx == 1:
            for src in range(nz):
                send_across(i, src, x).wait_send()
                g_across(i, src).wait_send()
    all_docs().wait_send()
    reduce_sent(0)
    reduce_sent(1)
    sums_sent()
    for n in range(len(results)):
        result(n).wait()


def hand_out(arrays):
    count = len(arrays)
    thin = [array.shape[0] == 1 for array in arrays]
    leaving = [
        jax.ShapeDtypeStruct(array.shape[1:] if flat else array.shape, array.dtype) for array, flat in zip(arrays, thin)
    ]

    def body(*refs):
        given, taken, came, goes, sems = (
            refs[:count],
            refs[count : 2 * count],
            refs[2 * count : 3 * count],
            refs[3 * count : -1],
            refs[-1],
        )
        reads = [pltpu.make_async_copy(given[n], came[n], sems.at[0, n]) for n in range(count)]
        writes = [
            pltpu.make_async_copy(goes[n] if thin[n] else came[n], taken[n], sems.at[1, n]) for n in range(count)
        ]
        order = sorted(range(count), key=lambda n: thin[n])
        for n in order:
            reads[n].start()
        for n in order:
            reads[n].wait()
            if thin[n]:
                goes[n][...] = came[n][0]
            writes[n].start()
        for n in order:
            writes[n].wait()

    far = pl.BlockSpec(memory_space=pl.ANY)
    return list(
        pl.pallas_call(
            body,
            out_shape=leaving,
            in_specs=[far] * count,
            out_specs=[far] * count,
            scratch_shapes=[pltpu.VMEM(array.shape, array.dtype) for array in arrays]
            + [pltpu.VMEM(part.shape if flat else (8, 128), part.dtype) for part, flat in zip(leaving, thin)]
            + [pltpu.SemaphoreType.DMA((2, count))],
            name="hand_out",
        )(*arrays)
    )


def on_device(
    nt,
    n_dp,
    tokens,
    cotangent,
    segments,
    ln_gain,
    ln_bias,
    w_qkv,
    b_qkv,
    w_dense,
    b_dense,
    w_up,
    b_up,
    w_down,
    b_down,
):
    R, D = tokens.shape
    length = segments.shape[1]
    r = w_qkv.shape[0]
    nz = n_dp // 4
    heads = w_qkv.shape[1] // (3 * HEAD)
    gx = 2 if heads % 4 == 0 and 4 * length * D <= 1 << 21 else 1
    members = 2 * gx
    heads = heads // members
    hp = 2 if heads % 2 == 0 else 1
    na = heads // hp
    units = w_up.shape[1] // members
    pw = 512 if units % 512 == 0 else units
    nm = units // pw
    nbuf = gx
    peers, mates, steps = (nz if gx == 2 else 2 * nz), members * nt, max(nt - 1, 1)
    sizes = dict(nt=nt, nz=nz, gx=gx, na=na, nm=nm, hp=hp, length=length, R=R, r=r, pw=pw, nbuf=nbuf)

    widths = ((na, 512), (nm, pw), (nm, pw))
    count = na + 2 * nm
    rows = members * length
    own = D if gx == 2 else D // 2
    chip = 2 * r
    split = D // 4
    V = pltpu.VMEM
    DMA = pltpu.SemaphoreType.DMA

    def some(shape):
        return V(shape if gx == 2 else (1, 1, 8, 128)[-len(shape) :], BF16)

    scratch = (
        [V((members, na, r, 512), BF16), V((na, 1, 384), F32)]
        + [V((length, 128), F32)] * 2
        + [V((members, 8, length), F32), V((members, length, 128), BF16)]
        + [V((n, D, w), BF16) for n, w in widths]
        + [V((rows, D), BF16), V((rows, D), BF16)]
        + [V((rows, 128), BF16)] * 4
        + [V((na, rows, 128), BF16), V((na, rows, 384), BF16)]
        + [V((length, 128), F32)] * 2
        + [V((nm, rows, pw), BF16), V((nm, rows, pw), F32), V((nm, rows, pw), BF16)]
        + [V((rows, D) if gx == 2 else (8, 128), BF16)]
        + [V((nbuf, gx * length, D), BF16), some((nbuf, nt, R, split)), some((nbuf, nt, R, D - split))]
        + [some((nbuf, R, D)), V((nbuf, nt, R, D), BF16)]
        + [V((n, own, w), F32) for n, w in widths]
        + [V((n, own, w) if gx == 1 else (n, 8, 128), BF16) for _ in range(2) for n, w in widths]
        + [V((n, own, w), BF16) for _ in range(3) for n, w in widths]
        + [V((n, gx * chip, w), BF16) for n, w in widths]
        + [V((n, members, r, w), BF16) for n, w in widths]
        + [V((8, D // 2), F32), V((peers, 8, D // 2), F32), V((mates, 8, D // 2), F32)]
        + [DMA((count,)), DMA((22,)), DMA((count + 1,)), DMA((count + 1,))]
        + [DMA((count,)), DMA((count,)), DMA((count, nz))]
        + [DMA((count, nz) if gx == 1 else (1, 1))] * 2
        + [DMA((4, steps))] * 2
        + [DMA((4,))] * 2
        + [DMA((4, steps))] * 4
        + [DMA((2, gx, nt))] * 2
        + [DMA((count, nz) if gx == 1 else (1, 1))] * 2
        + [DMA((count,)), DMA((count, nz + 1))]
        + [DMA((count,))] * 2
        + [DMA((2, gx))] * 2
        + [DMA((1,))] * 4
        + [pltpu.SemaphoreType.REGULAR((2,))]
    )
    far = pl.BlockSpec(memory_space=pl.ANY)

    def row(vector):
        return vector.reshape(1, -1)

    args = (
        tokens,
        cotangent,
        segments,
        row(ln_gain),
        row(ln_bias),
        w_qkv,
        b_qkv,
        w_dense.T,
        row(b_dense),
        w_up,
        row(b_up),
        w_down.T,
        row(b_down),
    )
    shapes = (
        jax.ShapeDtypeStruct((R, D), BF16),
        jax.ShapeDtypeStruct((R, D), F32),
        jax.ShapeDtypeStruct((1, D), F32),
        jax.ShapeDtypeStruct((1, D), F32),
        jax.ShapeDtypeStruct(w_qkv.shape, F32),
        jax.ShapeDtypeStruct((1, w_qkv.shape[1]), F32),
        jax.ShapeDtypeStruct(w_dense.shape[::-1], F32),
        jax.ShapeDtypeStruct((1, D), F32),
        jax.ShapeDtypeStruct(w_up.shape, F32),
        jax.ShapeDtypeStruct((1, w_up.shape[1]), F32),
        jax.ShapeDtypeStruct(w_down.shape[::-1], F32),
    )
    out = pl.pallas_call(
        functools.partial(kernel, sizes),
        out_shape=shapes,
        in_specs=[far] * len(args),
        out_specs=[far] * len(shapes),
        scratch_shapes=[V(args[n].shape, args[n].dtype) for n in (0, 1, 2, 3, 4, 5, 6, 7, 8, 10, 12)]
        + [V(shape.shape, shape.dtype) for shape in shapes]
        + scratch,
        compiler_params=pltpu.CompilerParams(
            collective_id=0, has_side_effects=True, vmem_limit_bytes=67043328
        ),
        name="layer",
    )(*args)
    out = hand_out((*out, out[7]))
    out[6], out[10] = out[6].T, out[10].T
    return tuple(out)


def solution(mesh):
    return jax.shard_map(
        functools.partial(on_device, mesh.shape["tensor"], mesh.shape["dp"]),
        mesh=mesh,
        in_specs=(
            P(("dp", "tensor"), None),
            P(("dp", "tensor"), None),
            P("dp", None),
            P(),
            P(),
            P("dp", "tensor"),
            P("tensor"),
            P("tensor", "dp"),
            P(),
            P("dp", "tensor"),
            P("tensor"),
            P("tensor", "dp"),
            P(),
        ),
        out_specs=(
            P(("dp", "tensor"), None),
            P(("dp", "tensor"), None),
            P(),
            P(),
            P("dp", "tensor"),
            P("tensor"),
            P("tensor", "dp"),
            P(),
            P("dp", "tensor"),
            P("tensor"),
            P("tensor", "dp"),
            P(),
        ),
        check_vma=False,
    )
```

```python
import functools

import jax
import jax.numpy as jnp
import numpy as np
from jax import lax
from jax.experimental import pallas as pl
from jax.experimental.pallas import tpu as pltpu
from jax.sharding import PartitionSpec as P

HEAD = 64
ROT = 16
NORM_EPS = 1e-05
ROTARY_BASE = 10000.0
MESH = pl.DeviceIdType.MESH
F32 = jnp.float32
BF16 = jnp.bfloat16


def dot(left, right, over_left, over_right):
    return lax.dot_general(
        left, right, (((over_left,), (over_right,)), ((), ())), preferred_element_type=F32
    )


def normalize(rows):
    centred = rows - jnp.mean(rows, axis=-1, keepdims=True)
    inverse = lax.rsqrt(jnp.mean(centred * centred, axis=-1, keepdims=True) + NORM_EPS)
    return centred * inverse, inverse


def padded(array):
    rest = -array.shape[1] % 128
    return jnp.concatenate([array, jnp.zeros((array.shape[0], rest), array.dtype)], axis=1) if rest else array


def kernel(
    sizes,
    tokens_hbm,
    cotangent_hbm,
    segments_hbm,
    gain_hbm,
    shift_hbm,
    w_qkv_hbm,
    b_qkv_hbm,
    w_dense_hbm,
    b_dense_hbm,
    w_up,
    b_up_hbm,
    w_down,
    b_down_hbm,
    output_hbm,
    input_grad_hbm,
    gain_grad_hbm,
    shift_grad_hbm,
    qkv_grad_hbm,
    qkv_bias_hbm,
    dense_grad_hbm,
    dense_bias_hbm,
    up_grad_hbm,
    up_bias_hbm,
    down_grad_hbm,
    tokens,
    cotangent,
    segments,
    gain,
    shift,
    w_qkv,
    b_qkv,
    w_dense,
    b_dense,
    b_up,
    b_down,
    output,
    input_grad,
    gain_grad,
    shift_grad,
    qkv_grad,
    qkv_bias,
    dense_grad,
    dense_bias,
    up_grad,
    up_bias,
    down_grad,
    wa_in,
    ba,
    cos_table,
    sin_table,
    docs,
    doc_column,
    wa,
    wu,
    wd,
    normed,
    grads,
    query,
    key,
    value,
    grad_out,
    attended,
    grad_z,
    key_sum,
    value_sum,
    active,
    slope,
    grad_u,
    late,
    core_in,
    corner_x,
    corner_t,
    side_x,
    side_t,
    own_a,
    own_u,
    own_d,
    xs_a,
    xs_u,
    xs_d,
    xr_a,
    xr_u,
    xr_d,
    zs_a,
    zs_u,
    zs_d,
    zu_a,
    zu_u,
    zu_d,
    zd_a,
    zd_u,
    zd_d,
    fs_a,
    fs_u,
    fs_d,
    fr_a,
    fr_u,
    fr_d,
    vec,
    vec_z,
    vec_m,
    local_sem,
    io_sem,
    share_send,
    share_recv,
    up_send,
    down_send,
    z_recv,
    x_send,
    x_recv,
    turn_send,
    turn_recv,
    side_send,
    side_recv,
    corner_x_send,
    corner_x_recv,
    corner_t_send,
    corner_t_recv,
    pass_send,
    pass_recv,
    gx_send,
    gx_recv,
    g_send,
    g_recv,
    fin_send,
    fin_recv,
    half_send,
    half_recv,
    peer_send,
    peer_recv,
    mate_send,
    mate_recv,
    credit,
):
    nt, nz, gx, na, nm, hp, length, R, r, pw, nbuf = (
        sizes[k] for k in ("nt", "nz", "gx", "na", "nm", "hp", "length", "R", "r", "pw", "nbuf")
    )
    D = tokens.shape[1]
    chip = 2 * r
    zb = gx * chip
    own = D if gx == 2 else D // 2
    members = 2 * gx
    wide = hp * HEAD
    units = nm * pw
    total_rows = members * length
    partials = (grads, late if gx == 2 else normed)
    dp, t = lax.axis_index("dp"), lax.axis_index("tensor")
    z, x, c = dp // 4, (dp // 2) % 2, dp % 2
    j = c * gx + x if gx == 2 else c

    def device(zz, xx, cc, tt):
        return (zz * 4 + xx * 2 + cc, tt)

    partner = device(z, x, 1 - c, t)
    across = device(z, 1 - x, c, t)

    def member(jj):
        return device(z, jj % 2, jj // 2, t) if gx == 2 else device(z, x, jj, t)

    def along(zz):
        return device(zz, x, c, t)

    def turned(tt):
        return device(z, x, c, tt)

    def other_j(k):
        return lax.rem(j + k, members)

    def other_z(k):
        return lax.rem(z + k, nz)

    def other_t(k):
        return lax.rem(t + k, nt)

    def step_of(src, tt):
        return lax.rem(tt - src + nt, nt) - 1

    def rows_at(start, size):
        return pl.ds(pl.multiple_of(start, size), size)

    def copy(src, dst, send, recv, to):
        return pltpu.make_async_remote_copy(
            src_ref=src, dst_ref=dst, send_sem=send, recv_sem=recv, device_id=to, device_id_type=MESH
        )

    A = list(range(na))
    U = list(range(na, na + nm))
    Dn = list(range(na + nm, na + 2 * nm))
    count = na + 2 * nm

    def of(a, u, d, i):
        if i in A:
            return a.at[i]
        return u.at[i - na] if i in U else d.at[i - na - nm]

    def weights(i):
        return of(wa, wu, wd, i)

    def z_rows(zz):
        return rows_at(zz * zb if gx == 2 else (x * nz + zz) * chip, zb)

    own_rows = rows_at(z * zb + (x * 2 + c) * r if gx == 2 else (x * nz + z) * chip + c * r, r)

    barrier = pltpu.get_barrier_semaphore()
    greeted = [member(other_j(k)) for k in range(1, members)] + ([] if gx == 2 else [across])
    greeted += [
        device(z, jj % 2 if gx == 2 else x, jj // 2 if gx == 2 else jj, other_t(k))
        for k in range(1, nt)
        for jj in [other_j(n) for n in range(members)]
    ]

    def greet(other):
        pl.semaphore_signal(barrier, inc=1, device_id=other, device_id_type=MESH)

    for other in greeted:
        greet(other)
    pl.when(z > 0)(lambda: greet(along(z - 1)))
    pl.when(z < nz - 1)(lambda: greet(along(z + 1)))

    reads = [
        pltpu.make_async_copy(src, dst, io_sem.at[n])
        for n, (src, dst) in enumerate(
            (
                (segments_hbm, segments),
                (gain_hbm, gain),
                (shift_hbm, shift),
                (b_qkv_hbm, b_qkv),
                (b_dense_hbm, b_dense),
                (b_up_hbm, b_up),
                (b_down_hbm, b_down),
                (w_qkv_hbm, w_qkv),
                (w_dense_hbm, w_dense),
                (tokens_hbm, tokens),
                (cotangent_hbm, cotangent),
            )
        )
    ]
    for read in reads:
        read.start()

    def enter():
        pl.semaphore_wait(barrier, len(greeted) + jnp.minimum(z, 1) + jnp.minimum(nz - 1 - z, 1))

    results = (
        (output, output_hbm),
        (input_grad, input_grad_hbm),
        (qkv_grad, qkv_grad_hbm),
        (dense_grad, dense_grad_hbm),
        (up_grad, up_grad_hbm),
        (down_grad, down_grad_hbm),
        (gain_grad, gain_grad_hbm),
        (shift_grad, shift_grad_hbm),
        (qkv_bias, qkv_bias_hbm),
        (dense_bias, dense_bias_hbm),
        (up_bias, up_bias_hbm),
    )

    def result(n):
        return pltpu.make_async_copy(*results[n], io_sem.at[11 + n])

    def part_of(i, jj):
        if i in A:
            return wa_in.at[jj, i]
        ref, k = (w_up, i - na) if i in U else (w_down, i - na - nm)
        return ref.at[:, rows_at(jj * units + k * pw, pw)]

    def local_copy(i):
        return pltpu.make_async_copy(part_of(i, j), weights(i).at[own_rows], local_sem.at[i])

    def give_part(i, jj):
        dst = weights(i).at[own_rows]
        return copy(part_of(i, jj), dst, share_send.at[i], share_recv.at[i], member(jj))

    def all_parts(i):
        rows = weights(i).at[pl.ds(0, (members - 1) * r)]
        return copy(rows, rows, share_send.at[i], share_recv.at[i], partner)

    def member_rows(jj):
        return rows_at(z * zb + (jj % 2 * 2 + jj // 2) * r if gx == 2 else (x * nz + z) * chip + jj * r, r)

    def share(i):
        local_copy(i).start()
        for k in range(1, members):
            give_part(i, other_j(k)).start()

    def head_part(array, jj, k, part):
        at = [((jj * na + k) * hp + h) * 3 * HEAD + part * HEAD for h in range(hp)]
        return padded(jnp.concatenate([array[:, a : a + HEAD] for a in at], axis=1))

    def own_doc(jj):
        return copy(docs.at[j], docs.at[j], share_send.at[count], share_recv.at[count], member(jj))

    def all_docs():
        rows = docs.at[pl.ds(0, members - 1)]
        return copy(rows, rows, share_send.at[count], share_recv.at[count], partner)

    def stage():
        for read in reads[:9]:
            read.wait()
        for jj in range(members):
            for k in range(na):
                for part in range(3):
                    wa_in[jj, k, :, part * 128 : (part + 1) * 128] = head_part(w_qkv[...], jj, k, part)
                at = (jj * na + k) * wide
                wa_in[jj, k, :, 384:512] = padded(w_dense[:, at : at + wide])
        docs[j] = jnp.broadcast_to(segments[...].astype(F32), docs.shape[1:])

    def give_docs():
        for k in range(1, members):
            own_doc(other_j(k)).start()

    def permute(rows):
        if gx == 2:
            return rows
        return jnp.concatenate(
            [rows[:, (zz * 2 + xx) * chip : (zz * 2 + xx + 1) * chip] for xx in range(2) for zz in range(nz)],
            axis=1,
        )

    def restore(rows):
        if gx == 2:
            return rows
        return jnp.concatenate(
            [rows[:, (xx * nz + zz) * chip : (xx * nz + zz + 1) * chip] for zz in range(nz) for xx in range(2)],
            axis=1,
        )

    acts = (normed, grads)
    tile = min(64, R)
    split = D * 3 // 8
    over_x, over_t = slice(0, split), slice(split, D)
    back_split = D // 4
    back_x, back_t = slice(0, back_split), slice(back_split, D)

    def act_rows(jj, tt):
        return rows_at((jj * nt + tt) * R, R)

    across_j = c * gx + 1 - x if gx == 2 else c
    partner_j = (1 - c) * gx + x if gx == 2 else 1 - c
    far_j = (1 - c) * gx + 1 - x if gx == 2 else 1 - c
    near = (j, partner_j, across_j, far_j)

    def fill_normed():
        reads[9].wait()

        def body(n, carry):
            rows = rows_at(n * tile, tile)
            normal, _ = normalize(tokens[rows, :].astype(F32))
            normed[rows_at((j * nt + t) * R + n * tile, tile), :] = permute(
                (normal * gain[...] + shift[...]).astype(BF16)
            )
            return carry

        lax.fori_loop(0, R // tile, body, 0)

    def fill_grads():
        reads[10].wait()

        def body(n, carry):
            grads[rows_at((j * nt + t) * R + n * tile, tile), :] = permute(cotangent[rows_at(n * tile, tile), :])
            return carry

        lax.fori_loop(0, R // tile, body, 0)

    def act_turn(a, tt, src):
        b = acts[a].at[act_rows(j, src)]
        return copy(b, b, turn_send.at[a, step_of(src, tt)], turn_recv.at[a, step_of(src, tt)], turned(tt))

    def act_side(a, jj):
        b = acts[a].at[act_rows(jj, t)]
        return copy(b, b, side_send.at[a], side_recv.at[a], across)

    def act_corner_x(a, jj, tt):
        b = acts[a].at[act_rows(jj, tt), over_x]
        return copy(b, b, corner_x_send.at[a, step_of(t, tt)], corner_x_recv.at[a, step_of(t, tt)], across)

    def act_corner_t(a, tt, src):
        b = acts[a].at[act_rows(across_j, src), over_t]
        return copy(b, b, corner_t_send.at[a, step_of(src, tt)], corner_t_recv.at[a, step_of(src, tt)], turned(tt))

    def act_pass(a, jj, tt):
        b = acts[a].at[act_rows(jj, tt)]
        return copy(b, b, pass_send.at[a, jj % gx, tt], pass_recv.at[a, jj % gx, tt], partner)

    def act_start_side(a):
        if gx == 2:
            act_side(a, j).start()

    def act_start_turn(a):
        for k in range(1, nt):
            act_turn(a, other_t(k), t).start()
        act_pass(a, j, t).start()

    def act_start(a):
        act_start_side(a)
        act_start_turn(a)

    def act_from_turn(a):
        for k in range(1, nt):
            src = other_t(k)
            act_turn(a, t, src).wait_recv()
            if gx == 2:
                act_corner_x(a, j, src).start()
            act_pass(a, j, src).start()

    def act_from_side(a):
        if gx == 2:
            act_side(a, across_j).wait_recv()
            for k in range(1, nt):
                act_corner_t(a, other_t(k), t).start()
            act_pass(a, across_j, t).start()

    def act_finish(a):
        if gx == 2:
            for k in range(1, nt):
                src = other_t(k)
                act_corner_x(a, across_j, src).wait_recv()
                act_corner_t(a, t, src).wait_recv()
                act_pass(a, across_j, src).start()

    def act_wait_of(a, jj):
        for k in range(nt):
            act_pass(a, jj, k).wait_recv()

    def act_wait(a):
        for xx in range(gx):
            act_wait_of(a, (1 - c) * gx + xx)

    def act_sent(a):
        if gx == 2:
            act_side(a, j).wait_send()
        for k in range(1, nt):
            act_turn(a, other_t(k), t).wait_send()
            if gx == 2:
                act_corner_x(a, j, other_t(k)).wait_send()
                act_corner_t(a, other_t(k), t).wait_send()
        for xx in range(gx):
            for k in range(nt):
                act_pass(a, c * gx + xx, k).wait_send()

    def w_block(i, zz):
        return weights(i).at[z_rows(zz)]

    def send_up(i, src):
        b = w_block(i, src)
        return copy(b, b, up_send.at[i], z_recv.at[i, src], along(z + 1))

    def send_down(i, src):
        b = w_block(i, src)
        return copy(b, b, down_send.at[i], z_recv.at[i, src], along(z - 1))

    def send_across(i, src, xx):
        b = weights(i).at[rows_at((xx * nz + src) * chip, chip)]
        return copy(b, b, x_send.at[i, src], x_recv.at[i, src], across)

    def send_first(i):
        def along_z(sems, to):
            return copy(part_of(i, j), weights(i).at[own_rows], sems.at[i], z_recv.at[i, z], to)

        pl.when(z < nz - 1)(lambda: along_z(up_send, along(z + 1)).start())
        pl.when(z > 0)(lambda: along_z(down_send, along(z - 1)).start())

    def send_own(i):
        local_copy(i).wait()
        all_parts(i).wait_recv()
        for k in range(1, members):
            jj = other_j(k)
            rows = weights(i).at[member_rows(jj)]

            def along_z(sems, to):
                return copy(rows, rows, sems.at[i], z_recv.at[i, z], to)

            pl.when(z < nz - 1)(lambda: along_z(up_send, along(z + 1)).start())
            pl.when(z > 0)(lambda: along_z(down_send, along(z - 1)).start())
        if gx == 1:
            send_across(i, z, x).start()

    def forward_up(i, d):
        @pl.when(z >= d)
        def _():
            send_up(i, z - d).wait_recv()
            pl.when(z < nz - 1)(lambda: send_up(i, z - d).start())
            if gx == 1:
                send_across(i, z - d, x).start()

    def forward_down(i, d):
        @pl.when(z + d <= nz - 1)
        def _():
            send_down(i, z + d).wait_recv()
            pl.when(z > 0)(lambda: send_down(i, z + d).start())
            if gx == 1:
                send_across(i, z + d, x).start()

    def gathered(i):
        if gx == 1:
            for src in range(nz):
                send_across(i, src, 1 - x).wait_recv()

    def own_of(i):
        return of(own_a, own_u, own_d, i)

    def g_across(i, to_z):
        b = pl.ds(to_z * chip, chip)
        return copy(
            of(xs_a, xs_u, xs_d, i).at[b],
            of(xr_a, xr_u, xr_d, i).at[b],
            gx_send.at[i, to_z],
            gx_recv.at[i, to_z],
            across,
        )

    def g_up(i, to_z):
        b = rows_at(to_z * zb, zb)
        return copy(
            of(zs_a, zs_u, zs_d, i).at[b],
            of(zu_a, zu_u, zu_d, i).at[b],
            g_send.at[i],
            g_recv.at[i, to_z + 1],
            along(z + 1),
        )

    def g_down(i, to_z):
        b = rows_at(to_z * zb, zb)
        return copy(
            of(zs_a, zs_u, zs_d, i).at[b],
            of(zd_a, zd_u, zd_d, i).at[b],
            g_send.at[i],
            g_recv.at[i, to_z],
            along(z - 1),
        )

    def g_final(i, jj, src):
        at = (jj % 2 * 2 + jj // 2) * r if gx == 2 else jj * r
        return copy(
            of(fs_a, fs_u, fs_d, i).at[rows_at(at, r)],
            of(fr_a, fr_u, fr_d, i).at[src],
            fin_send.at[i],
            fin_recv.at[i],
            member(jj),
        )

    def all_given(i):
        rows = of(fs_a, fs_u, fs_d, i).at[pl.ds(0, (members - 1) * r)]
        return copy(rows, rows, fin_send.at[i], fin_recv.at[i], partner)

    def all_taken(i):
        rows = of(fr_a, fr_u, fr_d, i).at[pl.ds(0, members - 1)]
        return copy(rows, rows, fin_send.at[i], fin_recv.at[i], partner)

    def products(i, columns):
        if i in A:
            return [
                (0, 384, dot(normed[:, columns], grad_z[i], 0, 0)),
                (384, 512, dot(grads[:, columns], attended[i], 0, 0)),
            ]
        if i in U:
            return [(0, pw, dot(normed[:, columns], grad_u[i - na], 0, 0))]
        return [(0, pw, dot(grads[:, columns], active[i - na - nm], 0, 0))]

    cut = min(512, own)

    def weight_grad_cut(i, n):
        at = n * cut if gx == 2 else x * own + n * cut
        for lo, hi, part in products(i, rows_at(at, cut)):
            own_of(i)[n * cut : (n + 1) * cut, lo:hi] = part

    def weight_grad(i):
        if gx == 1:
            xs = of(xs_a, xs_u, xs_d, i)
            for n in range(own // cut):
                for lo, hi, part in products(i, rows_at((1 - x) * own + n * cut, cut)):
                    xs[n * cut : (n + 1) * cut, lo:hi] = part.astype(BF16)
            for to_z in range(nz):
                g_across(i, to_z).start()
        for n in range(own // cut):
            weight_grad_cut(i, n)

    def sum_x(i):
        if gx == 1:
            xr = of(xr_a, xr_u, xr_d, i)
            for to_z in range(nz):
                g_across(i, to_z).wait_recv()
                b = slice(to_z * chip, (to_z + 1) * chip)
                own_of(i)[b, :] += xr[b, :].astype(F32)

    def chain_step(i, to_z, last, came, buffer, send):
        b = rows_at(to_z * zb, zb)
        zs = of(zs_a, zs_u, zs_d, i)

        @pl.when(last)
        def _():
            zs[b, :] = own_of(i)[b, :].astype(BF16)

        @pl.when(jnp.logical_not(last))
        def _():
            came.wait_recv()
            zs[b, :] = (own_of(i)[b, :] + buffer[b, :].astype(F32)).astype(BF16)

        send.start()

    def chain_up(i, n):
        @pl.when(z <= n)
        def _():
            to_z = nz - 1 - n + z
            chain_step(i, to_z, z == 0, g_up(i, to_z), of(zu_a, zu_u, zu_d, i), g_up(i, to_z))

    def chain_down(i, n):
        @pl.when(nz - 1 - z <= n)
        def _():
            to_z = n - (nz - 1 - z)
            chain_step(i, to_z, z == nz - 1, g_down(i, to_z), of(zd_a, zd_u, zd_d, i), g_down(i, to_z))

    def own_index():
        return x * 2 + c if gx == 2 else c

    def chain_end(i):
        b = rows_at(z * zb, zb)

        @pl.when(z > 0)
        def _():
            g_up(i, z).wait_recv()
            own_of(i)[b, :] += of(zu_a, zu_u, zu_d, i)[b, :].astype(F32)

        @pl.when(z < nz - 1)
        def _():
            g_down(i, z).wait_recv()
            own_of(i)[b, :] += of(zd_a, zd_u, zd_d, i)[b, :].astype(F32)

        of(fs_a, fs_u, fs_d, i)[...] = own_of(i)[b, :].astype(BF16)
        for k in range(1, members):
            g_final(i, other_j(k), j).start()

    def finish(i):
        all_taken(i).wait_recv()
        keep = own_of(i)[rows_at(z * zb + own_index() * r, r), :]
        came = of(fr_a, fr_u, fr_d, i)
        for jj in range(members):
            part = jnp.where(j == jj, keep, came[jj].astype(F32))
            if i in A:
                heads = [
                    part[:, p * 128 + h * HEAD : p * 128 + (h + 1) * HEAD] for h in range(hp) for p in range(3)
                ]
                at = (jj * na + i) * wide
                qkv_grad[:, 3 * at : 3 * (at + wide)] = jnp.concatenate(heads, axis=1)
                dense_grad[:, at : at + wide] = part[:, 384 : 384 + wide]
            else:
                out, k = (up_grad, i - na) if i in U else (down_grad, i - na - nm)
                out[:, jj * units + k * pw : jj * units + (k + 1) * pw] = part
        if i == A[-1]:
            result(2).start()
            result(3).start()
        if i in (U[-1], Dn[-1]):
            result(4 if i in U else 5).start()

    def pick(parts):
        total = parts[0]
        for jj in range(1, members):
            total = jnp.where(j == jj, parts[jj], total)
        return total

    def prepare():
        for k in range(na):
            for part in range(3):
                ba[k, :, part * 128 : (part + 1) * 128] = pick(
                    [head_part(b_qkv[...].reshape(1, -1), jj, k, part) for jj in range(members)]
                )
        steps = np.arange(ROT // 2, dtype=np.float32) * 2.0 / ROT
        inverse = (np.float32(ROTARY_BASE) ** -steps).astype(np.float32)
        lane = lax.broadcasted_iota(jnp.int32, (128, 128), 1) % HEAD
        scale = jnp.zeros((128, 128), F32)
        for n in range(ROT):
            scale = jnp.where(lane == n, inverse[n % (ROT // 2)], scale)

        def table(n, carry):
            rows = rows_at(n * 128, 128)
            place = (n * 128 + lax.broadcasted_iota(jnp.int32, (128, 128), 0)).astype(F32)
            cos, sin = jnp.cos(place * scale), jnp.sin(place * scale)
            cos_table[rows, :] = cos
            sin_table[rows, :] = jnp.where(lane < ROT // 2, -sin, sin)
            return carry

        lax.fori_loop(0, length // 128, table, 0)

    def prepare_docs():
        all_docs().wait_recv()
        for s in range(members):
            for n in range(length // 128):
                cut = slice(n * 128, (n + 1) * 128)
                rows = jnp.broadcast_to(docs[s, 0:1, cut], (128, 128))
                doc_column[s, cut, :] = jnp.transpose(rows).astype(BF16)

    RT = min(512, total_rows)
    tiles = total_rows // RT
    lanes = lax.broadcasted_iota(jnp.int32, (1, 128), 1)
    first = lanes < HEAD
    low = lanes % HEAD < ROT // 2
    turning = lanes % HEAD < ROT

    def rotated(rows, places, sign):
        near = jnp.where(low, pltpu.roll(rows, 128 - ROT // 2, 1), pltpu.roll(rows, ROT // 2, 1))
        return rows * cos_table[places, :] + jnp.where(turning, sign * near * sin_table[places, :], 0.0)

    def project(k, n):
        rows = rows_at(n * RT, RT)
        places = rows_at(lax.rem(n * RT, length), RT)
        packed = dot(normed[rows, :], wa[k, :, 0:384], 1, 0) + ba[k]
        query[rows, :] = (rotated(packed[:, 0:128], places, 1.0) * (HEAD**-0.5)).astype(BF16)
        key[rows, :] = rotated(packed[:, 128:256], places, 1.0).astype(BF16)
        value[rows, :] = packed[:, 256:384].astype(BF16)

    def project_back(k, n):
        rows = rows_at(n * RT, RT)
        grad_out[rows, :] = dot(grads[rows, :], wa[k, :, 384:512], 1, 0).astype(BF16)

    def each_tile(step, k):
        def body(n, carry):
            step(k, n)
            return carry

        lax.fori_loop(0, tiles, body, 0)

    block = min(128, length // 4)
    window = length // 4 + block

    def stacked(rows):
        if hp == 1:
            return rows
        zero = jnp.zeros_like(rows)
        return jnp.concatenate([jnp.where(first, rows, zero), jnp.where(first, zero, rows)], axis=0)

    def unstacked(rows):
        if hp == 1:
            return rows
        return jnp.where(first, rows[:window], rows[window:])

    def attend(k, s):
        key_sum[...] = jnp.zeros_like(key_sum)
        value_sum[...] = jnp.zeros_like(value_sum)

        def body(n, carry):
            q_at = pl.multiple_of(n * block, block)
            k_at = pl.multiple_of(jnp.maximum(q_at - length // 4, 0), block)
            q_rows = rows_at(s * length + q_at, block)
            k_rows = pl.ds(pl.multiple_of(s * length + k_at, block), window)
            q = query[q_rows, :]
            g = grad_out[q_rows, :]
            keys, values = stacked(key[k_rows, :]), stacked(value[k_rows, :])
            scores = dot(q, keys, 1, 1)
            grad_p = dot(g, values, 1, 1)
            at = k_at + lax.broadcasted_iota(jnp.int32, (block, window), 1)
            here = q_at + lax.broadcasted_iota(jnp.int32, (block, window), 0)
            own_doc_of = doc_column[s, pl.ds(q_at, block), 0:1].astype(F32)
            same = own_doc_of == docs[s, 0:1, pl.ds(k_at, window)]
            allowed = same & (at <= here)
            probs, grad_s = [], []
            for h in range(hp):
                cut = slice(h * window, (h + 1) * window)
                sc = jnp.where(allowed, scores[:, cut], -1e30)
                expos = jnp.exp(sc - jnp.max(sc, axis=-1, keepdims=True))
                p = expos / jnp.sum(expos, axis=-1, keepdims=True)
                gp = grad_p[:, cut]
                inner = jnp.sum(p * gp, axis=-1, keepdims=True)
                probs.append(p.astype(BF16))
                grad_s.append((p * (gp - inner)).astype(BF16))
            p = jnp.concatenate(probs, axis=1) if hp > 1 else probs[0]
            gs = jnp.concatenate(grad_s, axis=1) if hp > 1 else grad_s[0]
            attended[k, q_rows, :] = dot(p, values, 1, 0).astype(BF16)
            places = pl.ds(q_at, block)
            back = rotated(dot(gs, keys, 1, 0) * (HEAD**-0.5), places, -1.0)
            grad_z[k, q_rows, 0:128] = back.astype(BF16)
            here_rows = pl.ds(k_at, window)
            key_sum[here_rows, :] += unstacked(dot(gs, q, 0, 0))
            value_sum[here_rows, :] += unstacked(dot(p, g, 0, 0))
            return carry

        lax.fori_loop(0, length // block, body, 0)
        rows = rows_at(s * length, length)
        grad_z[k, rows, 128:256] = rotated(key_sum[...], slice(None), -1.0).astype(BF16)
        grad_z[k, rows, 256:384] = value_sum[...].astype(BF16)

    def hidden(k, n):
        rows = rows_at(n * RT, RT)
        u = dot(normed[rows, :], wu[k], 1, 0) + b_up[:, rows_at(j * units + k * pw, pw)]
        phi = 0.5 * (1.0 + lax.erf(u * np.float32(0.5**0.5)))
        active[k, rows, :] = (u * phi).astype(BF16)
        slope[k, rows, :] = phi + u * (jnp.exp(-0.5 * u * u) * np.float32((2 * np.pi) ** -0.5))

    def hidden_back(k, n):
        rows = rows_at(n * RT, RT)
        grad_u[k, rows, :] = (dot(grads[rows, :], wd[k], 1, 0) * slope[k, rows, :]).astype(BF16)

    HT = min(512, length)

    def branch(a, jj):
        def body(n, carry):
            rows = rows_at(jj * length + n * HT, HT)
            total = None
            for k in range(na):
                if a == 0:
                    part = dot(attended[k, rows, :], wa[k, :, 384:512], 1, 1)
                else:
                    part = dot(grad_z[k, rows, :], wa[k, :, 0:384], 1, 1)
                total = part if total is None else total + part
            for k in range(nm):
                if a == 0:
                    part = dot(active[k, rows, :], wd[k], 1, 1)
                else:
                    part = dot(grad_u[k, rows, :], wu[k], 1, 1)
                total = total + part
            partials[a][rows, :] = total.astype(BF16)
            return carry

        lax.fori_loop(0, length // HT, body, 0)

    def half_copy(a, jj):
        at = jj - (1 - c) * gx
        return copy(
            partials[a].at[rows_at(jj * length, length)],
            core_in.at[a % nbuf, rows_at(at * length, length)],
            half_send.at[a, at],
            half_recv.at[a, at],
            partner,
        )

    def branch_give(a, jj):
        branch(a, jj)
        half_copy(a, jj).start()

    def branches(a):
        for n, jj in enumerate((far_j, partner_j)[2 - gx :]):
            branch(a, jj)
            if n == 0 and nbuf == 1 and a == second:
                pl.semaphore_wait(credit.at[0], 1)
            half_copy(a, jj).start()
        for jj in (across_j, j)[2 - gx :]:
            branch(a, jj)

    def block_rows(jj, tt):
        return rows_at((jj * nt + tt) * R, R)

    def in_rows(jj, tt):
        return rows_at(((jj - c * gx) * nt + tt) * R, R)

    def both_cores(a, jj, tt, columns=slice(None)):
        return (
            partials[a][block_rows(jj, tt), columns].astype(F32)
            + core_in[a % nbuf, in_rows(jj, tt), columns].astype(F32)
        )

    def corner_t_copy(a, tt, src):
        b = partials[a].at[block_rows(across_j, tt), back_t]
        n = step_of(src, tt)
        return copy(b, corner_t.at[a % nbuf, src], corner_t_send.at[2 + a, n], corner_t_recv.at[2 + a, n], turned(tt))

    def corner_x_copy(a, jj, tt):
        b = partials[a].at[block_rows(jj, tt), back_x]
        n = step_of(t, tt)
        return copy(b, corner_x.at[a % nbuf, tt], corner_x_send.at[2 + a, n], corner_x_recv.at[2 + a, n], across)

    def side_copy(a, jj):
        b = partials[a].at[block_rows(jj, t)]
        return copy(b, side_x.at[a % nbuf], side_send.at[2 + a], side_recv.at[2 + a], across)

    def turn_copy(a, tt, src):
        b = partials[a].at[block_rows(j, tt)]
        n = step_of(src, tt)
        return copy(b, side_t.at[a % nbuf, src], turn_send.at[2 + a, n], turn_recv.at[2 + a, n], turned(tt))

    def reduce_corner(a):
        if gx == 2:
            half_copy(a, far_j).wait_recv()
            for k in range(1, nt):
                tt = other_t(k)
                partials[a][block_rows(across_j, tt), :] = both_cores(a, across_j, tt).astype(BF16)
                corner_t_copy(a, tt, t).start()
                corner_x_copy(a, across_j, tt).start()

    def reduce_side(a):
        if gx == 2:
            total = both_cores(a, across_j, t, back_t)
            for k in range(1, nt):
                corner_t_copy(a, t, other_t(k)).wait_recv()
                total = total + corner_t[a % nbuf, other_t(k)].astype(F32)
            partials[a][block_rows(across_j, t), back_t] = total.astype(BF16)
            partials[a][block_rows(across_j, t), back_x] = both_cores(a, across_j, t, back_x).astype(BF16)
            side_copy(a, across_j).start()

    def reduce_turn(a):
        if nbuf == 1 and a == second and nt > 1:
            pl.semaphore_wait(credit.at[1], nt - 1)
        half_copy(a, partner_j).wait_recv()
        for k in range(1, nt):
            tt = other_t(k)
            if gx == 2:
                corner_x_copy(a, j, tt).wait_recv()
                total = both_cores(a, j, tt, back_x) + corner_x[a % nbuf, tt].astype(F32)
                partials[a][block_rows(j, tt), back_x] = total.astype(BF16)
                partials[a][block_rows(j, tt), back_t] = both_cores(a, j, tt, back_t).astype(BF16)
            else:
                partials[a][block_rows(j, tt), :] = both_cores(a, j, tt).astype(BF16)
            turn_copy(a, tt, t).start()

    def reduce_wait(a):
        if gx == 2:
            side_copy(a, across_j).wait_recv()
        for k in range(1, nt):
            turn_copy(a, t, other_t(k)).wait_recv()

    def reduced(a, n):
        mine = rows_at((j * nt + t) * R + n * tile, tile)
        came = rows_at(((j - c * gx) * nt + t) * R + n * tile, tile)
        rows = rows_at(n * tile, tile)
        total = partials[a][mine, :].astype(F32) + core_in[a % nbuf, came, :].astype(F32)
        if gx == 2:
            total = total + side_x[a % nbuf, rows, :].astype(F32)
        for k in range(1, nt):
            total = total + side_t[a % nbuf, other_t(k), rows, :].astype(F32)
        return restore(total)

    def reduce_sent(a):
        for xx in range(gx):
            half_copy(a, (1 - c) * gx + xx).wait_send()
        if gx == 2:
            side_copy(a, across_j).wait_send()
        for k in range(1, nt):
            tt = other_t(k)
            turn_copy(a, tt, t).wait_send()
            if gx == 2:
                corner_t_copy(a, tt, t).wait_send()
                corner_x_copy(a, across_j, tt).wait_send()

    def free_buffers():
        if nbuf == 1:
            pl.semaphore_signal(credit.at[0], inc=1, device_id=partner, device_id_type=MESH)
            for k in range(1, nt):
                pl.semaphore_signal(credit.at[1], inc=1, device_id=turned(other_t(k)), device_id_type=MESH)

    def write_output():
        def body(n, carry):
            rows = rows_at(n * tile, tile)
            total = tokens[rows, :].astype(F32) + reduced(0, n) + b_dense[...] + b_down[...]
            output[rows, :] = total.astype(BF16)
            return carry

        lax.fori_loop(0, R // tile, body, 0)
        result(0).start()

    def put(row, at, values):
        at += row * D
        end = at + values.shape[1]
        for h in range(vec.shape[0]):
            lo, hi = max(at, h * D // 2), min(end, (h + 1) * D // 2)
            if lo < hi:
                cols = slice(lo - h * D // 2, hi - h * D // 2)
                vec[h : h + 1, cols] += values[:, lo - at : hi - at]

    def taken(array, row, count=2):
        return jnp.concatenate([array[2 * row + h : 2 * row + h + 1] for h in range(count)], axis=1)

    def sum_biases():
        vec[...] = jnp.zeros_like(vec)
        for k in range(nm):
            put(3, k * pw, jnp.sum(grad_u[k].astype(F32), axis=0, keepdims=True))
        for k in range(na):
            put(3, units + k * 384, jnp.sum(grad_z[k].astype(F32), axis=0, keepdims=True))

    def write_input_grad():
        def body(n, carry):
            rows = rows_at(n * tile, tile)
            normal, inverse = normalize(tokens[rows, :].astype(F32))
            up = cotangent[rows, :].astype(F32)
            grad = reduced(1, n)
            put(0, 0, jnp.sum(grad * normal, axis=0, keepdims=True))
            put(1, 0, jnp.sum(grad, axis=0, keepdims=True))
            put(2, 0, jnp.sum(up, axis=0, keepdims=True))
            scaled = grad * gain[...]
            input_grad[rows, :] = up + inverse * (
                scaled
                - jnp.mean(scaled, axis=-1, keepdims=True)
                - normal * jnp.mean(scaled * normal, axis=-1, keepdims=True)
            )
            return carry

        lax.fori_loop(0, R // tile, body, 0)
        result(1).start()

    peers = nz if gx == 2 else 2 * nz
    mates = members * nt
    peer = z if gx == 2 else z * 2 + x
    mate = j * nt + t

    def peer_copy(to, src):
        device_to = device(to, x, c, t) if gx == 2 else device(to // 2, to % 2, c, t)
        return copy(vec_z.at[peer], vec_z.at[src], peer_send.at[0], peer_recv.at[0], device_to)

    def mate_copy(to, src):
        jj, tt = to // nt, to % nt
        device_to = device(z, jj % 2, jj // 2, tt) if gx == 2 else device(z, x, jj, tt)
        return copy(vec_m.at[mate], vec_m.at[src], mate_send.at[0], mate_recv.at[0], device_to)

    def all_peers():
        rows = vec_z.at[pl.ds(0, peers - 1)]
        return copy(rows, rows, peer_send.at[0], peer_recv.at[0], partner)

    def all_mates():
        rows = vec_m.at[pl.ds(0, mates - 1)]
        return copy(rows, rows, mate_send.at[0], mate_recv.at[0], partner)

    def sums_start():
        vec_z[peer] = vec[...]
        for k in range(1, peers):
            peer_copy(lax.rem(peer + k, peers), peer).start()

    def sums_group():
        all_peers().wait_recv()
        total = vec_z[0]
        for k in range(1, peers):
            total = total + vec_z[k]
        vec_m[mate] = total
        for k in range(1, mates):
            mate_copy(lax.rem(mate + k, mates), mate).start()

    def sums_end():
        all_mates().wait_recv()
        total = vec_m[0]
        for k in range(1, mates):
            total = total + vec_m[k]
        gain_grad[...] = taken(total, 0)
        shift_grad[...] = taken(total, 1)
        dense_bias[...] = taken(total, 2)
        for jj in range(members):
            row = taken(vec_m[jj * nt + t], 3, vec.shape[0] - 6)
            up_bias[:, jj * units : (jj + 1) * units] = row[:, :units]
            for k in range(na):
                part = row[:, units + k * 384 : units + (k + 1) * 384]
                heads = [part[:, p * 128 + h * HEAD : p * 128 + (h + 1) * HEAD] for h in range(hp) for p in range(3)]
                at = (jj * na + k) * wide
                qkv_bias[:, 3 * at : 3 * (at + wide)] = jnp.concatenate(heads, axis=1)
        for n in range(6, 11):
            result(n).start()

    def sums_sent():
        all_peers().wait_send()
        all_mates().wait_send()

    def forwards(some, lo, hi):
        for d in range(lo, hi):
            for i in some:
                forward_up(i, d)
                forward_down(i, d)

    def chains(some, lo, hi):
        for n in range(lo, hi):
            for i in some:
                chain_up(i, n)
                chain_down(i, n)

    second = 0 if gx == 2 else 1

    def any_order():
        stage()
        fill_normed()
        enter()
        for i in U + A + Dn:
            send_first(i)
            share(i)
        give_docs()
        act_start(0)
        fill_grads()
        act_start(1)
        for i in U + A:
            send_own(i)
        prepare()
        prepare_docs()
        forwards(U + A, 1, 2)
        act_from_turn(0)
        act_from_side(0)
        for i in Dn:
            send_own(i)
        forwards(U, 2, nz)
        act_finish(0)
        act_wait(0)
        for i in U:
            gathered(i)
            each_tile(hidden, i - na)
        act_from_turn(1)
        act_from_side(1)
        forwards(A, 2, nz)
        forwards(Dn, 1, nz)
        act_finish(1)
        act_wait(1)
        for i in Dn:
            weight_grad(i)
            sum_x(i)
        chains(Dn, 0, nz - 1)
        for i in A:
            gathered(i)
            each_tile(project, i)
            each_tile(project_back, i)
            for s in range(members):
                attend(i, s)
            weight_grad(i)
            sum_x(i)
        chains(A, 0, nz - 1)
        for i in Dn:
            gathered(i)
            each_tile(hidden_back, i - na - nm)
        for i in U:
            weight_grad(i)
            sum_x(i)
        act_sent(0)
        act_sent(1)
        sum_biases()
        for a in (1, 0) if gx == 2 else (0, 1):
            branches(a)
            reduce_corner(a)
            if a != second:
                chains(U, 0, nz - 1)
            reduce_side(a)
            reduce_turn(a)
            if a != second:
                for i in Dn + A:
                    chain_end(i)
            reduce_wait(a)
            if a == 0:
                write_output()
            else:
                write_input_grad()
                sums_start()
            if a != second:
                free_buffers()
        for i in U:
            chain_end(i)
        sums_group()
        for i in Dn + A + U:
            finish(i)
        sums_end()

    def tuned_order():
        (a,), (u,), (d,) = A, U, Dn
        stage()
        enter()
        share(a)
        give_docs()
        send_first(a)
        send_first(d)
        share(u)
        send_first(u)
        fill_grads()
        fill_normed()
        act_start_turn(0)
        send_own(a)
        act_start_side(0)
        act_start_side(1)
        share(d)
        send_own(u)
        forward_up(a, 1)
        forward_down(a, 1)
        prepare()
        prepare_docs()
        act_start_turn(1)
        forward_up(u, 1)
        forward_down(u, 1)
        forward_down(a, 2)
        act_from_side(0)
        act_from_turn(0)
        forward_up(a, 2)
        act_wait_of(0, partner_j)
        forward_up(u, 2)
        forward_up(a, 3)
        forward_down(a, 3)
        act_from_turn(1)
        forward_down(u, 2)
        project(0, partner_j)
        act_from_side(1)
        act_wait_of(1, partner_j)
        send_own(d)
        project_back(0, partner_j)
        project(0, j)
        project_back(0, j)
        attend(0, partner_j)
        act_finish(0)
        forward_up(u, 3)
        forward_down(u, 3)
        project(0, across_j)
        hidden(0, across_j)
        hidden(0, j)
        hidden(0, partner_j)
        act_wait_of(0, far_j)
        forward_down(d, 1)
        forward_up(d, 1)
        act_finish(1)
        hidden(0, far_j)
        project(0, far_j)
        project_back(0, across_j)
        act_wait_of(1, far_j)
        weight_grad_cut(d, 1)
        chain_up(d, 0)
        weight_grad_cut(d, 0)
        chain_down(d, 0)
        project_back(0, far_j)
        attend(0, j)
        forward_up(d, 2)
        forward_down(d, 2)
        attend(0, across_j)
        chain_up(d, 1)
        chain_down(d, 1)
        attend(0, far_j)
        forward_up(d, 3)
        forward_down(d, 3)
        hidden_back(0, across_j)
        hidden_back(0, far_j)
        branch_give(1, far_j)
        chain_up(d, 2)
        chain_down(d, 2)
        branch(1, across_j)
        weight_grad_cut(a, 0)
        reduce_corner(1)
        weight_grad_cut(a, 1)
        chain_down(a, 0)
        chain_up(a, 0)
        hidden_back(0, j)
        act_sent(0)
        act_sent(1)
        branch_give(0, far_j)
        hidden_back(0, partner_j)
        weight_grad_cut(u, 1)
        chain_end(d)
        chain_up(u, 0)
        weight_grad_cut(u, 0)
        chain_down(u, 0)
        branch(0, across_j)
        reduce_corner(0)
        chain_up(a, 1)
        reduce_side(1)
        chain_down(a, 1)
        branch(0, j)
        branch_give(1, partner_j)
        branch(1, j)
        finish(d)
        branch_give(0, partner_j)
        chain_up(u, 1)
        reduce_turn(1)
        chain_down(u, 1)
        chain_down(a, 2)
        chain_up(a, 2)
        reduce_side(0)
        reduce_turn(0)
        chain_up(u, 2)
        chain_down(u, 2)
        sum_biases()
        reduce_wait(1)
        write_input_grad()
        chain_end(a)
        sums_start()
        chain_end(u)
        sums_group()
        finish(u)
        finish(a)
        reduce_wait(0)
        write_output()
        sums_end()

    if (gx, na, nm, nz, tiles, RT) == (2, 1, 1, 4, 4, length):
        tuned_order()
    else:
        any_order()

    for i in range(count):
        all_given(i).wait_send()
        all_parts(i).wait_send()
        for n in range(1, nz):
            blocks = weights(i).at[pl.ds(0, n * zb)]
            pl.when(z == n - 1)(
                lambda: copy(blocks, blocks, up_send.at[i], z_recv.at[i, 0], along(z + 1)).wait_send()
            )
            pl.when(z == nz - n)(
                lambda: copy(blocks, blocks, down_send.at[i], z_recv.at[i, 0], along(z - 1)).wait_send()
            )
        sums = of(zs_a, zs_u, zs_d, i).at[pl.ds(0, (nz - 1) * zb)]
        copy(sums, sums, g_send.at[i], g_recv.at[i, 0], partner).wait_send()
        if gx == 1:
            for src in range(nz):
                send_across(i, src, x).wait_send()
                g_across(i, src).wait_send()
    all_docs().wait_send()
    reduce_sent(0)
    reduce_sent(1)
    sums_sent()
    for n in range(len(results)):
        result(n).wait()


def hand_out(arrays):
    count = len(arrays)
    thin = [array.shape[0] == 1 for array in arrays]
    leaving = [
        jax.ShapeDtypeStruct(array.shape[1:] if flat else array.shape, array.dtype) for array, flat in zip(arrays, thin)
    ]

    def body(*refs):
        given, taken, came, goes, sems = (
            refs[:count],
            refs[count : 2 * count],
            refs[2 * count : 3 * count],
            refs[3 * count : -1],
            refs[-1],
        )
        reads = [pltpu.make_async_copy(given[n], came[n], sems.at[0, n]) for n in range(count)]
        writes = [
            pltpu.make_async_copy(goes[n] if thin[n] else came[n], taken[n], sems.at[1, n]) for n in range(count)
        ]
        order = sorted(range(count), key=lambda n: thin[n])
        for n in order:
            reads[n].start()
        for n in order:
            reads[n].wait()
            if thin[n]:
                goes[n][...] = came[n][0]
            writes[n].start()
        for n in order:
            writes[n].wait()

    far = pl.BlockSpec(memory_space=pl.ANY)
    return list(
        pl.pallas_call(
            body,
            out_shape=leaving,
            in_specs=[far] * count,
            out_specs=[far] * count,
            scratch_shapes=[pltpu.VMEM(array.shape, array.dtype) for array in arrays]
            + [pltpu.VMEM(part.shape if flat else (8, 128), part.dtype) for part, flat in zip(leaving, thin)]
            + [pltpu.SemaphoreType.DMA((2, count))],
            name="hand_out",
        )(*arrays)
    )


def on_device(
    nt,
    n_dp,
    tokens,
    cotangent,
    segments,
    ln_gain,
    ln_bias,
    w_qkv,
    b_qkv,
    w_dense,
    b_dense,
    w_up,
    b_up,
    w_down,
    b_down,
):
    R, D = tokens.shape
    length = segments.shape[1]
    r = w_qkv.shape[0]
    nz = n_dp // 4
    heads = w_qkv.shape[1] // (3 * HEAD)
    gx = 2 if heads % 4 == 0 and 4 * length * D <= 1 << 21 else 1
    members = 2 * gx
    heads = heads // members
    hp = 2 if heads % 2 == 0 else 1
    na = heads // hp
    units = w_up.shape[1] // members
    pw = 512 if units % 512 == 0 else units
    nm = units // pw
    nbuf = gx
    peers, mates, steps = (nz if gx == 2 else 2 * nz), members * nt, max(nt - 1, 1)
    sizes = dict(nt=nt, nz=nz, gx=gx, na=na, nm=nm, hp=hp, length=length, R=R, r=r, pw=pw, nbuf=nbuf)

    widths = ((na, 512), (nm, pw), (nm, pw))
    count = na + 2 * nm
    rows = members * length
    own = D if gx == 2 else D // 2
    chip = 2 * r
    small = -(-(6 * (D // 2) + units + na * 384) // (4 * D)) * 8
    split = D // 4
    V = pltpu.VMEM
    DMA = pltpu.SemaphoreType.DMA

    def some(shape):
        return V(shape if gx == 2 else (1, 1, 8, 128)[-len(shape) :], BF16)

    scratch = (
        [V((members, na, r, 512), BF16), V((na, 1, 384), F32)]
        + [V((length, 128), F32)] * 2
        + [V((members, 8, length), F32), V((members, length, 128), BF16)]
        + [V((n, D, w), BF16) for n, w in widths]
        + [V((rows, D), BF16), V((rows, D), BF16)]
        + [V((rows, 128), BF16)] * 4
        + [V((na, rows, 128), BF16), V((na, rows, 384), BF16)]
        + [V((length, 128), F32)] * 2
        + [V((nm, rows, pw), BF16), V((nm, rows, pw), F32), V((nm, rows, pw), BF16)]
        + [V((rows, D) if gx == 2 else (8, 128), BF16)]
        + [V((nbuf, gx * length, D), BF16), some((nbuf, nt, R, split)), some((nbuf, nt, R, D - split))]
        + [some((nbuf, R, D)), V((nbuf, nt, R, D), BF16)]
        + [V((n, own, w), F32) for n, w in widths]
        + [V((n, own, w) if gx == 1 else (n, 8, 128), BF16) for _ in range(2) for n, w in widths]
        + [V((n, own, w), BF16) for _ in range(3) for n, w in widths]
        + [V((n, gx * chip, w), BF16) for n, w in widths]
        + [V((n, members, r, w), BF16) for n, w in widths]
        + [V((small, D // 2), F32), V((peers, small, D // 2), F32), V((mates, small, D // 2), F32)]
        + [DMA((count,)), DMA((22,)), DMA((count + 1,)), DMA((count + 1,))]
        + [DMA((count,)), DMA((count,)), DMA((count, nz))]
        + [DMA((count, nz) if gx == 1 else (1, 1))] * 2
        + [DMA((4, steps))] * 2
        + [DMA((4,))] * 2
        + [DMA((4, steps))] * 4
        + [DMA((2, gx, nt))] * 2
        + [DMA((count, nz) if gx == 1 else (1, 1))] * 2
        + [DMA((count,)), DMA((count, nz + 1))]
        + [DMA((count,))] * 2
        + [DMA((2, gx))] * 2
        + [DMA((1,))] * 4
        + [pltpu.SemaphoreType.REGULAR((2,))]
    )
    far = pl.BlockSpec(memory_space=pl.ANY)

    def row(vector):
        return vector.reshape(1, -1)

    args = (
        tokens,
        cotangent,
        segments,
        row(ln_gain),
        row(ln_bias),
        w_qkv,
        b_qkv,
        w_dense.T,
        row(b_dense),
        w_up,
        row(b_up),
        w_down.T,
        row(b_down),
    )
    shapes = (
        jax.ShapeDtypeStruct((R, D), BF16),
        jax.ShapeDtypeStruct((R, D), F32),
        jax.ShapeDtypeStruct((1, D), F32),
        jax.ShapeDtypeStruct((1, D), F32),
        jax.ShapeDtypeStruct(w_qkv.shape, F32),
        jax.ShapeDtypeStruct((1, w_qkv.shape[1]), F32),
        jax.ShapeDtypeStruct(w_dense.shape[::-1], F32),
        jax.ShapeDtypeStruct((1, D), F32),
        jax.ShapeDtypeStruct(w_up.shape, F32),
        jax.ShapeDtypeStruct((1, w_up.shape[1]), F32),
        jax.ShapeDtypeStruct(w_down.shape[::-1], F32),
    )
    out = pl.pallas_call(
        functools.partial(kernel, sizes),
        out_shape=shapes,
        in_specs=[far] * len(args),
        out_specs=[far] * len(shapes),
        scratch_shapes=[V(args[n].shape, args[n].dtype) for n in (0, 1, 2, 3, 4, 5, 6, 7, 8, 10, 12)]
        + [V(shape.shape, shape.dtype) for shape in shapes]
        + scratch,
        compiler_params=pltpu.CompilerParams(
            collective_id=0, has_side_effects=True, vmem_limit_bytes=67043328
        ),
        name="layer",
    )(*args)
    out = hand_out((*out, out[7]))
    out[6], out[10] = out[6].T, out[10].T
    return tuple(out)


def solution(mesh):
    return jax.shard_map(
        functools.partial(on_device, mesh.shape["tensor"], mesh.shape["dp"]),
        mesh=mesh,
        in_specs=(
            P(("dp", "tensor"), None),
            P(("dp", "tensor"), None),
            P("dp", None),
            P(),
            P(),
            P("dp", "tensor"),
            P("tensor"),
            P("tensor", "dp"),
            P(),
            P("dp", "tensor"),
            P("tensor"),
            P("tensor", "dp"),
            P(),
        ),
        out_specs=(
            P(("dp", "tensor"), None),
            P(("dp", "tensor"), None),
            P(),
            P(),
            P("dp", "tensor"),
            P("tensor"),
            P("tensor", "dp"),
            P(),
            P("dp", "tensor"),
            P("tensor"),
            P("tensor", "dp"),
            P(),
        ),
        check_vma=False,
    )
```

```python
import functools

import jax
import jax.numpy as jnp
import numpy as np
from jax import lax
from jax.experimental import pallas as pl
from jax.experimental.pallas import tpu as pltpu
from jax.sharding import PartitionSpec as P

HEAD = 64
ROT = 16
NORM_EPS = 1e-05
ROTARY_BASE = 10000.0
MESH = pl.DeviceIdType.MESH
F32 = jnp.float32
BF16 = jnp.bfloat16


def dot(left, right, over_left, over_right):
    return lax.dot_general(
        left, right, (((over_left,), (over_right,)), ((), ())), preferred_element_type=F32
    )


def normalize(rows):
    centred = rows - jnp.mean(rows, axis=-1, keepdims=True)
    inverse = lax.rsqrt(jnp.mean(centred * centred, axis=-1, keepdims=True) + NORM_EPS)
    return centred * inverse, inverse


def padded(array):
    rest = -array.shape[1] % 128
    return jnp.concatenate([array, jnp.zeros((array.shape[0], rest), array.dtype)], axis=1) if rest else array


def kernel(
    sizes,
    tokens_hbm,
    cotangent_hbm,
    segments_hbm,
    gain_hbm,
    shift_hbm,
    w_qkv_hbm,
    b_qkv_hbm,
    w_dense_hbm,
    b_dense_hbm,
    w_up,
    b_up_hbm,
    w_down,
    b_down_hbm,
    output_hbm,
    input_grad_hbm,
    gain_grad_hbm,
    shift_grad_hbm,
    qkv_grad_hbm,
    qkv_bias_hbm,
    dense_grad_hbm,
    dense_bias_hbm,
    up_grad_hbm,
    up_bias_hbm,
    down_grad_hbm,
    tokens,
    cotangent,
    segments,
    gain,
    shift,
    w_qkv,
    b_qkv,
    w_dense,
    b_dense,
    b_up,
    b_down,
    output,
    input_grad,
    gain_grad,
    shift_grad,
    qkv_grad,
    qkv_bias,
    dense_grad,
    dense_bias,
    up_grad,
    up_bias,
    down_grad,
    wa_in,
    ba,
    cos_table,
    sin_table,
    docs,
    doc_column,
    wa,
    wu,
    wd,
    normed,
    grads,
    query,
    key,
    value,
    grad_out,
    attended,
    grad_z,
    key_sum,
    value_sum,
    active,
    slope,
    grad_u,
    late,
    core_in,
    corner_x,
    corner_t,
    side_x,
    side_t,
    own_a,
    own_u,
    own_d,
    xs_a,
    xs_u,
    xs_d,
    xr_a,
    xr_u,
    xr_d,
    zs_a,
    zs_u,
    zs_d,
    zu_a,
    zu_u,
    zu_d,
    zd_a,
    zd_u,
    zd_d,
    fs_a,
    fs_u,
    fs_d,
    fr_a,
    fr_u,
    fr_d,
    vec,
    vec_z,
    vec_m,
    local_sem,
    io_sem,
    share_send,
    share_recv,
    up_send,
    down_send,
    z_recv,
    x_send,
    x_recv,
    turn_send,
    turn_recv,
    side_send,
    side_recv,
    corner_x_send,
    corner_x_recv,
    corner_t_send,
    corner_t_recv,
    pass_send,
    pass_recv,
    gx_send,
    gx_recv,
    g_send,
    g_recv,
    fin_send,
    fin_recv,
    half_send,
    half_recv,
    peer_send,
    peer_recv,
    mate_send,
    mate_recv,
    credit,
):
    nt, nz, gx, na, nm, hp, length, R, r, pw, nbuf = (
        sizes[k] for k in ("nt", "nz", "gx", "na", "nm", "hp", "length", "R", "r", "pw", "nbuf")
    )
    D = tokens.shape[1]
    chip = 2 * r
    zb = gx * chip
    own = D if gx == 2 else D // 2
    members = 2 * gx
    wide = hp * HEAD
    units = nm * pw
    total_rows = members * length
    partials = (grads, late if gx == 2 else normed)
    dp, t = lax.axis_index("dp"), lax.axis_index("tensor")
    z, x, c = dp // 4, (dp // 2) % 2, dp % 2
    j = c * gx + x if gx == 2 else c

    def device(zz, xx, cc, tt):
        return (zz * 4 + xx * 2 + cc, tt)

    partner = device(z, x, 1 - c, t)
    across = device(z, 1 - x, c, t)

    def member(jj):
        return device(z, jj % 2, jj // 2, t) if gx == 2 else device(z, x, jj, t)

    def along(zz):
        return device(zz, x, c, t)

    def turned(tt):
        return device(z, x, c, tt)

    def other_j(k):
        return lax.rem(j + k, members)

    def other_z(k):
        return lax.rem(z + k, nz)

    def other_t(k):
        return lax.rem(t + k, nt)

    def step_of(src, tt):
        return lax.rem(tt - src + nt, nt) - 1

    def rows_at(start, size):
        return pl.ds(pl.multiple_of(start, size), size)

    def copy(src, dst, send, recv, to):
        return pltpu.make_async_remote_copy(
            src_ref=src, dst_ref=dst, send_sem=send, recv_sem=recv, device_id=to, device_id_type=MESH
        )

    A = list(range(na))
    U = list(range(na, na + nm))
    Dn = list(range(na + nm, na + 2 * nm))
    count = na + 2 * nm

    def of(a, u, d, i):
        if i in A:
            return a.at[i]
        return u.at[i - na] if i in U else d.at[i - na - nm]

    def weights(i):
        return of(wa, wu, wd, i)

    def z_rows(zz):
        return rows_at(zz * zb if gx == 2 else (x * nz + zz) * chip, zb)

    own_rows = rows_at(z * zb + (x * 2 + c) * r if gx == 2 else (x * nz + z) * chip + c * r, r)

    barrier = pltpu.get_barrier_semaphore()
    greeted = [member(other_j(k)) for k in range(1, members)] + ([] if gx == 2 else [across])
    greeted += [
        device(z, jj % 2 if gx == 2 else x, jj // 2 if gx == 2 else jj, other_t(k))
        for k in range(1, nt)
        for jj in [other_j(n) for n in range(members)]
    ]

    def greet(other):
        pl.semaphore_signal(barrier, inc=1, device_id=other, device_id_type=MESH)

    for other in greeted:
        greet(other)
    pl.when(z > 0)(lambda: greet(along(z - 1)))
    pl.when(z < nz - 1)(lambda: greet(along(z + 1)))

    reads = [
        pltpu.make_async_copy(src, dst, io_sem.at[n])
        for n, (src, dst) in enumerate(
            (
                (segments_hbm, segments),
                (gain_hbm, gain),
                (shift_hbm, shift),
                (b_qkv_hbm, b_qkv),
                (b_dense_hbm, b_dense),
                (b_up_hbm, b_up),
                (b_down_hbm, b_down),
                (w_qkv_hbm, w_qkv),
                (w_dense_hbm, w_dense),
                (tokens_hbm, tokens),
                (cotangent_hbm, cotangent),
            )
        )
    ]
    for read in reads:
        read.start()

    def enter():
        pl.semaphore_wait(barrier, len(greeted) + jnp.minimum(z, 1) + jnp.minimum(nz - 1 - z, 1))

    results = (
        (output, output_hbm),
        (input_grad, input_grad_hbm),
        (qkv_grad, qkv_grad_hbm),
        (dense_grad, dense_grad_hbm),
        (up_grad, up_grad_hbm),
        (down_grad, down_grad_hbm),
        (gain_grad, gain_grad_hbm),
        (shift_grad, shift_grad_hbm),
        (qkv_bias, qkv_bias_hbm),
        (dense_bias, dense_bias_hbm),
        (up_bias, up_bias_hbm),
    )

    def result(n):
        return pltpu.make_async_copy(*results[n], io_sem.at[11 + n])

    def part_of(i, jj):
        if i in A:
            return wa_in.at[jj, i]
        ref, k = (w_up, i - na) if i in U else (w_down, i - na - nm)
        return ref.at[:, rows_at(jj * units + k * pw, pw)]

    def local_copy(i):
        return pltpu.make_async_copy(part_of(i, j), weights(i).at[own_rows], local_sem.at[i])

    def give_part(i, jj):
        dst = weights(i).at[own_rows]
        return copy(part_of(i, jj), dst, share_send.at[i], share_recv.at[i], member(jj))

    def all_parts(i):
        rows = weights(i).at[pl.ds(0, (members - 1) * r)]
        return copy(rows, rows, share_send.at[i], share_recv.at[i], partner)

    def member_rows(jj):
        return rows_at(z * zb + (jj % 2 * 2 + jj // 2) * r if gx == 2 else (x * nz + z) * chip + jj * r, r)

    def share(i):
        local_copy(i).start()
        for k in range(1, members):
            give_part(i, other_j(k)).start()

    def head_part(array, jj, k, part):
        at = [((jj * na + k) * hp + h) * 3 * HEAD + part * HEAD for h in range(hp)]
        return padded(jnp.concatenate([array[:, a : a + HEAD] for a in at], axis=1))

    def own_doc(jj):
        return copy(docs.at[j], docs.at[j], share_send.at[count], share_recv.at[count], member(jj))

    def all_docs():
        rows = docs.at[pl.ds(0, members - 1)]
        return copy(rows, rows, share_send.at[count], share_recv.at[count], partner)

    def stage():
        for read in reads[:9]:
            read.wait()
        for jj in range(members):
            for k in range(na):
                for part in range(3):
                    wa_in[jj, k, :, part * 128 : (part + 1) * 128] = head_part(w_qkv[...], jj, k, part)
                at = (jj * na + k) * wide
                wa_in[jj, k, :, 384:512] = padded(w_dense[:, at : at + wide])
        docs[j] = jnp.broadcast_to(segments[...].astype(F32), docs.shape[1:])

    def give_docs():
        for k in range(1, members):
            own_doc(other_j(k)).start()

    def permute(rows):
        if gx == 2:
            return rows
        return jnp.concatenate(
            [rows[:, (zz * 2 + xx) * chip : (zz * 2 + xx + 1) * chip] for xx in range(2) for zz in range(nz)],
            axis=1,
        )

    def restore(rows):
        if gx == 2:
            return rows
        return jnp.concatenate(
            [rows[:, (xx * nz + zz) * chip : (xx * nz + zz + 1) * chip] for zz in range(nz) for xx in range(2)],
            axis=1,
        )

    acts = (normed, grads)
    tile = min(64, R)
    split = D * 3 // 8
    over_x, over_t = slice(0, split), slice(split, D)
    back_split = D // 4
    back_x, back_t = slice(0, back_split), slice(back_split, D)

    def act_rows(jj, tt):
        return rows_at((jj * nt + tt) * R, R)

    across_j = c * gx + 1 - x if gx == 2 else c
    partner_j = (1 - c) * gx + x if gx == 2 else 1 - c
    far_j = (1 - c) * gx + 1 - x if gx == 2 else 1 - c
    near = (j, partner_j, across_j, far_j)

    def fill_normed():
        reads[9].wait()

        def body(n, carry):
            rows = rows_at(n * tile, tile)
            normal, _ = normalize(tokens[rows, :].astype(F32))
            normed[rows_at((j * nt + t) * R + n * tile, tile), :] = permute(
                (normal * gain[...] + shift[...]).astype(BF16)
            )
            return carry

        lax.fori_loop(0, R // tile, body, 0)

    def fill_grads():
        reads[10].wait()

        def body(n, carry):
            grads[rows_at((j * nt + t) * R + n * tile, tile), :] = permute(cotangent[rows_at(n * tile, tile), :])
            return carry

        lax.fori_loop(0, R // tile, body, 0)

    def act_turn(a, tt, src):
        b = acts[a].at[act_rows(j, src)]
        return copy(b, b, turn_send.at[a, step_of(src, tt)], turn_recv.at[a, step_of(src, tt)], turned(tt))

    def act_side(a, jj):
        b = acts[a].at[act_rows(jj, t)]
        return copy(b, b, side_send.at[a], side_recv.at[a], across)

    def act_corner_x(a, jj, tt):
        b = acts[a].at[act_rows(jj, tt), over_x]
        return copy(b, b, corner_x_send.at[a, step_of(t, tt)], corner_x_recv.at[a, step_of(t, tt)], across)

    def act_corner_t(a, tt, src):
        b = acts[a].at[act_rows(across_j, src), over_t]
        return copy(b, b, corner_t_send.at[a, step_of(src, tt)], corner_t_recv.at[a, step_of(src, tt)], turned(tt))

    def act_pass(a, jj, tt):
        b = acts[a].at[act_rows(jj, tt)]
        return copy(b, b, pass_send.at[a, jj % gx, tt], pass_recv.at[a, jj % gx, tt], partner)

    def act_start_side(a):
        if gx == 2:
            act_side(a, j).start()

    def act_start_turn(a):
        for k in range(1, nt):
            act_turn(a, other_t(k), t).start()
        act_pass(a, j, t).start()

    def act_start(a):
        act_start_side(a)
        act_start_turn(a)

    def act_from_turn(a):
        for k in range(1, nt):
            src = other_t(k)
            act_turn(a, t, src).wait_recv()
            if gx == 2:
                act_corner_x(a, j, src).start()
            act_pass(a, j, src).start()

    def act_from_side(a):
        if gx == 2:
            act_side(a, across_j).wait_recv()
            for k in range(1, nt):
                act_corner_t(a, other_t(k), t).start()
            act_pass(a, across_j, t).start()

    def act_finish(a):
        if gx == 2:
            for k in range(1, nt):
                src = other_t(k)
                act_corner_x(a, across_j, src).wait_recv()
                act_corner_t(a, t, src).wait_recv()
                act_pass(a, across_j, src).start()

    def act_wait_of(a, jj):
        for k in range(nt):
            act_pass(a, jj, k).wait_recv()

    def act_wait(a):
        for xx in range(gx):
            act_wait_of(a, (1 - c) * gx + xx)

    def act_sent(a):
        if gx == 2:
            act_side(a, j).wait_send()
        for k in range(1, nt):
            act_turn(a, other_t(k), t).wait_send()
            if gx == 2:
                act_corner_x(a, j, other_t(k)).wait_send()
                act_corner_t(a, other_t(k), t).wait_send()
        for xx in range(gx):
            for k in range(nt):
                act_pass(a, c * gx + xx, k).wait_send()

    def w_block(i, zz):
        return weights(i).at[z_rows(zz)]

    def send_up(i, src):
        b = w_block(i, src)
        return copy(b, b, up_send.at[i], z_recv.at[i, src], along(z + 1))

    def send_down(i, src):
        b = w_block(i, src)
        return copy(b, b, down_send.at[i], z_recv.at[i, src], along(z - 1))

    def send_across(i, src, xx):
        b = weights(i).at[rows_at((xx * nz + src) * chip, chip)]
        return copy(b, b, x_send.at[i, src], x_recv.at[i, src], across)

    def send_first(i):
        def along_z(sems, to):
            return copy(part_of(i, j), weights(i).at[own_rows], sems.at[i], z_recv.at[i, z], to)

        pl.when(z < nz - 1)(lambda: along_z(up_send, along(z + 1)).start())
        pl.when(z > 0)(lambda: along_z(down_send, along(z - 1)).start())

    def send_own(i):
        local_copy(i).wait()
        all_parts(i).wait_recv()
        for k in range(1, members):
            jj = other_j(k)
            rows = weights(i).at[member_rows(jj)]

            def along_z(sems, to):
                return copy(rows, rows, sems.at[i], z_recv.at[i, z], to)

            pl.when(z < nz - 1)(lambda: along_z(up_send, along(z + 1)).start())
            pl.when(z > 0)(lambda: along_z(down_send, along(z - 1)).start())
        if gx == 1:
            send_across(i, z, x).start()

    def forward_up(i, d):
        @pl.when(z >= d)
        def _():
            send_up(i, z - d).wait_recv()
            pl.when(z < nz - 1)(lambda: send_up(i, z - d).start())
            if gx == 1:
                send_across(i, z - d, x).start()

    def forward_down(i, d):
        @pl.when(z + d <= nz - 1)
        def _():
            send_down(i, z + d).wait_recv()
            pl.when(z > 0)(lambda: send_down(i, z + d).start())
            if gx == 1:
                send_across(i, z + d, x).start()

    def gathered(i):
        if gx == 1:
            for src in range(nz):
                send_across(i, src, 1 - x).wait_recv()

    def own_of(i):
        return of(own_a, own_u, own_d, i)

    def g_across(i, to_z):
        b = pl.ds(to_z * chip, chip)
        return copy(
            of(xs_a, xs_u, xs_d, i).at[b],
            of(xr_a, xr_u, xr_d, i).at[b],
            gx_send.at[i, to_z],
            gx_recv.at[i, to_z],
            across,
        )

    def g_up(i, to_z):
        b = rows_at(to_z * zb, zb)
        return copy(
            of(zs_a, zs_u, zs_d, i).at[b],
            of(zu_a, zu_u, zu_d, i).at[b],
            g_send.at[i],
            g_recv.at[i, to_z + 1],
            along(z + 1),
        )

    def g_down(i, to_z):
        b = rows_at(to_z * zb, zb)
        return copy(
            of(zs_a, zs_u, zs_d, i).at[b],
            of(zd_a, zd_u, zd_d, i).at[b],
            g_send.at[i],
            g_recv.at[i, to_z],
            along(z - 1),
        )

    def g_final(i, jj, src):
        at = (jj % 2 * 2 + jj // 2) * r if gx == 2 else jj * r
        return copy(
            of(fs_a, fs_u, fs_d, i).at[rows_at(at, r)],
            of(fr_a, fr_u, fr_d, i).at[src],
            fin_send.at[i],
            fin_recv.at[i],
            member(jj),
        )

    def all_given(i):
        rows = of(fs_a, fs_u, fs_d, i).at[pl.ds(0, (members - 1) * r)]
        return copy(rows, rows, fin_send.at[i], fin_recv.at[i], partner)

    def all_taken(i):
        rows = of(fr_a, fr_u, fr_d, i).at[pl.ds(0, members - 1)]
        return copy(rows, rows, fin_send.at[i], fin_recv.at[i], partner)

    def products(i, columns):
        if i in A:
            return [
                (0, 384, dot(normed[:, columns], grad_z[i], 0, 0)),
                (384, 512, dot(grads[:, columns], attended[i], 0, 0)),
            ]
        if i in U:
            return [(0, pw, dot(normed[:, columns], grad_u[i - na], 0, 0))]
        return [(0, pw, dot(grads[:, columns], active[i - na - nm], 0, 0))]

    cut = min(512, own)

    def weight_grad_cut(i, n):
        at = n * cut if gx == 2 else x * own + n * cut
        for lo, hi, part in products(i, rows_at(at, cut)):
            own_of(i)[n * cut : (n + 1) * cut, lo:hi] = part

    def weight_grad(i):
        if gx == 1:
            xs = of(xs_a, xs_u, xs_d, i)
            for n in range(own // cut):
                for lo, hi, part in products(i, rows_at((1 - x) * own + n * cut, cut)):
                    xs[n * cut : (n + 1) * cut, lo:hi] = part.astype(BF16)
            for to_z in range(nz):
                g_across(i, to_z).start()
        for n in range(own // cut):
            weight_grad_cut(i, n)

    def sum_x(i):
        if gx == 1:
            xr = of(xr_a, xr_u, xr_d, i)
            for to_z in range(nz):
                g_across(i, to_z).wait_recv()
                b = slice(to_z * chip, (to_z + 1) * chip)
                own_of(i)[b, :] += xr[b, :].astype(F32)

    def chain_step(i, to_z, last, came, buffer, send):
        b = rows_at(to_z * zb, zb)
        zs = of(zs_a, zs_u, zs_d, i)

        @pl.when(last)
        def _():
            zs[b, :] = own_of(i)[b, :].astype(BF16)

        @pl.when(jnp.logical_not(last))
        def _():
            came.wait_recv()
            zs[b, :] = (own_of(i)[b, :] + buffer[b, :].astype(F32)).astype(BF16)

        send.start()

    def chain_up(i, n):
        @pl.when(z <= n)
        def _():
            to_z = nz - 1 - n + z
            chain_step(i, to_z, z == 0, g_up(i, to_z), of(zu_a, zu_u, zu_d, i), g_up(i, to_z))

    def chain_down(i, n):
        @pl.when(nz - 1 - z <= n)
        def _():
            to_z = n - (nz - 1 - z)
            chain_step(i, to_z, z == nz - 1, g_down(i, to_z), of(zd_a, zd_u, zd_d, i), g_down(i, to_z))

    def own_index():
        return x * 2 + c if gx == 2 else c

    def chain_end(i):
        b = rows_at(z * zb, zb)

        @pl.when(z > 0)
        def _():
            g_up(i, z).wait_recv()
            own_of(i)[b, :] += of(zu_a, zu_u, zu_d, i)[b, :].astype(F32)

        @pl.when(z < nz - 1)
        def _():
            g_down(i, z).wait_recv()
            own_of(i)[b, :] += of(zd_a, zd_u, zd_d, i)[b, :].astype(F32)

        of(fs_a, fs_u, fs_d, i)[...] = own_of(i)[b, :].astype(BF16)
        for k in range(1, members):
            g_final(i, other_j(k), j).start()

    def finish(i):
        all_taken(i).wait_recv()
        keep = own_of(i)[rows_at(z * zb + own_index() * r, r), :]
        came = of(fr_a, fr_u, fr_d, i)
        for jj in range(members):
            part = jnp.where(j == jj, keep, came[jj].astype(F32))
            if i in A:
                heads = [
                    part[:, p * 128 + h * HEAD : p * 128 + (h + 1) * HEAD] for h in range(hp) for p in range(3)
                ]
                at = (jj * na + i) * wide
                qkv_grad[:, 3 * at : 3 * (at + wide)] = jnp.concatenate(heads, axis=1)
                dense_grad[:, at : at + wide] = part[:, 384 : 384 + wide]
            else:
                out, k = (up_grad, i - na) if i in U else (down_grad, i - na - nm)
                out[:, jj * units + k * pw : jj * units + (k + 1) * pw] = part
        if i == A[-1]:
            result(2).start()
            result(3).start()
        if i in (U[-1], Dn[-1]):
            result(4 if i in U else 5).start()

    def pick(parts):
        total = parts[0]
        for jj in range(1, members):
            total = jnp.where(j == jj, parts[jj], total)
        return total

    def prepare():
        for k in range(na):
            for part in range(3):
                ba[k, :, part * 128 : (part + 1) * 128] = pick(
                    [head_part(b_qkv[...].reshape(1, -1), jj, k, part) for jj in range(members)]
                )
        steps = np.arange(ROT // 2, dtype=np.float32) * 2.0 / ROT
        inverse = (np.float32(ROTARY_BASE) ** -steps).astype(np.float32)
        lane = lax.broadcasted_iota(jnp.int32, (128, 128), 1) % HEAD
        scale = jnp.zeros((128, 128), F32)
        for n in range(ROT):
            scale = jnp.where(lane == n, inverse[n % (ROT // 2)], scale)

        def table(n, carry):
            rows = rows_at(n * 128, 128)
            place = (n * 128 + lax.broadcasted_iota(jnp.int32, (128, 128), 0)).astype(F32)
            cos, sin = jnp.cos(place * scale), jnp.sin(place * scale)
            cos_table[rows, :] = cos
            sin_table[rows, :] = jnp.where(lane < ROT // 2, -sin, sin)
            return carry

        lax.fori_loop(0, length // 128, table, 0)

    def prepare_docs():
        all_docs().wait_recv()
        for s in range(members):
            for n in range(length // 128):
                cut = slice(n * 128, (n + 1) * 128)
                rows = jnp.broadcast_to(docs[s, 0:1, cut], (128, 128))
                doc_column[s, cut, :] = jnp.transpose(rows).astype(BF16)

    RT = min(512, total_rows)
    tiles = total_rows // RT
    lanes = lax.broadcasted_iota(jnp.int32, (1, 128), 1)
    first = lanes < HEAD
    low = lanes % HEAD < ROT // 2
    turning = lanes % HEAD < ROT

    def rotated(rows, places, sign):
        near = jnp.where(low, pltpu.roll(rows, 128 - ROT // 2, 1), pltpu.roll(rows, ROT // 2, 1))
        return rows * cos_table[places, :] + jnp.where(turning, sign * near * sin_table[places, :], 0.0)

    def project(k, n):
        rows = rows_at(n * RT, RT)
        places = rows_at(lax.rem(n * RT, length), RT)
        packed = dot(normed[rows, :], wa[k, :, 0:384], 1, 0) + ba[k]
        query[rows, :] = (rotated(packed[:, 0:128], places, 1.0) * (HEAD**-0.5)).astype(BF16)
        key[rows, :] = rotated(packed[:, 128:256], places, 1.0).astype(BF16)
        value[rows, :] = packed[:, 256:384].astype(BF16)

    def project_back(k, n):
        rows = rows_at(n * RT, RT)
        grad_out[rows, :] = dot(grads[rows, :], wa[k, :, 384:512], 1, 0).astype(BF16)

    def each_tile(step, k):
        def body(n, carry):
            step(k, n)
            return carry

        lax.fori_loop(0, tiles, body, 0)

    block = min(128, length // 4)
    window = length // 4 + block

    def stacked(rows):
        if hp == 1:
            return rows
        zero = jnp.zeros_like(rows)
        return jnp.concatenate([jnp.where(first, rows, zero), jnp.where(first, zero, rows)], axis=0)

    def unstacked(rows):
        if hp == 1:
            return rows
        return jnp.where(first, rows[:window], rows[window:])

    def attend(k, s):
        key_sum[...] = jnp.zeros_like(key_sum)
        value_sum[...] = jnp.zeros_like(value_sum)

        def body(n, carry):
            q_at = pl.multiple_of(n * block, block)
            k_at = pl.multiple_of(jnp.maximum(q_at - length // 4, 0), block)
            q_rows = rows_at(s * length + q_at, block)
            k_rows = pl.ds(pl.multiple_of(s * length + k_at, block), window)
            q = query[q_rows, :]
            g = grad_out[q_rows, :]
            keys, values = stacked(key[k_rows, :]), stacked(value[k_rows, :])
            scores = dot(q, keys, 1, 1)
            grad_p = dot(g, values, 1, 1)
            at = k_at + lax.broadcasted_iota(jnp.int32, (block, window), 1)
            here = q_at + lax.broadcasted_iota(jnp.int32, (block, window), 0)
            own_doc_of = doc_column[s, pl.ds(q_at, block), 0:1].astype(F32)
            same = own_doc_of == docs[s, 0:1, pl.ds(k_at, window)]
            allowed = same & (at <= here)
            probs, grad_s = [], []
            for h in range(hp):
                cut = slice(h * window, (h + 1) * window)
                sc = jnp.where(allowed, scores[:, cut], -1e30)
                expos = jnp.exp(sc - jnp.max(sc, axis=-1, keepdims=True))
                p = expos / jnp.sum(expos, axis=-1, keepdims=True)
                gp = grad_p[:, cut]
                inner = jnp.sum(p * gp, axis=-1, keepdims=True)
                probs.append(p.astype(BF16))
                grad_s.append((p * (gp - inner)).astype(BF16))
            p = jnp.concatenate(probs, axis=1) if hp > 1 else probs[0]
            gs = jnp.concatenate(grad_s, axis=1) if hp > 1 else grad_s[0]
            attended[k, q_rows, :] = dot(p, values, 1, 0).astype(BF16)
            places = pl.ds(q_at, block)
            back = rotated(dot(gs, keys, 1, 0) * (HEAD**-0.5), places, -1.0)
            grad_z[k, q_rows, 0:128] = back.astype(BF16)
            here_rows = pl.ds(k_at, window)
            key_sum[here_rows, :] += unstacked(dot(gs, q, 0, 0))
            value_sum[here_rows, :] += unstacked(dot(p, g, 0, 0))
            return carry

        lax.fori_loop(0, length // block, body, 0, unroll=2)
        rows = rows_at(s * length, length)
        grad_z[k, rows, 128:256] = rotated(key_sum[...], slice(None), -1.0).astype(BF16)
        grad_z[k, rows, 256:384] = value_sum[...].astype(BF16)

    def hidden(k, n):
        rows = rows_at(n * RT, RT)
        u = dot(normed[rows, :], wu[k], 1, 0) + b_up[:, rows_at(j * units + k * pw, pw)]
        phi = 0.5 * (1.0 + lax.erf(u * np.float32(0.5**0.5)))
        active[k, rows, :] = (u * phi).astype(BF16)
        slope[k, rows, :] = phi + u * (jnp.exp(-0.5 * u * u) * np.float32((2 * np.pi) ** -0.5))

    def hidden_back(k, n):
        rows = rows_at(n * RT, RT)
        grad_u[k, rows, :] = (dot(grads[rows, :], wd[k], 1, 0) * slope[k, rows, :]).astype(BF16)

    HT = min(512, length)

    def branch(a, jj):
        def body(n, carry):
            rows = rows_at(jj * length + n * HT, HT)
            total = None
            for k in range(na):
                if a == 0:
                    part = dot(attended[k, rows, :], wa[k, :, 384:512], 1, 1)
                else:
                    part = dot(grad_z[k, rows, :], wa[k, :, 0:384], 1, 1)
                total = part if total is None else total + part
            for k in range(nm):
                if a == 0:
                    part = dot(active[k, rows, :], wd[k], 1, 1)
                else:
                    part = dot(grad_u[k, rows, :], wu[k], 1, 1)
                total = total + part
            partials[a][rows, :] = total.astype(BF16)
            return carry

        lax.fori_loop(0, length // HT, body, 0)

    def half_copy(a, jj):
        at = jj - (1 - c) * gx
        return copy(
            partials[a].at[rows_at(jj * length, length)],
            core_in.at[a % nbuf, rows_at(at * length, length)],
            half_send.at[a, at],
            half_recv.at[a, at],
            partner,
        )

    def branch_give(a, jj):
        branch(a, jj)
        half_copy(a, jj).start()

    def branches(a):
        for n, jj in enumerate((far_j, partner_j)[2 - gx :]):
            branch(a, jj)
            if n == 0 and nbuf == 1 and a == second:
                pl.semaphore_wait(credit.at[0], 1)
            half_copy(a, jj).start()
        for jj in (across_j, j)[2 - gx :]:
            branch(a, jj)

    def block_rows(jj, tt):
        return rows_at((jj * nt + tt) * R, R)

    def in_rows(jj, tt):
        return rows_at(((jj - c * gx) * nt + tt) * R, R)

    def both_cores(a, jj, tt, columns=slice(None)):
        return (
            partials[a][block_rows(jj, tt), columns].astype(F32)
            + core_in[a % nbuf, in_rows(jj, tt), columns].astype(F32)
        )

    def corner_t_copy(a, tt, src):
        b = partials[a].at[block_rows(across_j, tt), back_t]
        n = step_of(src, tt)
        return copy(b, corner_t.at[a % nbuf, src], corner_t_send.at[2 + a, n], corner_t_recv.at[2 + a, n], turned(tt))

    def corner_x_copy(a, jj, tt):
        b = partials[a].at[block_rows(jj, tt), back_x]
        n = step_of(t, tt)
        return copy(b, corner_x.at[a % nbuf, tt], corner_x_send.at[2 + a, n], corner_x_recv.at[2 + a, n], across)

    def side_copy(a, jj):
        b = partials[a].at[block_rows(jj, t)]
        return copy(b, side_x.at[a % nbuf], side_send.at[2 + a], side_recv.at[2 + a], across)

    def turn_copy(a, tt, src):
        b = partials[a].at[block_rows(j, tt)]
        n = step_of(src, tt)
        return copy(b, side_t.at[a % nbuf, src], turn_send.at[2 + a, n], turn_recv.at[2 + a, n], turned(tt))

    def reduce_corner(a):
        if gx == 2:
            half_copy(a, far_j).wait_recv()
            for k in range(1, nt):
                tt = other_t(k)
                partials[a][block_rows(across_j, tt), :] = both_cores(a, across_j, tt).astype(BF16)
                corner_t_copy(a, tt, t).start()
                corner_x_copy(a, across_j, tt).start()

    def reduce_side(a):
        if gx == 2:
            total = both_cores(a, across_j, t, back_t)
            for k in range(1, nt):
                corner_t_copy(a, t, other_t(k)).wait_recv()
                total = total + corner_t[a % nbuf, other_t(k)].astype(F32)
            partials[a][block_rows(across_j, t), back_t] = total.astype(BF16)
            partials[a][block_rows(across_j, t), back_x] = both_cores(a, across_j, t, back_x).astype(BF16)
            side_copy(a, across_j).start()

    def reduce_turn(a):
        if nbuf == 1 and a == second and nt > 1:
            pl.semaphore_wait(credit.at[1], nt - 1)
        half_copy(a, partner_j).wait_recv()
        for k in range(1, nt):
            tt = other_t(k)
            if gx == 2:
                corner_x_copy(a, j, tt).wait_recv()
                total = both_cores(a, j, tt, back_x) + corner_x[a % nbuf, tt].astype(F32)
                partials[a][block_rows(j, tt), back_x] = total.astype(BF16)
                partials[a][block_rows(j, tt), back_t] = both_cores(a, j, tt, back_t).astype(BF16)
            else:
                partials[a][block_rows(j, tt), :] = both_cores(a, j, tt).astype(BF16)
            turn_copy(a, tt, t).start()

    def reduce_wait(a):
        if gx == 2:
            side_copy(a, across_j).wait_recv()
        for k in range(1, nt):
            turn_copy(a, t, other_t(k)).wait_recv()

    def reduced(a, n):
        mine = rows_at((j * nt + t) * R + n * tile, tile)
        came = rows_at(((j - c * gx) * nt + t) * R + n * tile, tile)
        rows = rows_at(n * tile, tile)
        total = partials[a][mine, :].astype(F32) + core_in[a % nbuf, came, :].astype(F32)
        if gx == 2:
            total = total + side_x[a % nbuf, rows, :].astype(F32)
        for k in range(1, nt):
            total = total + side_t[a % nbuf, other_t(k), rows, :].astype(F32)
        return restore(total)

    def reduce_sent(a):
        for xx in range(gx):
            half_copy(a, (1 - c) * gx + xx).wait_send()
        if gx == 2:
            side_copy(a, across_j).wait_send()
        for k in range(1, nt):
            tt = other_t(k)
            turn_copy(a, tt, t).wait_send()
            if gx == 2:
                corner_t_copy(a, tt, t).wait_send()
                corner_x_copy(a, across_j, tt).wait_send()

    def free_buffers():
        if nbuf == 1:
            pl.semaphore_signal(credit.at[0], inc=1, device_id=partner, device_id_type=MESH)
            for k in range(1, nt):
                pl.semaphore_signal(credit.at[1], inc=1, device_id=turned(other_t(k)), device_id_type=MESH)

    def write_output():
        def body(n, carry):
            rows = rows_at(n * tile, tile)
            total = tokens[rows, :].astype(F32) + reduced(0, n) + b_dense[...] + b_down[...]
            output[rows, :] = total.astype(BF16)
            return carry

        lax.fori_loop(0, R // tile, body, 0)
        result(0).start()

    def put(row, at, values):
        at += row * D
        end = at + values.shape[1]
        for h in range(vec.shape[0]):
            lo, hi = max(at, h * D // 2), min(end, (h + 1) * D // 2)
            if lo < hi:
                cols = slice(lo - h * D // 2, hi - h * D // 2)
                vec[h : h + 1, cols] += values[:, lo - at : hi - at]

    def taken(array, row, count=2):
        return jnp.concatenate([array[2 * row + h : 2 * row + h + 1] for h in range(count)], axis=1)

    def sum_biases():
        vec[...] = jnp.zeros_like(vec)
        for k in range(nm):
            put(3, k * pw, jnp.sum(grad_u[k].astype(F32), axis=0, keepdims=True))
        for k in range(na):
            put(3, units + k * 384, jnp.sum(grad_z[k].astype(F32), axis=0, keepdims=True))

    def write_input_grad():
        def body(n, carry):
            rows = rows_at(n * tile, tile)
            normal, inverse = normalize(tokens[rows, :].astype(F32))
            up = cotangent[rows, :].astype(F32)
            grad = reduced(1, n)
            put(0, 0, jnp.sum(grad * normal, axis=0, keepdims=True))
            put(1, 0, jnp.sum(grad, axis=0, keepdims=True))
            put(2, 0, jnp.sum(up, axis=0, keepdims=True))
            scaled = grad * gain[...]
            input_grad[rows, :] = up + inverse * (
                scaled
                - jnp.mean(scaled, axis=-1, keepdims=True)
                - normal * jnp.mean(scaled * normal, axis=-1, keepdims=True)
            )
            return carry

        lax.fori_loop(0, R // tile, body, 0)
        result(1).start()

    peers = nz if gx == 2 else 2 * nz
    mates = members * nt
    peer = z if gx == 2 else z * 2 + x
    mate = j * nt + t

    def peer_copy(to, src):
        device_to = device(to, x, c, t) if gx == 2 else device(to // 2, to % 2, c, t)
        return copy(vec_z.at[peer], vec_z.at[src], peer_send.at[0], peer_recv.at[0], device_to)

    def mate_copy(to, src):
        jj, tt = to // nt, to % nt
        device_to = device(z, jj % 2, jj // 2, tt) if gx == 2 else device(z, x, jj, tt)
        return copy(vec_m.at[mate], vec_m.at[src], mate_send.at[0], mate_recv.at[0], device_to)

    def all_peers():
        rows = vec_z.at[pl.ds(0, peers - 1)]
        return copy(rows, rows, peer_send.at[0], peer_recv.at[0], partner)

    def all_mates():
        rows = vec_m.at[pl.ds(0, mates - 1)]
        return copy(rows, rows, mate_send.at[0], mate_recv.at[0], partner)

    def sums_start():
        vec_z[peer] = vec[...]
        for k in range(1, peers):
            peer_copy(lax.rem(peer + k, peers), peer).start()

    def sums_group():
        all_peers().wait_recv()
        total = vec_z[0]
        for k in range(1, peers):
            total = total + vec_z[k]
        vec_m[mate] = total
        for k in range(1, mates):
            mate_copy(lax.rem(mate + k, mates), mate).start()

    def sums_end():
        all_mates().wait_recv()
        total = vec_m[0]
        for k in range(1, mates):
            total = total + vec_m[k]
        gain_grad[...] = taken(total, 0)
        shift_grad[...] = taken(total, 1)
        dense_bias[...] = taken(total, 2)
        for jj in range(members):
            row = taken(vec_m[jj * nt + t], 3, vec.shape[0] - 6)
            up_bias[:, jj * units : (jj + 1) * units] = row[:, :units]
            for k in range(na):
                part = row[:, units + k * 384 : units + (k + 1) * 384]
                heads = [part[:, p * 128 + h * HEAD : p * 128 + (h + 1) * HEAD] for h in range(hp) for p in range(3)]
                at = (jj * na + k) * wide
                qkv_bias[:, 3 * at : 3 * (at + wide)] = jnp.concatenate(heads, axis=1)
        for n in range(6, 11):
            result(n).start()

    def sums_sent():
        all_peers().wait_send()
        all_mates().wait_send()

    def forwards(some, lo, hi):
        for d in range(lo, hi):
            for i in some:
                forward_up(i, d)
                forward_down(i, d)

    def chains(some, lo, hi):
        for n in range(lo, hi):
            for i in some:
                chain_up(i, n)
                chain_down(i, n)

    second = 0 if gx == 2 else 1

    def any_order():
        stage()
        fill_normed()
        enter()
        for i in U + A + Dn:
            send_first(i)
            share(i)
        give_docs()
        act_start(0)
        fill_grads()
        act_start(1)
        for i in U + A:
            send_own(i)
        prepare()
        prepare_docs()
        forwards(U + A, 1, 2)
        act_from_turn(0)
        act_from_side(0)
        for i in Dn:
            send_own(i)
        forwards(U, 2, nz)
        act_finish(0)
        act_wait(0)
        for i in U:
            gathered(i)
            each_tile(hidden, i - na)
        act_from_turn(1)
        act_from_side(1)
        forwards(A, 2, nz)
        forwards(Dn, 1, nz)
        act_finish(1)
        act_wait(1)
        for i in Dn:
            weight_grad(i)
            sum_x(i)
        chains(Dn, 0, nz - 1)
        for i in A:
            gathered(i)
            each_tile(project, i)
            each_tile(project_back, i)
            for s in range(members):
                attend(i, s)
            weight_grad(i)
            sum_x(i)
        chains(A, 0, nz - 1)
        for i in Dn:
            gathered(i)
            each_tile(hidden_back, i - na - nm)
        for i in U:
            weight_grad(i)
            sum_x(i)
        act_sent(0)
        act_sent(1)
        sum_biases()
        for a in (1, 0) if gx == 2 else (0, 1):
            branches(a)
            reduce_corner(a)
            if a != second:
                chains(U, 0, nz - 1)
            reduce_side(a)
            reduce_turn(a)
            if a != second:
                for i in Dn + A:
                    chain_end(i)
            reduce_wait(a)
            if a == 0:
                write_output()
            else:
                write_input_grad()
                sums_start()
            if a != second:
                free_buffers()
        for i in U:
            chain_end(i)
        sums_group()
        for i in Dn + A + U:
            finish(i)
        sums_end()

    def tuned_order():
        (a,), (u,), (d,) = A, U, Dn
        stage()
        enter()
        share(a)
        give_docs()
        send_first(a)
        send_first(d)
        share(u)
        send_first(u)
        fill_grads()
        fill_normed()
        act_start_turn(0)
        send_own(a)
        act_start_side(0)
        act_start_side(1)
        share(d)
        send_own(u)
        forward_up(a, 1)
        forward_down(a, 1)
        prepare()
        prepare_docs()
        act_start_turn(1)
        forward_up(u, 1)
        forward_down(u, 1)
        forward_down(a, 2)
        act_from_side(0)
        act_from_turn(0)
        forward_up(a, 2)
        act_wait_of(0, partner_j)
        forward_up(u, 2)
        forward_up(a, 3)
        forward_down(a, 3)
        act_from_turn(1)
        forward_down(u, 2)
        project(0, partner_j)
        act_from_side(1)
        act_wait_of(1, partner_j)
        send_own(d)
        project_back(0, partner_j)
        project(0, j)
        project_back(0, j)
        attend(0, partner_j)
        act_finish(0)
        forward_up(u, 3)
        forward_down(u, 3)
        project(0, across_j)
        hidden(0, across_j)
        hidden(0, j)
        hidden(0, partner_j)
        act_wait_of(0, far_j)
        forward_down(d, 1)
        forward_up(d, 1)
        act_finish(1)
        hidden(0, far_j)
        project(0, far_j)
        project_back(0, across_j)
        act_wait_of(1, far_j)
        weight_grad_cut(d, 1)
        chain_up(d, 0)
        weight_grad_cut(d, 0)
        chain_down(d, 0)
        project_back(0, far_j)
        attend(0, j)
        forward_up(d, 2)
        forward_down(d, 2)
        attend(0, across_j)
        chain_up(d, 1)
        chain_down(d, 1)
        attend(0, far_j)
        forward_up(d, 3)
        forward_down(d, 3)
        hidden_back(0, across_j)
        hidden_back(0, far_j)
        branch_give(1, far_j)
        chain_up(d, 2)
        chain_down(d, 2)
        branch(1, across_j)
        weight_grad_cut(a, 0)
        reduce_corner(1)
        weight_grad_cut(a, 1)
        chain_down(a, 0)
        chain_up(a, 0)
        hidden_back(0, j)
        act_sent(0)
        act_sent(1)
        branch_give(0, far_j)
        hidden_back(0, partner_j)
        weight_grad_cut(u, 1)
        chain_end(d)
        chain_up(u, 0)
        weight_grad_cut(u, 0)
        chain_down(u, 0)
        branch(0, across_j)
        reduce_corner(0)
        chain_up(a, 1)
        reduce_side(1)
        chain_down(a, 1)
        branch(0, j)
        branch_give(1, partner_j)
        branch(1, j)
        finish(d)
        branch_give(0, partner_j)
        chain_up(u, 1)
        reduce_turn(1)
        chain_down(u, 1)
        chain_down(a, 2)
        chain_up(a, 2)
        reduce_side(0)
        reduce_turn(0)
        chain_up(u, 2)
        chain_down(u, 2)
        sum_biases()
        reduce_wait(1)
        write_input_grad()
        chain_end(a)
        sums_start()
        chain_end(u)
        sums_group()
        finish(u)
        finish(a)
        reduce_wait(0)
        write_output()
        sums_end()

    if (gx, na, nm, nz, tiles, RT) == (2, 1, 1, 4, 4, length):
        tuned_order()
    else:
        any_order()

    for i in range(count):
        all_given(i).wait_send()
        all_parts(i).wait_send()
        for n in range(1, nz):
            blocks = weights(i).at[pl.ds(0, n * zb)]
            pl.when(z == n - 1)(
                lambda: copy(blocks, blocks, up_send.at[i], z_recv.at[i, 0], along(z + 1)).wait_send()
            )
            pl.when(z == nz - n)(
                lambda: copy(blocks, blocks, down_send.at[i], z_recv.at[i, 0], along(z - 1)).wait_send()
            )
        sums = of(zs_a, zs_u, zs_d, i).at[pl.ds(0, (nz - 1) * zb)]
        copy(sums, sums, g_send.at[i], g_recv.at[i, 0], partner).wait_send()
        if gx == 1:
            for src in range(nz):
                send_across(i, src, x).wait_send()
                g_across(i, src).wait_send()
    all_docs().wait_send()
    reduce_sent(0)
    reduce_sent(1)
    sums_sent()
    for n in range(len(results)):
        result(n).wait()


def hand_out(arrays):
    count = len(arrays)
    thin = [array.shape[0] == 1 for array in arrays]
    leaving = [
        jax.ShapeDtypeStruct(array.shape[1:] if flat else array.shape, array.dtype) for array, flat in zip(arrays, thin)
    ]

    def body(*refs):
        given, taken, came, goes, sems = (
            refs[:count],
            refs[count : 2 * count],
            refs[2 * count : 3 * count],
            refs[3 * count : -1],
            refs[-1],
        )
        reads = [pltpu.make_async_copy(given[n], came[n], sems.at[0, n]) for n in range(count)]
        writes = [
            pltpu.make_async_copy(goes[n] if thin[n] else came[n], taken[n], sems.at[1, n]) for n in range(count)
        ]
        order = sorted(range(count), key=lambda n: thin[n])
        for n in order:
            reads[n].start()
        for n in order:
            reads[n].wait()
            if thin[n]:
                goes[n][...] = came[n][0]
            writes[n].start()
        for n in order:
            writes[n].wait()

    far = pl.BlockSpec(memory_space=pl.ANY)
    return list(
        pl.pallas_call(
            body,
            out_shape=leaving,
            in_specs=[far] * count,
            out_specs=[far] * count,
            scratch_shapes=[pltpu.VMEM(array.shape, array.dtype) for array in arrays]
            + [pltpu.VMEM(part.shape if flat else (8, 128), part.dtype) for part, flat in zip(leaving, thin)]
            + [pltpu.SemaphoreType.DMA((2, count))],
            name="hand_out",
        )(*arrays)
    )


def on_device(
    nt,
    n_dp,
    tokens,
    cotangent,
    segments,
    ln_gain,
    ln_bias,
    w_qkv,
    b_qkv,
    w_dense,
    b_dense,
    w_up,
    b_up,
    w_down,
    b_down,
):
    R, D = tokens.shape
    length = segments.shape[1]
    r = w_qkv.shape[0]
    nz = n_dp // 4
    heads = w_qkv.shape[1] // (3 * HEAD)
    gx = 2 if heads % 4 == 0 and 4 * length * D <= 1 << 21 else 1
    members = 2 * gx
    heads = heads // members
    hp = 2 if heads % 2 == 0 else 1
    na = heads // hp
    units = w_up.shape[1] // members
    pw = 512 if units % 512 == 0 else units
    nm = units // pw
    nbuf = gx
    peers, mates, steps = (nz if gx == 2 else 2 * nz), members * nt, max(nt - 1, 1)
    sizes = dict(nt=nt, nz=nz, gx=gx, na=na, nm=nm, hp=hp, length=length, R=R, r=r, pw=pw, nbuf=nbuf)

    widths = ((na, 512), (nm, pw), (nm, pw))
    count = na + 2 * nm
    rows = members * length
    own = D if gx == 2 else D // 2
    chip = 2 * r
    small = -(-(6 * (D // 2) + units + na * 384) // (4 * D)) * 8
    split = D // 4
    V = pltpu.VMEM
    DMA = pltpu.SemaphoreType.DMA

    def some(shape):
        return V(shape if gx == 2 else (1, 1, 8, 128)[-len(shape) :], BF16)

    scratch = (
        [V((members, na, r, 512), BF16), V((na, 1, 384), F32)]
        + [V((length, 128), F32)] * 2
        + [V((members, 8, length), F32), V((members, length, 128), BF16)]
        + [V((n, D, w), BF16) for n, w in widths]
        + [V((rows, D), BF16), V((rows, D), BF16)]
        + [V((rows, 128), BF16)] * 4
        + [V((na, rows, 128), BF16), V((na, rows, 384), BF16)]
        + [V((length, 128), F32)] * 2
        + [V((nm, rows, pw), BF16), V((nm, rows, pw), F32), V((nm, rows, pw), BF16)]
        + [V((rows, D) if gx == 2 else (8, 128), BF16)]
        + [V((nbuf, gx * length, D), BF16), some((nbuf, nt, R, split)), some((nbuf, nt, R, D - split))]
        + [some((nbuf, R, D)), V((nbuf, nt, R, D), BF16)]
        + [V((n, own, w), F32) for n, w in widths]
        + [V((n, own, w) if gx == 1 else (n, 8, 128), BF16) for _ in range(2) for n, w in widths]
        + [V((n, own, w), BF16) for _ in range(3) for n, w in widths]
        + [V((n, gx * chip, w), BF16) for n, w in widths]
        + [V((n, members, r, w), BF16) for n, w in widths]
        + [V((small, D // 2), F32), V((peers, small, D // 2), F32), V((mates, small, D // 2), F32)]
        + [DMA((count,)), DMA((22,)), DMA((count + 1,)), DMA((count + 1,))]
        + [DMA((count,)), DMA((count,)), DMA((count, nz))]
        + [DMA((count, nz) if gx == 1 else (1, 1))] * 2
        + [DMA((4, steps))] * 2
        + [DMA((4,))] * 2
        + [DMA((4, steps))] * 4
        + [DMA((2, gx, nt))] * 2
        + [DMA((count, nz) if gx == 1 else (1, 1))] * 2
        + [DMA((count,)), DMA((count, nz + 1))]
        + [DMA((count,))] * 2
        + [DMA((2, gx))] * 2
        + [DMA((1,))] * 4
        + [pltpu.SemaphoreType.REGULAR((2,))]
    )
    far = pl.BlockSpec(memory_space=pl.ANY)

    def row(vector):
        return vector.reshape(1, -1)

    args = (
        tokens,
        cotangent,
        segments,
        row(ln_gain),
        row(ln_bias),
        w_qkv,
        b_qkv,
        w_dense.T,
        row(b_dense),
        w_up,
        row(b_up),
        w_down.T,
        row(b_down),
    )
    shapes = (
        jax.ShapeDtypeStruct((R, D), BF16),
        jax.ShapeDtypeStruct((R, D), F32),
        jax.ShapeDtypeStruct((1, D), F32),
        jax.ShapeDtypeStruct((1, D), F32),
        jax.ShapeDtypeStruct(w_qkv.shape, F32),
        jax.ShapeDtypeStruct((1, w_qkv.shape[1]), F32),
        jax.ShapeDtypeStruct(w_dense.shape[::-1], F32),
        jax.ShapeDtypeStruct((1, D), F32),
        jax.ShapeDtypeStruct(w_up.shape, F32),
        jax.ShapeDtypeStruct((1, w_up.shape[1]), F32),
        jax.ShapeDtypeStruct(w_down.shape[::-1], F32),
    )
    out = pl.pallas_call(
        functools.partial(kernel, sizes),
        out_shape=shapes,
        in_specs=[far] * len(args),
        out_specs=[far] * len(shapes),
        scratch_shapes=[V(args[n].shape, args[n].dtype) for n in (0, 1, 2, 3, 4, 5, 6, 7, 8, 10, 12)]
        + [V(shape.shape, shape.dtype) for shape in shapes]
        + scratch,
        compiler_params=pltpu.CompilerParams(
            collective_id=0, has_side_effects=True, vmem_limit_bytes=67043328
        ),
        name="layer",
    )(*args)
    out = hand_out((*out, out[7]))
    out[6], out[10] = out[6].T, out[10].T
    return tuple(out)


def solution(mesh):
    return jax.shard_map(
        functools.partial(on_device, mesh.shape["tensor"], mesh.shape["dp"]),
        mesh=mesh,
        in_specs=(
            P(("dp", "tensor"), None),
            P(("dp", "tensor"), None),
            P("dp", None),
            P(),
            P(),
            P("dp", "tensor"),
            P("tensor"),
            P("tensor", "dp"),
            P(),
            P("dp", "tensor"),
            P("tensor"),
            P("tensor", "dp"),
            P(),
        ),
        out_specs=(
            P(("dp", "tensor"), None),
            P(("dp", "tensor"), None),
            P(),
            P(),
            P("dp", "tensor"),
            P("tensor"),
            P("tensor", "dp"),
            P(),
            P("dp", "tensor"),
            P("tensor"),
            P("tensor", "dp"),
            P(),
        ),
        check_vma=False,
    )
```
